128 devices in a mesh: dp: 4 (over x), tensor: 32 (over z, y, core).
Axes of the slice: x: 4, y: 4, z: 4, core: 2. Of those that a mesh axis runs over, the one named last changes fastest.
Arguments:
- tokens: bfloat16 [8192, 2048], P(('dp', 'tensor')), may hold values from -40 to 40
- attn_gain: bfloat16 [2048], replicated, may hold values from 0.099609375 to 1.8984375
- moe_gain: bfloat16 [2048], replicated, may hold values from 0.099609375 to 1.8984375
- q_gain: bfloat16 [128], replicated, may hold values from 0.099609375 to 1.8984375
- k_gain: bfloat16 [128], replicated, may hold values from 0.099609375 to 1.8984375
- query_weight: bfloat16 [2048, 4096], P(None, 'tensor'), may hold values from -0.125 to 0.125
- w_kv: bfloat16 [256, 4, 2048], P('tensor'), may hold values from -0.125 to 0.125
- w_o: bfloat16 [4096, 2048], P('tensor'), may hold values from -0.5 to 0.5
- w_gate: bfloat16 [64, 768, 2048], P('tensor'), may hold values from -0.125 to 0.125
- w_up: bfloat16 [64, 768, 2048], P('tensor'), may hold values from -0.125 to 0.125
- w_down: bfloat16 [64, 768, 2048], P('tensor'), may hold values from -0.21875 to 0.21875
- shrink_qkv: bfloat16 [16, 48, 2048], P('dp'), may hold values from -0.125 to 0.125
- shrink_o: bfloat16 [16, 16, 4096], P(None, None, 'tensor'), may hold values from -0.5 to 0.5
- query_up_factors: bfloat16 [16, 16, 4096], P(None, None, 'tensor'), may hold values from -1.5 to 1.5
- key_value_up_factors: bfloat16 [16, 16, 1024], replicated, may hold values from -1.5 to 1.5
- expand_o: bfloat16 [16, 16, 2048], replicated, may hold values from -1.5 to 1.5
- lengths: int32 [4, 32], P('dp'), may hold values from 1 to 256, 2048 in all within a row
- groups: int32 [4, 32], P('dp'), may hold values from 0 to 3, never falling along the last dimension, each value on 1 to 16 neighbouring positions
- adapter_of_request: int32 [4, 32], P('dp'), may hold values from 0 to 15
- adapter_slot: int32 [16], replicated, may hold values from 0 to 15, each once
- page_table: int32 [4, 64], P('dp'), may hold values from 0 to 63, each once within a row
- expert_ids: int32 [8192, 8], P('dp'), may hold values from 0 to 63, all different within a row; in each aligned block of 64 rows (0 to 63, 64 to 127, ...) at most 16 rows name the same one
- expert_gates: float32 [8192, 8], P('dp'), may hold values from 0.05 to 1
Outputs:
- attn_out: bfloat16 [8192, 2048], P(('dp', 'tensor'))
- moe_out: bfloat16 [8192, 2048], P(('dp', 'tensor'))
- kv_pages: bfloat16 [256, 1024, 128], P('dp', 'tensor')
The draws below stay inside these ranges and needn't reach their ends.
Inputs may be any that keep to these rules, and one draw needn't show every extreme that they name: `lengths`: each row sums to 2048; its largest entry is exactly 256. `groups`: never falling along a row; each group holds 1 to 16 consecutive requests, one exactly 16. `adapter_slot`: A permutation; the factors of slots k * 16 / 4 to (k + 1) * 16 / 4 - 1 are held at dp index k. `page_table`: each row is a permutation of the pages of that token group's pool. `expert_ids`: A token's 8 experts are distinct; within each aligned block of 64 rows (the rows of one device) no expert is chosen by more than 16 tokens, a bound that some block reaches.
All inputs are finite; a program needn't handle non-finite values.
Results may differ from the reference program's by a relative error of at most 0.025.
Values may be sent and summed in bfloat16 or wider, within the bound.
A program may use at most 128 MiB of HBM per device.

```python
import math
import jax
import jax.numpy as jnp
import numpy as np
from jax import lax

D = 2048
QUERY_HEADS = 32
KEY_VALUE_HEADS = 4
HEAD_DIM = 128
EXPERTS = 64
FF = 768
TOPK = 8
FACTOR_RANK = 16
ADAPTER_COUNT = 16
REQ = 32
GROUPS = 4
GMAX = 16
PAGE = 128
TOK_DEV = 64
CAP_DEV = 16
GROUP_TOKENS = 2048
TOKENS = 8192
QUERY_WIDTH = 4096
KVW = 1024
LMAX = 256
PAGES_DP = 64
PAGES = 256
CAP = 512
N_DP = 4
N_TENSOR = 32


def draw_tokens(key, part):
    key_rows, key_cols, key_base = jax.random.split(key, 3)
    row_scale = jnp.exp(jax.random.uniform(key_rows, (TOKENS, 1), jnp.float32, math.log(0.3), math.log(3.0)))
    col_scale = jnp.exp(jax.random.uniform(key_cols, (1, D), jnp.float32, math.log(0.3), math.log(3.0)))
    base = jax.random.normal(key_base, (TOKENS, D), jnp.float32)
    return jnp.clip(base * row_scale * col_scale, -40.0, 40.0).astype(jnp.bfloat16)


def touch_ends(drawn, rng, low, largest):
    longest = drawn.shape.index(max(drawn.shape))
    spots = []
    for shift in (0, 1):
        where = [jax.random.randint(jax.random.fold_in(rng, axis), (), 0, length) for axis, length in enumerate(drawn.shape)]
        where[longest] = (where[longest] + shift) % drawn.shape[longest]
        spots.append(tuple(where))
    return drawn.at[spots[0]].set(low).at[spots[1]].set(largest)


def block_scale(rng, dims, cuts, low, largest):
    def one(dim, blocks):
        heights = jax.random.uniform(jax.random.fold_in(jax.random.fold_in(rng, 6), dim), (blocks,), jnp.float32, low / len(cuts), largest / len(cuts))
        return jnp.repeat(jnp.exp(heights), dims[dim] // blocks).reshape((-1,) + (1,) * (len(dims) - dim - 1))

    level = one(*cuts[0])
    for cut in cuts[1:]:
        level = level * one(*cut)
    return level


def split_up(number_of, total, limit, skew):
    weights = [(1 << 20) // math.isqrt(rank ** skew) + 1 for rank in range(2, number_of + 1)]
    surplus, given = total - limit - (number_of - 1), [1] * (number_of - 1)
    while surplus > 0:
        free = [i for i in range(number_of - 1) if given[i] < limit]
        whole, budget = sum([weights[i] for i in free]), surplus
        for i in free:
            addition = min(limit - given[i], max(1, budget * weights[i] // whole), surplus)
            given[i] = given[i] + addition
            surplus = surplus - addition
    return np.array([limit] + given)


def ragged(key, number_of, total, bound, lean):
    if number_of == 2:
        one = jax.random.randint(key, (), max(1, total - bound), min(bound, total - 1) + 1)
        return jnp.stack([one, total - one])
    tallies = jnp.asarray(split_up(number_of, total, bound, lean), jnp.int32)
    pairs = (number_of - 1) // 2
    source_of, receiver = tallies[1:1 + 2 * pairs:2], tallies[2:2 + 2 * pairs:2]
    room = jnp.minimum(source_of - 1, bound - receiver)
    moved = jax.random.randint(jax.random.fold_in(key, 1), (pairs,), 0, 1 << 20) % (room + 1)
    tallies = tallies.at[1:1 + 2 * pairs:2].set(source_of - moved).at[2:2 + 2 * pairs:2].set(receiver + moved)
    return tallies[jax.random.permutation(jax.random.fold_in(key, 2), number_of)]


def routed_block(stream_key, own, number, rows, number_of, top, reach, skew):
    ranking = jax.random.permutation(stream_key, number_of)
    packed, common = portions_of(number_of, rows * top, reach, skew, True), portions_of(number_of, rows * top, reach, skew, False)
    places = jnp.arange(number_of)

    def named(sizes, rotation):
        used = int((sizes > 0).sum())
        fixed = max(1, used // 4)
        shifted = fixed + (places - fixed + rotation * (used - fixed)) % max(1, number_of - fixed)
        return jnp.zeros((number_of,), jnp.int32).at[ranking[jnp.where(places < fixed, places, shifted)]].set(jnp.asarray(sizes, jnp.int32))

    sizes = jnp.where(number % 4 == 0, named(packed, number // 4), named(common, number - number // 4 - 1))
    mixed = jax.random.permutation(jax.random.fold_in(own, 3), number_of)
    source_of, sink = mixed[0:number_of // 2 * 2:2], mixed[1:number_of // 2 * 2:2]
    room = jnp.minimum(sizes[source_of] - 1, reach - sizes[sink]) // 2
    room = jnp.where((source_of == ranking[0]) | (sink == ranking[0]) | (sizes[sink] == 0), 0, jnp.maximum(room, 0))
    shifted = jax.random.randint(jax.random.fold_in(own, 4), (number_of // 2,), 0, 1 << 20) % (room + 1)
    sizes = sizes.at[source_of].add(-shifted).at[sink].add(shifted)
    items = jnp.searchsorted(jnp.cumsum(sizes), jnp.arange(rows * top), side="right").astype(jnp.int32)
    table = items.reshape(top, rows).T
    table = table[jax.random.permutation(jax.random.fold_in(own, 1), rows)]
    rotation = jax.random.randint(jax.random.fold_in(own, 2), (rows, 1), 0, top)
    return jnp.take_along_axis(table, (jnp.arange(top)[None, :] + rotation) % top, axis=1)


def portions_of(number_of, total, bound, slope, full):
    portions = [(1 << 20) // math.isqrt(rank ** slope) + 1 for rank in range(1, number_of + 1)]
    largest = bound if full else min(bound, max(-(-total // number_of), total * portions[0] // sum(portions)))
    least = 1 if total - largest >= number_of - 1 else 0
    given, rest = [largest] + [least] * (number_of - 1), total - largest - least * (number_of - 1)
    while rest > 0:
        movable = [i for i in range(1, number_of) if given[i] < largest] or [i for i in range(1, number_of) if given[i] < bound]
        whole, left = sum([portions[i] for i in movable]), rest
        for i in movable:
            extra = min(bound - given[i], max(1, left * portions[i] // whole), rest)
            given[i] = given[i] + extra
            rest = rest - extra
    return np.array(given)


def bell_draw(rng, extent, width, bound, cuts=(), held_as=jnp.bfloat16):
    values = width * jax.random.normal(rng, extent, jnp.float32)
    if cuts:
        values = values * block_scale(rng, extent, cuts, -0.22, 0.18)
    return jnp.clip(values, -bound, bound).astype(held_as)


def setup_inputs(seed: int = 0) -> dict:
    key_list = jax.random.split(jax.random.key(seed), 24)
    tokens = draw_tokens(jax.random.fold_in(key_list[23], 71), 0)
    attn_gain = jnp.clip(1.0 + 0.18 * jax.random.normal(key_list[1], (D,), jnp.float32), 0.099609375, 1.8984375).astype(jnp.bfloat16)
    moe_gain = jnp.clip(1.0 + 0.18 * jax.random.normal(key_list[2], (D,), jnp.float32), 0.099609375, 1.8984375).astype(jnp.bfloat16)
    q_gain = jnp.clip(1.0 + 0.18 * jax.random.normal(key_list[3], (HEAD_DIM,), jnp.float32), 0.099609375, 1.8984375).astype(jnp.bfloat16)
    k_gain = jnp.clip(1.0 + 0.18 * jax.random.normal(key_list[4], (HEAD_DIM,), jnp.float32), 0.099609375, 1.8984375).astype(jnp.bfloat16)
    query_weight = bell_draw(key_list[5], (D, QUERY_WIDTH), D ** -0.5, 0.125, ((1, 32),))
    w_kv = bell_draw(key_list[6], (2 * HEAD_DIM, KEY_VALUE_HEADS, D), D ** -0.5, 0.125, ((0, 32),))
    w_o = bell_draw(key_list[7], (QUERY_WIDTH, D), HEAD_DIM ** -0.5, 0.5, ((0, 32),))
    w_gate = bell_draw(key_list[8], (EXPERTS, FF, D), D ** -0.5, 0.125, ((0, 32),))
    w_up = bell_draw(key_list[9], (EXPERTS, FF, D), D ** -0.5, 0.125, ((0, 32),))
    w_down = bell_draw(key_list[10], (EXPERTS, FF, D), FF ** -0.5, 0.21875, ((0, 32),))
    shrink_qkv = bell_draw(key_list[11], (ADAPTER_COUNT, 3 * FACTOR_RANK, D), D ** -0.5, 0.125, ((0, 4),))
    shrink_o = bell_draw(key_list[12], (ADAPTER_COUNT, FACTOR_RANK, QUERY_WIDTH), HEAD_DIM ** -0.5, 0.5, ((2, 32),))
    query_up_factors = bell_draw(key_list[13], (ADAPTER_COUNT, FACTOR_RANK, QUERY_WIDTH), FACTOR_RANK ** -0.5, 1.5, ((2, 32),))
    key_value_up_factors = bell_draw(key_list[14], (ADAPTER_COUNT, FACTOR_RANK, KVW), FACTOR_RANK ** -0.5, 1.5)
    expand_o = bell_draw(key_list[15], (ADAPTER_COUNT, FACTOR_RANK, D), FACTOR_RANK ** -0.5, 1.5)
    lengths = jax.vmap(lambda own: ragged(own, REQ, GROUP_TOKENS, LMAX, 2))(jax.random.split(key_list[16], N_DP)).reshape((N_DP, REQ)).astype(jnp.int32)
    groups = jax.vmap(lambda own: jnp.searchsorted(jnp.cumsum(ragged(own, GROUPS, REQ, GMAX, 2)), jnp.arange(REQ), side="right"))(jax.random.split(key_list[17], N_DP)).reshape((N_DP, REQ)).astype(jnp.int32)
    adapter_of_request = touch_ends(jax.random.randint(key_list[18], (N_DP, REQ), 0, ADAPTER_COUNT), jax.random.fold_in(key_list[18], 1), 0, ADAPTER_COUNT - 1).astype(jnp.int32)
    adapter_slot = jax.random.permutation(key_list[19], ADAPTER_COUNT).astype(jnp.int32)
    page_table = jax.vmap(lambda own: jax.random.permutation(own, PAGES_DP))(jax.random.split(key_list[20], N_DP)).reshape((N_DP, PAGES_DP)).astype(jnp.int32)
    expert_ids_keys = jax.random.split(jax.random.fold_in(key_list[21], 1), TOKENS // TOK_DEV)
    expert_ids_turns = jax.random.permutation(jax.random.fold_in(key_list[21], 3), TOKENS // TOK_DEV)
    expert_ids = jax.vmap(lambda own, number: routed_block(jax.random.fold_in(key_list[21], 2), own, number, TOK_DEV, EXPERTS, TOPK, CAP_DEV, 2))(expert_ids_keys, expert_ids_turns).reshape((TOKENS, TOPK))
    expert_gates = jnp.clip(jnp.exp(math.log(1.0) - 2.9957323 * jax.random.uniform(key_list[22], (TOKENS, TOPK), jnp.float32) ** block_scale(key_list[22], (TOKENS, TOPK), ((0, 4),), -0.2, 0.2)), 0.05, 1.0)
    return dict(tokens=tokens, attn_gain=attn_gain, moe_gain=moe_gain, q_gain=q_gain, k_gain=k_gain, query_weight=query_weight, w_kv=w_kv, w_o=w_o, w_gate=w_gate, w_up=w_up, w_down=w_down, shrink_qkv=shrink_qkv, shrink_o=shrink_o, query_up_factors=query_up_factors, key_value_up_factors=key_value_up_factors, expand_o=expand_o, lengths=lengths, groups=groups, adapter_of_request=adapter_of_request, adapter_slot=adapter_slot, page_table=page_table, expert_ids=expert_ids, expert_gates=expert_gates)


NORM_EPS = 1e-06
ROPE_BASE = 1000000.0
ADAPTER_FACTOR = 0.5

def normalize(values, gain):
    return values * lax.rsqrt(lax.optimization_barrier(jnp.mean(values * values, axis=-1, keepdims=True)) + NORM_EPS) * gain.astype(jnp.float32)

def rotate(values, position):
    half = values.shape[-1] // 2
    freq = jnp.exp(-jnp.arange(half, dtype=jnp.float32) * (2.0 * math.log(ROPE_BASE) / values.shape[-1]))
    angle = position.astype(jnp.float32)[:, None, None] * freq[None, None, :]
    cosine = jnp.cos(angle)
    sine = jnp.sin(angle)
    first = values[..., :half]
    second = values[..., half:]
    return jnp.concatenate([first * cosine - second * sine, second * cosine + first * sine], axis=-1)

def lookup(index_value, table):
    match = index_value[:, None] == jnp.arange(table.shape[0], dtype=jnp.int32)[None, :]
    return lax.optimization_barrier(jnp.sum(jnp.where(match, table[None, :], 0), axis=1)).astype(jnp.int32)

def token_layout(length_row, group_row, adapter_row, adapter_slot, page_row, grand_total):
    position = jnp.arange(grand_total, dtype=jnp.int32)
    ends = jnp.cumsum(length_row).astype(jnp.int32)
    starts = (ends - length_row).astype(jnp.int32)
    request = lax.optimization_barrier(jnp.sum((ends[None, :] <= position[:, None]).astype(jnp.int32), axis=1)).astype(jnp.int32)
    group = lookup(request, group_row)
    same = group_row[:, None] == group_row[None, :]
    group_first = lax.optimization_barrier(jnp.min(jnp.where(same, starts[None, :], grand_total), axis=1)).astype(jnp.int32)
    rope_pos = position - lookup(request, group_first)
    offset = position - lookup(request, starts)
    per_request = page_row.shape[0] // length_row.shape[0]
    page = lookup(request * per_request + offset // PAGE, page_row)
    cell = page * PAGE + offset % PAGE
    adapter_position = lookup(request, lookup(adapter_row, adapter_slot))
    return (group, rope_pos, cell, adapter_position)

def spread_rows(values, adapter_position, adapters):
    match = adapter_position[:, None] == jnp.arange(adapters, dtype=jnp.int32)[None, :]
    placed = jnp.where(match[:, :, None], values[:, None, :], jnp.zeros((), values.dtype))
    return placed.reshape(values.shape[0], -1)

def key_adapter_term(shrunken_rows, adapter_position, upward_columns, column_begin, head_length):
    adapters, rank, columns = upward_columns.shape
    table = upward_columns.reshape(adapters * rank, columns)
    key_part = jnp.dot(spread_rows(shrunken_rows[:, rank:2 * rank], adapter_position, adapters), table, preferred_element_type=jnp.float32)
    value_part = jnp.dot(spread_rows(shrunken_rows[:, 2 * rank:], adapter_position, adapters), table, preferred_element_type=jnp.float32)
    whether_key = (column_begin + jnp.arange(columns, dtype=jnp.int32)) % (2 * head_length) < head_length
    return jnp.where(whether_key[None, :], key_part, value_part)

def routing(chosen, gates, experts, capacity):
    token_count = chosen.shape[0]
    choose = chosen[:, :, None] == jnp.arange(experts, dtype=jnp.int32)[None, None, :]
    gates_f = gates.astype(jnp.float32)
    share = gates_f / lax.optimization_barrier(jnp.sum(gates_f, axis=1, keepdims=True))
    weight = lax.optimization_barrier(jnp.sum(jnp.where(choose, share[:, :, None], 0.0), axis=1))
    hit = jnp.any(choose, axis=1)
    place = (jnp.cumsum(hit.astype(jnp.int32), axis=0) - 1).astype(jnp.int32)
    column = jnp.where(hit, place, capacity)
    expert_grid = jnp.broadcast_to(jnp.arange(experts, dtype=jnp.int32)[None, :], hit.shape)
    token_grid = jnp.broadcast_to(jnp.arange(token_count, dtype=jnp.int32)[:, None], hit.shape)
    slot_token = jnp.zeros((experts, capacity + 1), jnp.int32).at[expert_grid, column].set(token_grid)[:, :capacity]
    slot_weight = jnp.zeros((experts, capacity + 1), jnp.float32).at[expert_grid, column].set(weight)[:, :capacity]
    return (slot_token, slot_weight)

def attend(query_rows_out, keys, values, group, scale):
    grand_total = query_rows_out.shape[0]
    block = min(512, grand_total)
    position = jnp.arange(grand_total, dtype=jnp.int32)

    def one_block(number):
        first = number * block
        query_block = lax.dynamic_slice_in_dim(query_rows_out, first, block, 0)
        rows_here = first + jnp.arange(block, dtype=jnp.int32)
        group_here = lax.dynamic_slice_in_dim(group, first, block, 0)
        allowed = (position[None, :] <= rows_here[:, None]) & (group[None, :] == group_here[:, None])
        scores = jnp.einsum('qhd,kd->hqk', query_block.astype(jnp.float32), keys.astype(jnp.float32)) * scale
        raised = jnp.where(allowed[None], jnp.exp(scores), 0.0)
        shares = (raised / lax.optimization_barrier(jnp.sum(raised, axis=-1, keepdims=True))).astype(jnp.bfloat16)
        mixed = jnp.einsum('hqk,kd->qhd', shares.astype(jnp.float32), values.astype(jnp.float32))
        return mixed.astype(jnp.bfloat16).reshape(block, -1)
    return lax.map(one_block, jnp.arange(grand_total // block, dtype=jnp.int32)).reshape(grand_total, -1)

def reference(tokens, attn_gain, moe_gain, q_gain, k_gain, query_weight, w_kv, w_o, w_gate, w_up, w_down, shrink_qkv, shrink_o, query_up_factors, key_value_up_factors, expand_o, lengths, groups, adapter_of_request, adapter_slot, page_table, expert_ids, expert_gates):
    heads_per_shard = QUERY_HEADS // N_TENSOR
    width_dev = heads_per_shard * HEAD_DIM
    kv_rows = w_kv.transpose(1, 0, 2).reshape(KVW, D)

    def one_group(items):
        x_rows, length_row, group_row, adapter_row, page_row, expert_row, gate_row = items
        group, rope_pos, cell, adapter_position = token_layout(length_row, group_row, adapter_row, adapter_slot, page_row, GROUP_TOKENS)
        normalized_input = normalize(x_rows.astype(jnp.float32), attn_gain).astype(jnp.bfloat16)
        projected = jnp.einsum('td,ard->tar', normalized_input.astype(jnp.float32), shrink_qkv.astype(jnp.float32))
        match = adapter_position[:, None] == jnp.arange(ADAPTER_COUNT, dtype=jnp.int32)[None, :]
        shrunken_rows = lax.optimization_barrier(jnp.sum(jnp.where(match[:, :, None], projected, 0.0), axis=1)).astype(jnp.bfloat16)
        query_rows_out = jnp.dot(normalized_input, query_weight, preferred_element_type=jnp.float32) + ADAPTER_FACTOR * jnp.dot(spread_rows(shrunken_rows[:, :FACTOR_RANK], adapter_position, ADAPTER_COUNT), query_up_factors.reshape(ADAPTER_COUNT * FACTOR_RANK, QUERY_WIDTH), preferred_element_type=jnp.float32)
        query_rows_out = rotate(normalize(query_rows_out.reshape(GROUP_TOKENS, QUERY_HEADS, HEAD_DIM), q_gain), rope_pos).astype(jnp.bfloat16)
        key_value_rows = lax.dot_general(normalized_input, kv_rows, (((1,), (1,)), ((), ())), preferred_element_type=jnp.float32)
        key_value_rows = (key_value_rows + ADAPTER_FACTOR * key_adapter_term(shrunken_rows, adapter_position, key_value_up_factors, 0, HEAD_DIM)).astype(jnp.bfloat16)
        divided_key_value = key_value_rows.reshape(GROUP_TOKENS, KEY_VALUE_HEADS, 2, HEAD_DIM)
        keys = rotate(normalize(divided_key_value[:, :, 0].astype(jnp.float32), k_gain), rope_pos).astype(jnp.bfloat16)
        values = divided_key_value[:, :, 1]
        entries = jnp.stack([keys, values], axis=2).reshape(GROUP_TOKENS, KVW)
        pages = jnp.zeros((PAGES_DP * PAGE, KVW), jnp.bfloat16).at[cell].set(entries)
        pages = pages.reshape(PAGES_DP, PAGE, KVW).transpose(0, 2, 1)
        retained_mask = jnp.repeat(match, FACTOR_RANK, axis=1)
        upward_wide_rows = expand_o.reshape(ADAPTER_COUNT * FACTOR_RANK, D).astype(jnp.float32)

        def head_group(carry, index_value):
            query_part = lax.dynamic_slice_in_dim(query_rows_out, index_value * heads_per_shard, heads_per_shard, 1)
            key_value_head = index_value * heads_per_shard // (QUERY_HEADS // KEY_VALUE_HEADS)
            key_part = lax.dynamic_index_in_dim(keys, key_value_head, 1, keepdims=False)
            value_part = lax.dynamic_index_in_dim(values, key_value_head, 1, keepdims=False)
            mixed = attend(query_part, key_part, value_part, group, HEAD_DIM ** (-0.5))
            out_rows = lax.dynamic_slice_in_dim(w_o, index_value * width_dev, width_dev, 0)
            shrink_part = lax.dynamic_slice_in_dim(shrink_o, index_value * width_dev, width_dev, 2).reshape(ADAPTER_COUNT * FACTOR_RANK, width_dev)
            lower_rank_rows = lax.dot_general(mixed, shrink_part, (((1,), (1,)), ((), ())), preferred_element_type=jnp.float32)
            adapter_contribution = jnp.dot(mixed, out_rows, preferred_element_type=jnp.float32)
            adapter_contribution = adapter_contribution + ADAPTER_FACTOR * jnp.dot(jnp.where(retained_mask, lower_rank_rows, 0.0), upward_wide_rows, precision=lax.Precision.HIGHEST)
            return (carry + lax.optimization_barrier(adapter_contribution.astype(jnp.bfloat16)).astype(jnp.float32), None)
        attn_total, unused = lax.scan(head_group, jnp.zeros((GROUP_TOKENS, D), jnp.float32), jnp.arange(N_TENSOR, dtype=jnp.int32))
        residual = x_rows.astype(jnp.float32) + attn_total
        moe_in = normalize(residual, moe_gain).astype(jnp.bfloat16)
        slot_token, slot_weight = routing(expert_row, gate_row, EXPERTS, CAP)

        def expert_step(carry, parts):
            token_list, weight_list, gate_rows, up_rows, down_rows = parts
            gathered = moe_in[token_list]
            gate_value = lax.dot_general(gathered, gate_rows, (((1,), (1,)), ((), ())), preferred_element_type=jnp.float32)
            up_value = lax.dot_general(gathered, up_rows, (((1,), (1,)), ((), ())), preferred_element_type=jnp.float32)
            hidden = (jax.nn.silu(gate_value) * up_value).astype(jnp.bfloat16)
            out = lax.optimization_barrier(jnp.dot(hidden, down_rows, preferred_element_type=jnp.float32).astype(jnp.bfloat16))
            return (carry.at[token_list].add(out.astype(jnp.float32) * weight_list[:, None]), None)
        moe_total, unused = lax.scan(expert_step, jnp.zeros((GROUP_TOKENS, D), jnp.float32), (slot_token, slot_weight, w_gate, w_up, w_down))
        return (attn_total.astype(jnp.bfloat16), moe_total.astype(jnp.bfloat16), pages)
    results = lax.map(one_group, (tokens.reshape(N_DP, GROUP_TOKENS, D), lengths, groups, adapter_of_request, page_table, expert_ids.reshape(N_DP, GROUP_TOKENS, TOPK), expert_gates.reshape(N_DP, GROUP_TOKENS, TOPK)))
    return (results[0].reshape(TOKENS, D), results[1].reshape(TOKENS, D), results[2].reshape(PAGES, KVW, PAGE))
```

```python
import math

import jax
import jax.numpy as jnp
from jax import lax
from jax.sharding import PartitionSpec as P

EXPERTS = 64
PAGE = 128
CAP_DEV = 16


NORM_EPS = 1e-06
ROPE_BASE = 1000000.0
ADAPTER_FACTOR = 0.5


def normalize(values, gain):
    return (
        values
        * lax.rsqrt(jnp.mean(values * values, axis=-1, keepdims=True) + NORM_EPS)
        * gain.astype(jnp.float32)
    )


def rotate(values, position):
    half = values.shape[-1] // 2
    freq = jnp.exp(
        -jnp.arange(half, dtype=jnp.float32) * (2.0 * math.log(ROPE_BASE) / values.shape[-1])
    )
    angle = position.astype(jnp.float32)[:, None, None] * freq[None, None, :]
    cosine = jnp.cos(angle)
    sine = jnp.sin(angle)
    first = values[..., :half]
    second = values[..., half:]
    return jnp.concatenate(
        [first * cosine - second * sine, second * cosine + first * sine], axis=-1
    )


def lookup(index_value, table):
    match = index_value[:, None] == jnp.arange(table.shape[0], dtype=jnp.int32)[None, :]
    return jnp.sum(jnp.where(match, table[None, :], 0), axis=1)


def token_layout(length_row, group_row, adapter_row, adapter_slot, page_row, grand_total):
    position = jnp.arange(grand_total, dtype=jnp.int32)
    ends = jnp.cumsum(length_row)
    starts = ends - length_row
    request = jnp.sum((ends[None, :] <= position[:, None]).astype(jnp.int32), axis=1)
    group = lookup(request, group_row)
    same = group_row[:, None] == group_row[None, :]
    group_first = jnp.min(jnp.where(same, starts[None, :], grand_total), axis=1)
    rope_pos = position - lookup(request, group_first)
    offset = position - lookup(request, starts)
    per_request = page_row.shape[0] // length_row.shape[0]
    page = lookup(request * per_request + offset // PAGE, page_row)
    cell = page * PAGE + offset % PAGE
    adapter_position = lookup(request, lookup(adapter_row, adapter_slot))
    return (group, rope_pos, cell, adapter_position)


def spread_rows(values, adapter_position, adapters):
    match = adapter_position[:, None] == jnp.arange(adapters, dtype=jnp.int32)[None, :]
    placed = jnp.where(match[:, :, None], values[:, None, :], jnp.zeros((), values.dtype))
    return placed.reshape(values.shape[0], -1)


def attend(query_rows_out, keys, values, group, scale):
    grand_total = query_rows_out.shape[0]
    block = min(512, grand_total)
    position = jnp.arange(grand_total, dtype=jnp.int32)

    def one_block(number):
        first = number * block
        query_block = lax.dynamic_slice_in_dim(query_rows_out, first, block, 0)
        rows_here = first + jnp.arange(block, dtype=jnp.int32)
        group_here = lax.dynamic_slice_in_dim(group, first, block, 0)
        allowed = (position[None, :] <= rows_here[:, None]) & (
            group[None, :] == group_here[:, None]
        )
        scores = (
            jnp.einsum("qhd,kd->hqk", query_block, keys, preferred_element_type=jnp.float32) * scale
        )
        raised = jnp.where(allowed[None], jnp.exp(scores), 0.0)
        shares = (raised / jnp.sum(raised, axis=-1, keepdims=True)).astype(jnp.bfloat16)
        mixed = jnp.einsum("hqk,kd->qhd", shares, values, preferred_element_type=jnp.float32)
        return mixed.astype(jnp.bfloat16).reshape(block, -1)

    return lax.map(one_block, jnp.arange(grand_total // block, dtype=jnp.int32)).reshape(
        grand_total, -1
    )


def expert_apply(rows, gate_rows, up_rows, down_rows):
    gate_value = jnp.einsum("secx,efx->secf", rows, gate_rows, preferred_element_type=jnp.float32)
    up_value = jnp.einsum("secx,efx->secf", rows, up_rows, preferred_element_type=jnp.float32)
    hidden = (jax.nn.silu(gate_value) * up_value).astype(jnp.bfloat16)
    out = jnp.einsum("secf,efx->secx", hidden, down_rows, preferred_element_type=jnp.float32)
    return lax.optimization_barrier(out.astype(jnp.bfloat16))


def local(
    tokens,
    attn_gain,
    moe_gain,
    q_gain,
    k_gain,
    query_weight,
    w_kv,
    w_o,
    w_gate,
    w_up,
    w_down,
    shrink_qkv,
    shrink_o,
    query_up_factors,
    key_value_up_factors,
    expand_o,
    lengths,
    groups,
    adapter_of_request,
    adapter_slot,
    page_table,
    expert_ids,
    expert_gates,
):
    parts = lax.axis_size("tensor")
    place = lax.axis_index("tensor")
    own_rows, width = tokens.shape
    grand_total = own_rows * parts
    head_length = q_gain.shape[0]
    adapters, rank, kv_width = key_value_up_factors.shape
    key_value_heads = kv_width // (2 * head_length)
    group, rope_pos, cell, adapter_position = token_layout(
        lengths[0], groups[0], adapter_of_request[0], adapter_slot, page_table[0], grand_total
    )
    own_slot = lax.dynamic_slice_in_dim(adapter_position, place * own_rows, own_rows, 0)
    normed_own = normalize(tokens.astype(jnp.float32), attn_gain).astype(jnp.bfloat16)
    piece = lax.all_gather(shrink_qkv, "dp", axis=0, tiled=True)
    projected = jnp.einsum("td,prd->tpr", normed_own, piece, preferred_element_type=jnp.float32)
    match = own_slot[:, None] == jnp.arange(piece.shape[0], dtype=jnp.int32)[None, :]
    shrunk_own = jnp.sum(jnp.where(match[:, :, None], projected, 0.0), axis=1)
    shrunk_own = shrunk_own.astype(jnp.bfloat16)
    normalized_input, shrunken_rows = (
        lax.all_gather(normed_own, "tensor", axis=0, tiled=True),
        lax.all_gather(shrunk_own, "tensor", axis=0, tiled=True),
    )
    head = place * key_value_heads // parts
    local_cols = kv_width // parts
    token_extent = w_kv.shape[0]
    span_begin = place * token_extent
    base_key_value = jnp.einsum(
        "td,chd->thc", normalized_input, w_kv, preferred_element_type=jnp.float32
    )
    upward_split = key_value_up_factors.reshape(adapters, rank, key_value_heads, 2 * head_length)
    upward_local = lax.dynamic_slice_in_dim(upward_split, span_begin, token_extent, 3).reshape(
        adapters * rank, key_value_heads * token_extent
    )
    key_adapter_delta = jnp.dot(
        spread_rows(shrunken_rows[:, rank : 2 * rank], adapter_position, adapters),
        upward_local,
        preferred_element_type=jnp.float32,
    )
    value_adapter_delta = jnp.dot(
        spread_rows(shrunken_rows[:, 2 * rank :], adapter_position, adapters),
        upward_local,
        preferred_element_type=jnp.float32,
    )
    whether_key = jnp.tile(
        span_begin + jnp.arange(token_extent, dtype=jnp.int32) < head_length, key_value_heads
    )
    adapter_delta_term = jnp.where(
        whether_key[None, :], key_adapter_delta, value_adapter_delta
    ).reshape(grand_total, key_value_heads, token_extent)
    resident_key_value = (base_key_value + ADAPTER_FACTOR * adapter_delta_term).astype(jnp.bfloat16)
    every_kv = lax.all_gather(resident_key_value, "tensor", axis=2, tiled=True)
    head_kv = lax.dynamic_index_in_dim(every_kv, head, 1, keepdims=False)
    divided_key_value = head_kv.reshape(grand_total, 2, head_length)
    keys = rotate(normalize(divided_key_value[:, :1].astype(jnp.float32), k_gain), rope_pos).astype(
        jnp.bfloat16
    )[:, 0]
    values = divided_key_value[:, 1]
    entries = jnp.concatenate([keys, values], axis=1)
    mine = lax.dynamic_slice_in_dim(
        entries, place * local_cols - head * 2 * head_length, local_cols, 1
    )
    pages_held = page_table.shape[1]
    kv_pages = jnp.zeros((pages_held * PAGE, local_cols), jnp.bfloat16).at[cell].set(mine)
    kv_pages = kv_pages.reshape(pages_held, PAGE, local_cols).transpose(0, 2, 1)
    query_cols = query_weight.shape[1]
    heads_here = query_cols // head_length
    query_rows_out = jnp.dot(
        normalized_input, query_weight, preferred_element_type=jnp.float32
    ) + ADAPTER_FACTOR * jnp.dot(
        spread_rows(shrunken_rows[:, :rank], adapter_position, adapters),
        query_up_factors.reshape(adapters * rank, query_cols),
        preferred_element_type=jnp.float32,
    )
    query_rows_out = rotate(
        normalize(query_rows_out.reshape(grand_total, heads_here, head_length), q_gain), rope_pos
    ).astype(jnp.bfloat16)
    mixed = attend(query_rows_out, keys, values, group, head_length ** (-0.5))
    shrink_table = shrink_o.reshape(adapters * rank, query_cols)
    upward_wide_rows = expand_o.reshape(adapters * rank, width).astype(jnp.float32)
    lower_rank_rows = lax.dot_general(
        mixed, shrink_table, (((1,), (1,)), ((), ())), preferred_element_type=jnp.float32
    )
    retained_mask = jnp.repeat(
        adapter_position[:, None] == jnp.arange(adapters, dtype=jnp.int32)[None, :], rank, axis=1
    )
    adapter_contribution = jnp.dot(mixed, w_o, preferred_element_type=jnp.float32)
    attn_own = lax.psum_scatter(
        (
            adapter_contribution
            + ADAPTER_FACTOR
            * jnp.dot(
                jnp.where(retained_mask, lower_rank_rows, 0.0),
                upward_wide_rows,
                precision=lax.Precision.HIGHEST,
            )
        ).astype(jnp.bfloat16),
        "tensor",
        scatter_dimension=0,
        tiled=True,
    ).astype(jnp.float32)
    moe_own = normalize(tokens.astype(jnp.float32) + attn_own, moe_gain).astype(jnp.bfloat16)
    experts_here = w_gate.shape[0]
    moe_in = lax.all_gather(moe_own, "tensor", axis=0, tiled=True)
    own_experts = place * experts_here + jnp.arange(experts_here, dtype=jnp.int32)
    choose = expert_ids[:, :, None] == own_experts[None, None, :]
    share = expert_gates / jnp.sum(expert_gates, axis=1, keepdims=True)
    weight = jnp.sum(jnp.where(choose, share[:, :, None], 0.0), axis=1)
    hit = jnp.any(choose, axis=1).reshape(parts, own_rows, experts_here)
    weight = weight.reshape(parts, own_rows, experts_here)
    below = jnp.tril(jnp.ones((own_rows, own_rows), jnp.bfloat16))
    rank_in_block = jnp.einsum(
        "ut,ste->sue", below, hit.astype(jnp.bfloat16), preferred_element_type=jnp.float32
    )
    numbers = jnp.arange(1, CAP_DEV + 1, dtype=jnp.float32)
    picked = hit[..., None] & (rank_in_block[..., None] == numbers)
    pick = picked.astype(jnp.bfloat16)
    slot_weight = jnp.sum(jnp.where(picked, weight[..., None], 0.0), axis=1)
    rows = jnp.einsum(
        "stek,std->eskd",
        pick,
        moe_in.reshape(parts, own_rows, width),
        preferred_element_type=jnp.float32,
    ).astype(jnp.bfloat16)
    rows = rows.reshape(1, experts_here, parts * CAP_DEV, width)
    outputs = expert_apply(rows, w_gate, w_up, w_down)[0]
    slot_weight = slot_weight.transpose(1, 0, 2).reshape(experts_here, parts * CAP_DEV, 1)
    weighted = (outputs.astype(jnp.float32) * slot_weight).astype(jnp.bfloat16)
    moe_terms = jnp.einsum(
        "stek,eskd->std",
        pick,
        weighted.reshape(experts_here, parts, CAP_DEV, width),
        preferred_element_type=jnp.float32,
    ).reshape(grand_total, width)
    moe_total = lax.psum_scatter(
        moe_terms.astype(jnp.bfloat16), "tensor", scatter_dimension=0, tiled=True
    )
    return (attn_own.astype(jnp.bfloat16), moe_total, kv_pages)


def solution(mesh):
    placed = (
        P(("dp", "tensor"), None),
        P(),
        P(),
        P(),
        P(),
        P(None, "tensor"),
        P("tensor", None, None),
        P("tensor", None),
        P("tensor", None, None),
        P("tensor", None, None),
        P("tensor", None, None),
        P("dp", None, None),
        P(None, None, "tensor"),
        P(None, None, "tensor"),
        P(),
        P(),
        P("dp", None),
        P("dp", None),
        P("dp", None),
        P(),
        P("dp", None),
        P("dp", None),
        P("dp", None),
    )
    return jax.shard_map(
        local,
        mesh=mesh,
        in_specs=placed,
        out_specs=(P(("dp", "tensor"), None), P(("dp", "tensor"), None), P("dp", "tensor", None)),
        check_vma=False,
    )
```

```python
import functools
import math
import jax, jax.numpy as jnp
from jax import lax
from jax.experimental import pallas as pl
from jax.experimental.pallas import tpu as pltpu
from jax.sharding import PartitionSpec as P

SIDE = 4
HALF = 32

def spot(z, y, core):
    return lax.rem(z, SIDE) * 8 + lax.rem(y, SIDE) * 2 + core

def whereabouts():
    me = lax.axis_index("tensor")
    return me, lax.div(me, 8), lax.rem(lax.div(me, 2), SIDE), lax.rem(me, 2)

def greet(partners):
    barrier = pltpu.get_barrier_semaphore()
    for partner in partners:
        pl.semaphore_signal(barrier, inc=1, device_id={"tensor": partner}, device_id_type=pl.DeviceIdType.MESH)
    pl.semaphore_wait(barrier, len(partners))

class Copies:
    def __init__(self, send, recv):
        self.send, self.recv, self.n, self.all = send, recv, 0, []
    def make(self, src, dst, axis, target):
        k = self.n
        self.n += 1
        copy = pltpu.make_async_remote_copy(src_ref=src, dst_ref=dst, send_sem=self.send.at[k], recv_sem=self.recv.at[k],
            device_id={axis: target}, device_id_type=pl.DeviceIdType.MESH)
        self.all.append(copy)
        return copy
    def go(self, src, dst, axis, target):
        copy = self.make(src, dst, axis, target)
        copy.start()
        return copy
    def finish(self):
        for copy in self.all:
            copy.wait_send()

def gather_rows(out, z, y, core, copies, hooks=()):
    hooks = list(hooks)
    def hook():
        if hooks:
            hooks.pop(0)()
    side = spot(z, y, 1 - core)
    shared = []
    def share(block, row, rows):
        piece = out.at[block, pl.ds(row, rows)]
        shared.append(copies.go(piece, piece, "tensor", side))
    def send(block, row, rows, target):
        piece = out.at[block, pl.ds(row, rows)]
        return copies.go(piece, piece, "tensor", target)
    class Part: pass
    parts = []
    for number in range(2):
        p = Part()
        p.row = number * HALF
        if number == 0:
            p.at = lambda u, v: spot(z + v, y + u, core)
        else:
            p.at = lambda u, v: spot(z + u, y + v, core)
        parts.append(p)
    def ring_open(p, along_u, u):
        block = p.at(u, 0)
        up, down = (p.at(1, 0), p.at(3, 0)) if along_u else (p.at(0, 1), p.at(0, 3))
        return [send(block, p.row, HALF, up), send(block, p.row, HALF, down)]
    def ring_pass(p, along_u, u, opened, which):
        opened[which].wait_recv()
        off = 3 if which == 0 else 1
        block = p.at(off, 0) if along_u else p.at(u, off)
        target = (p.at(1, 0), p.at(3, 0))[which] if along_u else (p.at(0, 1), p.at(0, 3))[which]
        fwd = send(block, p.row + which * (HALF // 2), HALF // 2, target)
        share(block, p.row, HALF)
        return fwd
    me = spot(z, y, core)
    for p in parts:
        p.u = ring_open(p, True, 0)
    for p in parts:
        p.v = {0: ring_open(p, False, 0)}
    share(me, 0, 2 * HALF)
    hook()
    for which in range(2):
        for p in parts:
            p.u.append(ring_pass(p, True, 0, p.u, which))
            off = 3 if which == 0 else 1
            p.v[off] = ring_open(p, False, off)
    for which in range(2):
        for p in parts:
            p.v[0].append(ring_pass(p, False, 0, p.v[0], which))
    hook()
    for p in parts:
        p.u[2].wait_recv()
        p.u[3].wait_recv()
        share(p.at(2, 0), p.row, HALF)
        p.v[2] = ring_open(p, False, 2)
    for off in (3, 1):
        for which in range(2):
            for p in parts:
                p.v[off].append(ring_pass(p, False, off, p.v[off], which))
        for p in parts:
            done = 0 if off == 3 else 3
            p.v[done][2].wait_recv()
            p.v[done][3].wait_recv()
            share(p.at(done, 2), p.row, HALF)
        hook()
    for which in range(2):
        for p in parts:
            p.v[2].append(ring_pass(p, False, 2, p.v[2], which))
    for off in (1, 2):
        for p in parts:
            p.v[off][2].wait_recv()
            p.v[off][3].wait_recv()
            share(p.at(off, 2), p.row, HALF)
    for copy in shared:
        copy.wait_recv()

def add_rows(dst, start, rows, sources):
    for first in range(0, rows, 16):
        total = dst[pl.ds(start + first, 16)].astype(jnp.float32)
        for ref, row in sources:
            total = total + ref[pl.ds(row + first, 16)].astype(jnp.float32)
        dst[pl.ds(start + first, 16)] = total.astype(dst.dtype)

ORDER = (2, 1, 3, 0)
SCATTER_COPIES = 32 + 32 + 8

def scatter_rows(terms, acc, sib, landed, local, z, y, core, copies, result):
    side = spot(z, y, 1 - core)
    loads, shared = {}, {}
    def cell(number, v, u):
        return (v, u) if number == 0 else (u, v)
    for v in ORDER:
        for u in ORDER:
            for number in range(2):
                i, j = cell(number, v, u)
                rows = pl.ds(number * HALF, HALF)
                shared[number, v, u] = copies.go(
                    terms.at[spot(z + i, y + j, 1 - core), rows], sib.at[i, j, rows], "tensor", side)
                load = pltpu.make_async_copy(
                    terms.at[spot(z + i, y + j, core), rows], acc.at[i, j, rows], local.at[number * 16 + v * 4 + u])
                load.start()
                loads[number, v, u] = load
    def neighbour(number, along_v, step):
        along_z = (number == 0) == along_v
        return spot(z + step, y, core) if along_z else spot(z, y + step, core)
    def own(number, v, u):
        return acc.at[cell(number, v, u)]
    def pair(number, v, u):
        loads[number, v, u].wait()
        shared[number, v, u].wait_recv()
        return (sib.at[cell(number, v, u)], number * HALF)
    def buf(number, u):
        return landed.at[number * 5 + u]
    ring = {}
    def far(number, along_v, u, block):
        row = number * HALF
        b = buf(number, u)
        key = (number, u)
        ring[key] = [
            copies.go(block.at[pl.ds(row, 16)], b.at[pl.ds(0, 16)], "tensor", neighbour(number, along_v, 1)),
            copies.go(block.at[pl.ds(row + 16, 16)], b.at[pl.ds(16, 16)], "tensor", neighbour(number, along_v, 3)),
        ]
    def near(number, along_v, u, block, which):
        row = number * HALF
        b = buf(number, u)
        ring[number, u].append(
            copies.go(block.at[pl.ds(row, HALF)], b.at[pl.ds(32 + 32 * which, HALF)], "tensor",
                      neighbour(number, along_v, (1, 3)[which])))
    for u in ORDER:
        for number in range(2):
            block = own(number, 2, u)
            add_rows(block, number * HALF, HALF, [pair(number, 2, u)])
            far(number, True, u, block)
    for u in ORDER:
        for number in range(2):
            row = number * HALF
            for which in range(2):
                v = (1, 3)[which]
                block = own(number, v, u)
                other, first = pair(number, v, u)
                ring[number, u][which].wait_recv()
                for part in range(2):
                    sources = [(other, first + 16 * part)]
                    if part == which:
                        sources.append((buf(number, u), 16 * which))
                    add_rows(block, row + 16 * part, 16, sources)
                near(number, True, u, block, which)
    for u in ORDER:
        for number in range(2):
            row = number * HALF
            block = own(number, 0, u)
            source = pair(number, 0, u)
            b = buf(number, u)
            ring[number, u][2].wait_recv()
            ring[number, u][3].wait_recv()
            sources = [source, (b, 32), (b, 64)]
            last = buf(number, 4)
            if u == 2:
                add_rows(block, row, HALF, sources)
                far(number, False, 4, block)
            elif u in (1, 3):
                which = (1, 3).index(u)
                ring[number, 4][which].wait_recv()
                for part in range(2):
                    more = [(ref, r + 16 * part) for ref, r in sources]
                    if part == which:
                        more.append((last, 16 * which))
                    add_rows(block, row + 16 * part, 16, more)
                near(number, False, 4, block, which)
            else:
                ring[number, 4][2].wait_recv()
                ring[number, 4][3].wait_recv()
                for first in range(0, HALF, 16):
                    total = block[pl.ds(row + first, 16)].astype(jnp.float32)
                    for ref, r in sources + [(last, 32), (last, 64)]:
                        total = total + ref[pl.ds(r + first, 16)].astype(jnp.float32)
                    result[pl.ds(row + first, 16)] = total

def scatter_scratch(width):
    return [
        pltpu.VMEM((4, 4, 64, width), jnp.bfloat16),
        pltpu.VMEM((4, 4, 64, width), jnp.bfloat16),
        pltpu.VMEM((10, 96, width), jnp.bfloat16),
        pltpu.SemaphoreType.DMA((32,)),
    ]

def partners(z, y, core):
    return [spot(z, y, 1 - core), spot(z + 1, y, core), spot(z + 3, y, core), spot(z, y + 1, core), spot(z, y + 3, core)]


GATHER_COPIES = 2 * 20 + 31
EXTRA_COPIES = 7 + 11
NORM_EPS = 1e-06
ROPE_BASE = 1000000.0
ADAPTER_FACTOR = 0.5
PAGE = 128
CAP_DEV = 16


def normalize(values, gain):
    return (
        values
        * lax.rsqrt(jnp.mean(values * values, axis=-1, keepdims=True) + NORM_EPS)
        * gain.astype(jnp.float32)
    )


def enter_kernel(
    tokens_ref, gain_ref, shrink_ref, wkv_ref, rows_ref, factors_ref, wkv_all_ref, local, send, recv
):
    me, z, y, core = whereabouts()
    group = lax.axis_index("dp")
    up, down = lax.rem(group + 1, SIDE), lax.rem(group + 3, SIDE)
    across = lax.rem(group + 2, SIDE)
    copies = Copies(send, recv)
    homes = [
        pltpu.make_async_copy(shrink_ref, factors_ref.at[pl.ds(4 * group, 4)], local.at[0]),
        pltpu.make_async_copy(wkv_ref.at[z], wkv_all_ref.at[y, core, z], local.at[1]),
    ]
    for home in homes:
        home.start()
    rows_ref[me] = normalize(tokens_ref[...].astype(jnp.float32), gain_ref[...]).astype(
        rows_ref.dtype
    )
    barrier = pltpu.get_barrier_semaphore()
    near = partners(z, y, core) + [spot(z + 2, y, core)]
    for partner in near:
        pl.semaphore_signal(
            barrier, inc=1, device_id={"tensor": partner}, device_id_type=pl.DeviceIdType.MESH
        )
    for partner in (up, down):
        pl.semaphore_signal(
            barrier, inc=1, device_id={"dp": partner}, device_id_type=pl.DeviceIdType.MESH
        )
    pl.semaphore_wait(barrier, len(near) + 2)
    side = spot(z, y, 1 - core)
    state = {}

    def open_extras():
        spread = []
        for step in (1, 3, 2):
            there = lax.rem(z + step, SIDE)
            spread.append(
                copies.go(
                    wkv_ref.at[there], wkv_all_ref.at[y, core, z], "tensor", spot(there, y, core)
                )
            )
        state["spread"] = spread
        half = factors_ref.at[pl.ds(4 * group + 2 * core, 2)]
        mine = shrink_ref.at[pl.ds(2 * core, 2)]
        state["factors"] = [copies.go(mine, half, "dp", up), copies.go(mine, half, "dp", down)]

    def kv(y_at, first=0, count=4):
        return wkv_all_ref.at[lax.rem(y_at, SIDE), core, pl.ds(first, count)]

    def middle_extras():
        for copy in state["spread"]:
            copy.wait_recv()
        homes[1].wait()
        block = kv(y)
        state["kv"] = [
            copies.go(block, block, "tensor", spot(z, y + 1, core)),
            copies.go(block, block, "tensor", spot(z, y + 3, core)),
        ]
        state["shared"] = [copies.go(block, block, "tensor", side)]
        for which, (origin, target) in enumerate(((down, up), (up, down))):
            state["factors"][which].wait_recv()
            one = factors_ref.at[4 * origin + 2 * core + which]
            state["factors"].append(copies.go(one, one, "dp", target))
            both = factors_ref.at[pl.ds(4 * origin + 2 * core, 2)]
            state["shared"].append(copies.go(both, both, "tensor", side))

    def pass_extras():
        for which, (origin, target) in enumerate(((y + 3, y + 1), (y + 1, y + 3))):
            state["kv"][which].wait_recv()
            piece = kv(origin, 2 * which, 2)
            state["kv"].append(copies.go(piece, piece, "tensor", spot(z, target, core)))
            whole = kv(origin)
            state["shared"].append(copies.go(whole, whole, "tensor", side))
        state["factors"][2].wait_recv()
        state["factors"][3].wait_recv()
        both = factors_ref.at[pl.ds(4 * across + 2 * core, 2)]
        state["shared"].append(copies.go(both, both, "tensor", side))

    def close_extras():
        state["kv"][2].wait_recv()
        state["kv"][3].wait_recv()
        whole = kv(y + 2)
        state["shared"].append(copies.go(whole, whole, "tensor", side))

    open_extras()
    gather_rows(rows_ref, z, y, core, copies, [middle_extras, pass_extras, close_extras])
    for copy in state["shared"]:
        copy.wait_recv()
    homes[0].wait()
    copies.finish()
    assert copies.n == GATHER_COPIES + EXTRA_COPIES, copies.n


def enter(tokens, gain, shrink, wkv):
    rows, width = tokens.shape
    count = GATHER_COPIES + EXTRA_COPIES
    return pl.pallas_call(
        enter_kernel,
        out_shape=(
            jax.ShapeDtypeStruct((32, rows, width), jnp.bfloat16),
            jax.ShapeDtypeStruct((4 * shrink.shape[0],) + shrink.shape[1:], jnp.bfloat16),
            jax.ShapeDtypeStruct((4, 2) + wkv.shape, jnp.bfloat16),
        ),
        in_specs=[
            pl.BlockSpec(memory_space=pltpu.VMEM),
            pl.BlockSpec(memory_space=pltpu.VMEM),
            pl.BlockSpec(memory_space=pl.ANY),
            pl.BlockSpec(memory_space=pl.ANY),
        ],
        out_specs=(
            pl.BlockSpec(memory_space=pltpu.VMEM),
            pl.BlockSpec(memory_space=pl.ANY),
            pl.BlockSpec(memory_space=pl.ANY),
        ),
        scratch_shapes=[
            pltpu.SemaphoreType.DMA((2,)),
            pltpu.SemaphoreType.DMA((count,)),
            pltpu.SemaphoreType.DMA((count,)),
        ],
        compiler_params=pltpu.CompilerParams(
            collective_id=0, has_side_effects=True, vmem_limit_bytes=32 << 20
        ),
    )(tokens, gain.reshape(1, width), shrink, wkv)


def middle_kernel(
    terms_ref, tokens_ref, gain_ref, out_ref, rows_ref, acc, sib, landed, local, total, send, recv
):
    me, z, y, core = whereabouts()
    greet(partners(z, y, core))
    copies = Copies(send, recv)
    scatter_rows(terms_ref, acc, sib, landed, local, z, y, core, copies, total)
    summed = total[...]
    out_ref[...] = summed.astype(out_ref.dtype)
    rows_ref[me] = normalize(tokens_ref[...].astype(jnp.float32) + summed, gain_ref[...]).astype(
        rows_ref.dtype
    )
    gather_rows(rows_ref, z, y, core, copies)
    copies.finish()
    assert copies.n == SCATTER_COPIES + GATHER_COPIES, copies.n


def middle(terms, tokens, gain):
    rows, width = tokens.shape
    count = SCATTER_COPIES + GATHER_COPIES
    vmem = pl.BlockSpec(memory_space=pltpu.VMEM)
    return pl.pallas_call(
        middle_kernel,
        out_shape=(
            jax.ShapeDtypeStruct((rows, width), jnp.bfloat16),
            jax.ShapeDtypeStruct((32, rows, width), jnp.bfloat16),
        ),
        in_specs=[pl.BlockSpec(memory_space=pl.ANY), vmem, vmem],
        out_specs=(vmem, vmem),
        scratch_shapes=scatter_scratch(width)
        + [
            pltpu.VMEM((rows, width), jnp.float32),
            pltpu.SemaphoreType.DMA((count,)),
            pltpu.SemaphoreType.DMA((count,)),
        ],
        compiler_params=pltpu.CompilerParams(
            collective_id=1, has_side_effects=True, vmem_limit_bytes=40 << 20
        ),
    )(terms, tokens, gain.reshape(1, width))


def leave_kernel(terms_ref, out_ref, acc, sib, landed, local, total, send, recv):
    me, z, y, core = whereabouts()
    greet(partners(z, y, core))
    copies = Copies(send, recv)
    scatter_rows(terms_ref, acc, sib, landed, local, z, y, core, copies, total)
    out_ref[...] = total[...].astype(out_ref.dtype)
    copies.finish()
    assert copies.n == SCATTER_COPIES, copies.n


def leave(terms):
    rows, width = terms.shape[1:]
    return pl.pallas_call(
        leave_kernel,
        out_shape=jax.ShapeDtypeStruct((rows, width), jnp.bfloat16),
        in_specs=[pl.BlockSpec(memory_space=pl.ANY)],
        out_specs=pl.BlockSpec(memory_space=pltpu.VMEM),
        scratch_shapes=scatter_scratch(width)
        + [
            pltpu.VMEM((rows, width), jnp.float32),
            pltpu.SemaphoreType.DMA((SCATTER_COPIES,)),
            pltpu.SemaphoreType.DMA((SCATTER_COPIES,)),
        ],
        compiler_params=pltpu.CompilerParams(
            collective_id=2, has_side_effects=True, vmem_limit_bytes=32 << 20
        ),
    )(terms)


def rotate(values, position):
    half = values.shape[-1] // 2
    freq = jnp.exp(
        -jnp.arange(half, dtype=jnp.float32) * (2.0 * math.log(ROPE_BASE) / values.shape[-1])
    )
    angle = position.astype(jnp.float32)[:, None, None] * freq[None, None, :]
    cosine = jnp.cos(angle)
    sine = jnp.sin(angle)
    first = values[..., :half]
    second = values[..., half:]
    return jnp.concatenate(
        [first * cosine - second * sine, second * cosine + first * sine], axis=-1
    )


def lookup(index_value, table):
    match = index_value[:, None] == jnp.arange(table.shape[0], dtype=jnp.int32)[None, :]
    return jnp.sum(jnp.where(match, table[None, :], 0), axis=1)


def token_layout(length_row, group_row, adapter_row, adapter_slot, page_row, grand_total):
    position = jnp.arange(grand_total, dtype=jnp.int32)
    ends = jnp.cumsum(length_row)
    starts = ends - length_row
    request = jnp.sum((ends[None, :] <= position[:, None]).astype(jnp.int32), axis=1)
    group = lookup(request, group_row)
    same = group_row[:, None] == group_row[None, :]
    group_first = jnp.min(jnp.where(same, starts[None, :], grand_total), axis=1)
    rope_pos = position - lookup(request, group_first)
    offset = position - lookup(request, starts)
    per_request = page_row.shape[0] // length_row.shape[0]
    page = lookup(request * per_request + offset // PAGE, page_row)
    cell = page * PAGE + offset % PAGE
    adapter_position = lookup(request, lookup(adapter_row, adapter_slot))
    return (group, rope_pos, cell, adapter_position)


def attend(query_rows_out, keys, values, group, scale):
    grand_total = query_rows_out.shape[0]
    block = min(512, grand_total)
    position = jnp.arange(grand_total, dtype=jnp.int32)

    def one_block(number):
        first = number * block
        query_block = lax.dynamic_slice_in_dim(query_rows_out, first, block, 0)
        rows_here = first + jnp.arange(block, dtype=jnp.int32)
        group_here = lax.dynamic_slice_in_dim(group, first, block, 0)
        allowed = (position[None, :] <= rows_here[:, None]) & (
            group[None, :] == group_here[:, None]
        )
        scores = (
            jnp.einsum("qhd,kd->hqk", query_block, keys, preferred_element_type=jnp.float32) * scale
        )
        raised = jnp.where(allowed[None], jnp.exp(scores), 0.0)
        shares = (raised / jnp.sum(raised, axis=-1, keepdims=True)).astype(jnp.bfloat16)
        mixed = jnp.einsum("hqk,kd->qhd", shares, values, preferred_element_type=jnp.float32)
        return mixed.astype(jnp.bfloat16).reshape(block, -1)

    return lax.map(one_block, jnp.arange(grand_total // block, dtype=jnp.int32)).reshape(
        grand_total, -1
    )


def expert_apply(rows, gate_rows, up_rows, down_rows):
    gate_value = jnp.einsum("secx,efx->secf", rows, gate_rows, preferred_element_type=jnp.float32)
    up_value = jnp.einsum("secx,efx->secf", rows, up_rows, preferred_element_type=jnp.float32)
    hidden = (jax.nn.silu(gate_value) * up_value).astype(jnp.bfloat16)
    out = jnp.einsum("secf,efx->secx", hidden, down_rows, preferred_element_type=jnp.float32)
    return lax.optimization_barrier(out.astype(jnp.bfloat16))


def local(
    tokens,
    attn_gain,
    moe_gain,
    q_gain,
    k_gain,
    query_weight,
    w_kv,
    w_o,
    w_gate,
    w_up,
    w_down,
    shrink_qkv,
    shrink_o,
    query_up_factors,
    key_value_up_factors,
    expand_o,
    lengths,
    groups,
    adapter_of_request,
    adapter_slot,
    page_table,
    expert_ids,
    expert_gates,
):
    parts = lax.axis_size("tensor")
    place = lax.axis_index("tensor")
    own_rows, width = tokens.shape
    grand_total = own_rows * parts
    head_length = q_gain.shape[0]
    adapters, rank, kv_width = key_value_up_factors.shape
    key_value_heads = kv_width // (2 * head_length)
    group, rope_pos, cell, adapter_position = token_layout(
        lengths[0], groups[0], adapter_of_request[0], adapter_slot, page_table[0], grand_total
    )
    x_rows, factors, wkv_all = enter(tokens, attn_gain, shrink_qkv, w_kv.transpose(1, 0, 2))
    normed = x_rows.reshape(grand_total, width)
    head = place * key_value_heads // parts
    local_cols = kv_width // parts
    head_width = 2 * head_length
    wkv_head = wkv_all.transpose(2, 0, 1, 3, 4).reshape(head_width, width)
    ranks = 3 * rank
    projected = lax.dot_general(
        normed,
        factors.reshape(adapters * ranks, width),
        (((1,), (1,)), ((), ())),
        preferred_element_type=jnp.float32,
    )
    slots = jnp.repeat(jnp.arange(adapters, dtype=jnp.int32), ranks)
    placed = jnp.where(adapter_position[:, None] == slots[None, :], projected, 0.0).astype(
        jnp.bfloat16
    )
    query_cols = query_weight.shape[1]
    heads_here = query_cols // head_length
    kv_up = lax.dynamic_slice_in_dim(key_value_up_factors, head * head_width, head_width, 2)
    raise_table = jnp.zeros((adapters, 3, rank, query_cols + head_width), jnp.bfloat16)
    raise_table = raise_table.at[:, 0, :, :query_cols].set(query_up_factors)
    raise_table = raise_table.at[:, 1, :, query_cols : query_cols + head_length].set(
        kv_up[:, :, :head_length]
    )
    raise_table = raise_table.at[:, 2, :, query_cols + head_length :].set(kv_up[:, :, head_length:])
    lora = ADAPTER_FACTOR * jnp.dot(
        placed,
        raise_table.reshape(adapters * ranks, query_cols + head_width),
        preferred_element_type=jnp.float32,
    )
    base_kv = lax.dot_general(
        normed, wkv_head, (((1,), (1,)), ((), ())), preferred_element_type=jnp.float32
    )
    head_kv = (base_kv + lora[:, query_cols:]).astype(jnp.bfloat16)
    divided_key_value = head_kv.reshape(grand_total, 2, head_length)
    keys = rotate(normalize(divided_key_value[:, :1].astype(jnp.float32), k_gain), rope_pos).astype(
        jnp.bfloat16
    )[:, 0]
    values = divided_key_value[:, 1]
    entries = jnp.concatenate([keys, values], axis=1)
    mine = lax.dynamic_slice_in_dim(
        entries, place * local_cols - head * head_width, local_cols, 1
    )
    pages_held = page_table.shape[1]
    kv_pages = jnp.zeros((pages_held * PAGE, local_cols), jnp.bfloat16).at[cell].set(mine)
    kv_pages = kv_pages.reshape(pages_held, PAGE, local_cols).transpose(0, 2, 1)
    query_rows_out = (
        jnp.dot(normed, query_weight, preferred_element_type=jnp.float32) + lora[:, :query_cols]
    )
    query_rows_out = rotate(
        normalize(query_rows_out.reshape(grand_total, heads_here, head_length), q_gain), rope_pos
    ).astype(jnp.bfloat16)
    mixed = attend(query_rows_out, keys, values, group, head_length ** (-0.5))
    shrink_table = shrink_o.reshape(adapters * rank, query_cols)
    upward_wide_rows = expand_o.reshape(adapters * rank, width).astype(jnp.float32)
    lower_rank_rows = lax.dot_general(
        mixed, shrink_table, (((1,), (1,)), ((), ())), preferred_element_type=jnp.float32
    )
    retained_mask = jnp.repeat(
        adapter_position[:, None] == jnp.arange(adapters, dtype=jnp.int32)[None, :], rank, axis=1
    )
    adapter_contribution = jnp.dot(mixed, w_o, preferred_element_type=jnp.float32)
    attn_terms = (
        adapter_contribution
        + ADAPTER_FACTOR
        * jnp.dot(
            jnp.where(retained_mask, lower_rank_rows, 0.0),
            upward_wide_rows,
            precision=lax.Precision.HIGHEST,
        )
    ).astype(jnp.bfloat16)
    attn_out, moe_in = middle(attn_terms.reshape(parts, own_rows, width), tokens, moe_gain)
    experts_here = w_gate.shape[0]
    own_experts = place * experts_here + jnp.arange(experts_here, dtype=jnp.int32)
    choose = expert_ids[:, :, None] == own_experts[None, None, :]
    share = expert_gates / jnp.sum(expert_gates, axis=1, keepdims=True)
    weight = jnp.sum(jnp.where(choose, share[:, :, None], 0.0), axis=1)
    hit = jnp.any(choose, axis=1).reshape(parts, own_rows, experts_here)
    weight = weight.reshape(parts, own_rows, experts_here)
    below = jnp.tril(jnp.ones((own_rows, own_rows), jnp.bfloat16))
    rank_in_block = jnp.einsum(
        "ut,ste->sue", below, hit.astype(jnp.bfloat16), preferred_element_type=jnp.float32
    )
    numbers = jnp.arange(1, CAP_DEV + 1, dtype=jnp.float32)
    picked = hit[..., None] & (rank_in_block[..., None] == numbers)
    pick = picked.astype(jnp.bfloat16)
    slot_weight = jnp.sum(jnp.where(picked, weight[..., None], 0.0), axis=1)
    rows = jnp.einsum(
        "stek,std->eskd",
        pick,
        moe_in,
        preferred_element_type=jnp.float32,
    ).astype(jnp.bfloat16)
    rows = rows.reshape(1, experts_here, parts * CAP_DEV, width)
    outputs = expert_apply(rows, w_gate, w_up, w_down)[0]
    slot_weight = slot_weight.transpose(1, 0, 2).reshape(experts_here, parts * CAP_DEV, 1)
    weighted = (outputs.astype(jnp.float32) * slot_weight).astype(jnp.bfloat16)
    moe_terms = jnp.einsum(
        "stek,eskd->std",
        pick,
        weighted.reshape(experts_here, parts, CAP_DEV, width),
        preferred_element_type=jnp.float32,
    )
    moe_total = leave(moe_terms.astype(jnp.bfloat16))
    return (attn_out, moe_total, kv_pages)


def solution(mesh):
    placed = (
        P(("dp", "tensor"), None),
        P(),
        P(),
        P(),
        P(),
        P(None, "tensor"),
        P("tensor", None, None),
        P("tensor", None),
        P("tensor", None, None),
        P("tensor", None, None),
        P("tensor", None, None),
        P("dp", None, None),
        P(None, None, "tensor"),
        P(None, None, "tensor"),
        P(),
        P(),
        P("dp", None),
        P("dp", None),
        P("dp", None),
        P(),
        P("dp", None),
        P("dp", None),
        P("dp", None),
    )
    return jax.shard_map(
        local,
        mesh=mesh,
        in_specs=placed,
        out_specs=(P(("dp", "tensor"), None), P(("dp", "tensor"), None), P("dp", "tensor", None)),
        check_vma=False,
    )
```

```python
import functools
import math
import jax, jax.numpy as jnp
from jax import lax
from jax.experimental import pallas as pl
from jax.experimental.pallas import tpu as pltpu
from jax.sharding import PartitionSpec as P

SIDE = 4
HALF = 32

def spot(z, y, core):
    return lax.rem(z, SIDE) * 8 + lax.rem(y, SIDE) * 2 + core

def whereabouts():
    me = lax.axis_index("tensor")
    return me, lax.div(me, 8), lax.rem(lax.div(me, 2), SIDE), lax.rem(me, 2)

def greet(partners):
    barrier = pltpu.get_barrier_semaphore()
    for partner in partners:
        pl.semaphore_signal(barrier, inc=1, device_id={"tensor": partner}, device_id_type=pl.DeviceIdType.MESH)
    pl.semaphore_wait(barrier, len(partners))

class Copies:
    def __init__(self, send, recv):
        self.send, self.recv, self.n, self.all = send, recv, 0, []
    def make(self, src, dst, axis, target):
        k = self.n
        self.n += 1
        copy = pltpu.make_async_remote_copy(src_ref=src, dst_ref=dst, send_sem=self.send.at[k], recv_sem=self.recv.at[k],
            device_id={axis: target}, device_id_type=pl.DeviceIdType.MESH)
        self.all.append(copy)
        return copy
    def go(self, src, dst, axis, target):
        copy = self.make(src, dst, axis, target)
        copy.start()
        return copy
    def finish(self):
        for copy in self.all:
            copy.wait_send()

def gather_rows(out, z, y, core, copies, hooks=()):
    hooks = list(hooks)
    def hook():
        if hooks:
            hooks.pop(0)()
    side = spot(z, y, 1 - core)
    shared = []
    def share(block, row, rows):
        piece = out.at[block, pl.ds(row, rows)]
        shared.append(copies.go(piece, piece, "tensor", side))
    def send(block, row, rows, target):
        piece = out.at[block, pl.ds(row, rows)]
        return copies.go(piece, piece, "tensor", target)
    class Part: pass
    parts = []
    for number in range(2):
        p = Part()
        p.row = number * HALF
        if number == 0:
            p.at = lambda u, v: spot(z + v, y + u, core)
        else:
            p.at = lambda u, v: spot(z + u, y + v, core)
        parts.append(p)
    def ring_open(p, along_u, u):
        block = p.at(u, 0)
        up, down = (p.at(1, 0), p.at(3, 0)) if along_u else (p.at(0, 1), p.at(0, 3))
        return [send(block, p.row, HALF, up), send(block, p.row, HALF, down)]
    def ring_pass(p, along_u, u, opened, which):
        opened[which].wait_recv()
        off = 3 if which == 0 else 1
        block = p.at(off, 0) if along_u else p.at(u, off)
        target = (p.at(1, 0), p.at(3, 0))[which] if along_u else (p.at(0, 1), p.at(0, 3))[which]
        fwd = send(block, p.row + which * (HALF // 2), HALF // 2, target)
        share(block, p.row, HALF)
        return fwd
    me = spot(z, y, core)
    for p in parts:
        p.u = ring_open(p, True, 0)
    for p in parts:
        p.v = {0: ring_open(p, False, 0)}
    share(me, 0, 2 * HALF)
    hook()
    for which in range(2):
        for p in parts:
            p.u.append(ring_pass(p, True, 0, p.u, which))
            off = 3 if which == 0 else 1
            p.v[off] = ring_open(p, False, off)
    for which in range(2):
        for p in parts:
            p.v[0].append(ring_pass(p, False, 0, p.v[0], which))
    hook()
    for p in parts:
        p.u[2].wait_recv()
        p.u[3].wait_recv()
        share(p.at(2, 0), p.row, HALF)
        p.v[2] = ring_open(p, False, 2)
    for off in (3, 1):
        for which in range(2):
            for p in parts:
                p.v[off].append(ring_pass(p, False, off, p.v[off], which))
        for p in parts:
            done = 0 if off == 3 else 3
            p.v[done][2].wait_recv()
            p.v[done][3].wait_recv()
            share(p.at(done, 2), p.row, HALF)
        hook()
    for which in range(2):
        for p in parts:
            p.v[2].append(ring_pass(p, False, 2, p.v[2], which))
    for off in (1, 2):
        for p in parts:
            p.v[off][2].wait_recv()
            p.v[off][3].wait_recv()
            share(p.at(off, 2), p.row, HALF)
    for copy in shared:
        copy.wait_recv()

def add_rows(dst, start, rows, sources):
    for first in range(0, rows, 16):
        total = dst[pl.ds(start + first, 16)].astype(jnp.float32)
        for ref, row in sources:
            total = total + ref[pl.ds(row + first, 16)].astype(jnp.float32)
        dst[pl.ds(start + first, 16)] = total.astype(dst.dtype)

ORDER = (2, 1, 3, 0)
SCATTER_COPIES = 32 + 32 + 8

def scatter_rows(terms, acc, sib, landed, local, z, y, core, copies, result):
    side = spot(z, y, 1 - core)
    loads, shared = {}, {}
    def cell(number, v, u):
        return (v, u) if number == 0 else (u, v)
    for v in ORDER:
        for u in ORDER:
            for number in range(2):
                i, j = cell(number, v, u)
                rows = pl.ds(number * HALF, HALF)
                shared[number, v, u] = copies.go(
                    terms.at[spot(z + i, y + j, 1 - core), rows], sib.at[i, j, rows], "tensor", side)
                load = pltpu.make_async_copy(
                    terms.at[spot(z + i, y + j, core), rows], acc.at[i, j, rows], local.at[number * 16 + v * 4 + u])
                load.start()
                loads[number, v, u] = load
    def neighbour(number, along_v, step):
        along_z = (number == 0) == along_v
        return spot(z + step, y, core) if along_z else spot(z, y + step, core)
    def own(number, v, u):
        return acc.at[cell(number, v, u)]
    def pair(number, v, u):
        loads[number, v, u].wait()
        shared[number, v, u].wait_recv()
        return (sib.at[cell(number, v, u)], number * HALF)
    def buf(number, u):
        return landed.at[number * 5 + u]
    ring = {}
    def far(number, along_v, u, block):
        row = number * HALF
        b = buf(number, u)
        key = (number, u)
        ring[key] = [
            copies.go(block.at[pl.ds(row, 16)], b.at[pl.ds(0, 16)], "tensor", neighbour(number, along_v, 1)),
            copies.go(block.at[pl.ds(row + 16, 16)], b.at[pl.ds(16, 16)], "tensor", neighbour(number, along_v, 3)),
        ]
    def near(number, along_v, u, block, which):
        row = number * HALF
        b = buf(number, u)
        ring[number, u].append(
            copies.go(block.at[pl.ds(row, HALF)], b.at[pl.ds(32 + 32 * which, HALF)], "tensor",
                      neighbour(number, along_v, (1, 3)[which])))
    for u in ORDER:
        for number in range(2):
            block = own(number, 2, u)
            add_rows(block, number * HALF, HALF, [pair(number, 2, u)])
            far(number, True, u, block)
    for u in ORDER:
        for number in range(2):
            row = number * HALF
            for which in range(2):
                v = (1, 3)[which]
                block = own(number, v, u)
                other, first = pair(number, v, u)
                ring[number, u][which].wait_recv()
                for part in range(2):
                    sources = [(other, first + 16 * part)]
                    if part == which:
                        sources.append((buf(number, u), 16 * which))
                    add_rows(block, row + 16 * part, 16, sources)
                near(number, True, u, block, which)
    for u in ORDER:
        for number in range(2):
            row = number * HALF
            block = own(number, 0, u)
            source = pair(number, 0, u)
            b = buf(number, u)
            ring[number, u][2].wait_recv()
            ring[number, u][3].wait_recv()
            sources = [source, (b, 32), (b, 64)]
            last = buf(number, 4)
            if u == 2:
                add_rows(block, row, HALF, sources)
                far(number, False, 4, block)
            elif u in (1, 3):
                which = (1, 3).index(u)
                ring[number, 4][which].wait_recv()
                for part in range(2):
                    more = [(ref, r + 16 * part) for ref, r in sources]
                    if part == which:
                        more.append((last, 16 * which))
                    add_rows(block, row + 16 * part, 16, more)
                near(number, False, 4, block, which)
            else:
                ring[number, 4][2].wait_recv()
                ring[number, 4][3].wait_recv()
                for first in range(0, HALF, 16):
                    total = block[pl.ds(row + first, 16)].astype(jnp.float32)
                    for ref, r in sources + [(last, 32), (last, 64)]:
                        total = total + ref[pl.ds(r + first, 16)].astype(jnp.float32)
                    result[pl.ds(row + first, 16)] = total

def scatter_scratch(width):
    return [
        pltpu.VMEM((4, 4, 64, width), jnp.bfloat16),
        pltpu.VMEM((4, 4, 64, width), jnp.bfloat16),
        pltpu.VMEM((10, 96, width), jnp.bfloat16),
        pltpu.SemaphoreType.DMA((32,)),
    ]

def partners(z, y, core):
    return [spot(z, y, 1 - core), spot(z + 1, y, core), spot(z + 3, y, core), spot(z, y + 1, core), spot(z, y + 3, core)]


GATHER_COPIES = 2 * 20 + 31
EXTRA_COPIES = 7 + 11
NORM_EPS = 1e-06
ROPE_BASE = 1000000.0
ADAPTER_FACTOR = 0.5
PAGE = 128
CAP_DEV = 16


def normalize(values, gain):
    return (
        values
        * lax.rsqrt(jnp.mean(values * values, axis=-1, keepdims=True) + NORM_EPS)
        * gain.astype(jnp.float32)
    )


def enter_kernel(
    tokens_ref, gain_ref, shrink_ref, wkv_ref, rows_ref, factors_ref, wkv_all_ref, local, send, recv
):
    me, z, y, core = whereabouts()
    group = lax.axis_index("dp")
    up, down = lax.rem(group + 1, SIDE), lax.rem(group + 3, SIDE)
    across = lax.rem(group + 2, SIDE)
    copies = Copies(send, recv)
    homes = [
        pltpu.make_async_copy(shrink_ref, factors_ref.at[pl.ds(4 * group, 4)], local.at[0]),
        pltpu.make_async_copy(wkv_ref.at[z], wkv_all_ref.at[z, y, core], local.at[1]),
    ]
    for home in homes:
        home.start()
    rows_ref[me] = normalize(tokens_ref[...].astype(jnp.float32), gain_ref[...]).astype(
        rows_ref.dtype
    )
    barrier = pltpu.get_barrier_semaphore()
    near = partners(z, y, core) + [spot(z + 2, y, core)]
    for partner in near:
        pl.semaphore_signal(
            barrier, inc=1, device_id={"tensor": partner}, device_id_type=pl.DeviceIdType.MESH
        )
    for partner in (up, down):
        pl.semaphore_signal(
            barrier, inc=1, device_id={"dp": partner}, device_id_type=pl.DeviceIdType.MESH
        )
    pl.semaphore_wait(barrier, len(near) + 2)
    side = spot(z, y, 1 - core)
    state = {}

    def open_extras():
        spread = []
        for step in (1, 3, 2):
            there = lax.rem(z + step, SIDE)
            spread.append(
                copies.go(
                    wkv_ref.at[there], wkv_all_ref.at[z, y, core], "tensor", spot(there, y, core)
                )
            )
        state["spread"] = spread
        half = factors_ref.at[pl.ds(4 * group + 2 * core, 2)]
        mine = shrink_ref.at[pl.ds(2 * core, 2)]
        state["factors"] = [copies.go(mine, half, "dp", up), copies.go(mine, half, "dp", down)]

    def kv(y_at, first=0, count=4):
        return wkv_all_ref.at[pl.ds(first, count), lax.rem(y_at, SIDE), core]

    def middle_extras():
        for copy in state["spread"]:
            copy.wait_recv()
        homes[1].wait()
        block = kv(y)
        state["kv"] = [
            copies.go(block, block, "tensor", spot(z, y + 1, core)),
            copies.go(block, block, "tensor", spot(z, y + 3, core)),
        ]
        state["shared"] = [copies.go(block, block, "tensor", side)]
        for which, (origin, target) in enumerate(((down, up), (up, down))):
            state["factors"][which].wait_recv()
            one = factors_ref.at[4 * origin + 2 * core + which]
            state["factors"].append(copies.go(one, one, "dp", target))
            both = factors_ref.at[pl.ds(4 * origin + 2 * core, 2)]
            state["shared"].append(copies.go(both, both, "tensor", side))

    def pass_extras():
        for which, (origin, target) in enumerate(((y + 3, y + 1), (y + 1, y + 3))):
            state["kv"][which].wait_recv()
            piece = kv(origin, 2 * which, 2)
            state["kv"].append(copies.go(piece, piece, "tensor", spot(z, target, core)))
            whole = kv(origin)
            state["shared"].append(copies.go(whole, whole, "tensor", side))
        state["factors"][2].wait_recv()
        state["factors"][3].wait_recv()
        both = factors_ref.at[pl.ds(4 * across + 2 * core, 2)]
        state["shared"].append(copies.go(both, both, "tensor", side))

    def close_extras():
        state["kv"][2].wait_recv()
        state["kv"][3].wait_recv()
        whole = kv(y + 2)
        state["shared"].append(copies.go(whole, whole, "tensor", side))

    open_extras()
    gather_rows(rows_ref, z, y, core, copies, [middle_extras, pass_extras, close_extras])
    for copy in state["shared"]:
        copy.wait_recv()
    homes[0].wait()
    copies.finish()
    assert copies.n == GATHER_COPIES + EXTRA_COPIES, copies.n


def enter(tokens, gain, shrink, wkv):
    rows, width = tokens.shape
    count = GATHER_COPIES + EXTRA_COPIES
    return pl.pallas_call(
        enter_kernel,
        out_shape=(
            jax.ShapeDtypeStruct((32, rows, width), jnp.bfloat16),
            jax.ShapeDtypeStruct((4 * shrink.shape[0],) + shrink.shape[1:], jnp.bfloat16),
            jax.ShapeDtypeStruct((4, 4, 2) + wkv.shape[1:], jnp.bfloat16),
        ),
        in_specs=[
            pl.BlockSpec(memory_space=pltpu.VMEM),
            pl.BlockSpec(memory_space=pltpu.VMEM),
            pl.BlockSpec(memory_space=pl.ANY),
            pl.BlockSpec(memory_space=pl.ANY),
        ],
        out_specs=(
            pl.BlockSpec(memory_space=pltpu.VMEM),
            pl.BlockSpec(memory_space=pl.ANY),
            pl.BlockSpec(memory_space=pl.ANY),
        ),
        scratch_shapes=[
            pltpu.SemaphoreType.DMA((2,)),
            pltpu.SemaphoreType.DMA((count,)),
            pltpu.SemaphoreType.DMA((count,)),
        ],
        compiler_params=pltpu.CompilerParams(
            collective_id=0, has_side_effects=True, vmem_limit_bytes=32 << 20
        ),
    )(tokens, gain.reshape(1, width), shrink, wkv)


def middle_kernel(
    terms_ref, tokens_ref, gain_ref, out_ref, rows_ref, acc, sib, landed, local, total, send, recv
):
    me, z, y, core = whereabouts()
    greet(partners(z, y, core))
    copies = Copies(send, recv)
    scatter_rows(terms_ref, acc, sib, landed, local, z, y, core, copies, total)
    summed = total[...]
    out_ref[...] = summed.astype(out_ref.dtype)
    rows_ref[me] = normalize(tokens_ref[...].astype(jnp.float32) + summed, gain_ref[...]).astype(
        rows_ref.dtype
    )
    gather_rows(rows_ref, z, y, core, copies)
    copies.finish()
    assert copies.n == SCATTER_COPIES + GATHER_COPIES, copies.n


def middle(terms, tokens, gain):
    rows, width = tokens.shape
    count = SCATTER_COPIES + GATHER_COPIES
    vmem = pl.BlockSpec(memory_space=pltpu.VMEM)
    return pl.pallas_call(
        middle_kernel,
        out_shape=(
            jax.ShapeDtypeStruct((rows, width), jnp.bfloat16),
            jax.ShapeDtypeStruct((32, rows, width), jnp.bfloat16),
        ),
        in_specs=[pl.BlockSpec(memory_space=pl.ANY), vmem, vmem],
        out_specs=(vmem, vmem),
        scratch_shapes=scatter_scratch(width)
        + [
            pltpu.VMEM((rows, width), jnp.float32),
            pltpu.SemaphoreType.DMA((count,)),
            pltpu.SemaphoreType.DMA((count,)),
        ],
        compiler_params=pltpu.CompilerParams(
            collective_id=1, has_side_effects=True, vmem_limit_bytes=40 << 20
        ),
    )(terms, tokens, gain.reshape(1, width))


def leave_kernel(terms_ref, out_ref, acc, sib, landed, local, total, send, recv):
    me, z, y, core = whereabouts()
    greet(partners(z, y, core))
    copies = Copies(send, recv)
    scatter_rows(terms_ref, acc, sib, landed, local, z, y, core, copies, total)
    out_ref[...] = total[...].astype(out_ref.dtype)
    copies.finish()
    assert copies.n == SCATTER_COPIES, copies.n


def leave(terms):
    rows, width = terms.shape[1:]
    return pl.pallas_call(
        leave_kernel,
        out_shape=jax.ShapeDtypeStruct((rows, width), jnp.bfloat16),
        in_specs=[pl.BlockSpec(memory_space=pl.ANY)],
        out_specs=pl.BlockSpec(memory_space=pltpu.VMEM),
        scratch_shapes=scatter_scratch(width)
        + [
            pltpu.VMEM((rows, width), jnp.float32),
            pltpu.SemaphoreType.DMA((SCATTER_COPIES,)),
            pltpu.SemaphoreType.DMA((SCATTER_COPIES,)),
        ],
        compiler_params=pltpu.CompilerParams(
            collective_id=2, has_side_effects=True, vmem_limit_bytes=32 << 20
        ),
    )(terms)


BLOCK = 512
KEY_BLOCK = 256
TRANSPOSED = (((1,), (1,)), ((), ()))


def heart_kernel(
    lens_s,
    groups_s,
    pages_s,
    lens_ref,
    groups_ref,
    adapters_ref,
    slots_ref,
    q_gain_ref,
    k_gain_ref,
    x_ref,
    factors_ref,
    wkv_ref,
    wq_ref,
    q_up_ref,
    kv_up_ref,
    wo_ref,
    shrink_o_ref,
    expand_ref,
    out_ref,
    pages_ref,
    tab,
    keys,
    values,
    across,
    acc,
):
    step = pl.program_id(0)
    place = lax.axis_index("tensor")
    head = lax.div(place, 8)
    f32, bf16 = jnp.float32, jnp.bfloat16
    requests = lens_ref.shape[1]
    adapters = slots_ref.shape[1]
    depth = wq_ref.shape[1]

    @pl.when(step == 0)
    def _():
        down = lax.broadcasted_iota(jnp.int32, (requests, requests), 0)
        over = lax.broadcasted_iota(jnp.int32, (requests, requests), 1)

        def column(row, number):
            a = lax.broadcasted_iota(jnp.int32, (number, number), 0)
            b = lax.broadcasted_iota(jnp.int32, (number, number), 1)
            return jnp.sum(
                jnp.where(a == b, jnp.broadcast_to(row, (number, number)), 0.0),
                axis=1,
                keepdims=True,
            )

        lens = lens_ref[...].astype(f32)
        groups = groups_ref[...].astype(f32)
        chosen = adapters_ref[...]
        slots = column(slots_ref[...].astype(f32), adapters)
        ends = jnp.sum(jnp.where(down <= over, column(lens, requests), 0.0), axis=0, keepdims=True)
        starts = ends - lens
        same = column(groups, requests) == groups
        firsts = jnp.min(
            jnp.where(same, column(starts, requests), 1e9), axis=0, keepdims=True
        )
        which = lax.broadcasted_iota(jnp.int32, (adapters, requests), 0)
        slot = jnp.sum(jnp.where(which == chosen, slots, 0.0), axis=0, keepdims=True)
        tab[0:1, :] = starts
        tab[1:2, :] = ends
        tab[2:3, :] = firsts
        tab[3:4, :] = slot

    first_row = step * BLOCK
    row = first_row + lax.broadcasted_iota(jnp.int32, (BLOCK, 1), 0)
    row_f = row.astype(f32)
    inside = (row_f >= tab[0:1, :]) & (row_f < tab[1:2, :])
    rope = row_f - jnp.sum(jnp.where(inside, tab[2:3, :], 0.0), axis=1, keepdims=True)
    slot = jnp.sum(jnp.where(inside, tab[3:4, :], 0.0), axis=1, keepdims=True).astype(jnp.int32)

    lane = lax.broadcasted_iota(jnp.int32, (1, depth), 1)
    half = depth // 2
    low = lane < half
    freq = jnp.exp(
        -jnp.where(low, lane, lane - half).astype(f32) * (2.0 * math.log(ROPE_BASE) / depth)
    )
    mixed_trig = jnp.sin(rope * freq + jnp.where(low, 0.5 * math.pi, 0.0))
    other_trig = pltpu.roll(mixed_trig, half, 1)
    cosine = jnp.where(low, mixed_trig, other_trig)
    sine = jnp.where(low, -other_trig, mixed_trig)

    def turn(vector):
        return vector * cosine + pltpu.roll(vector, half, 1) * sine

    def unit(vector, gain_ref):
        return (
            vector
            * lax.rsqrt(jnp.mean(vector * vector, axis=-1, keepdims=True) + NORM_EPS)
            * gain_ref[...].astype(f32)
        )

    rank = factors_ref.shape[1] // 3
    mine = slot == lax.div(lax.broadcasted_iota(jnp.int32, (1, adapters * rank), 1), rank)
    x = x_ref[...]
    lora = []
    for part in range(3):
        table = factors_ref[:, part * rank : (part + 1) * rank, :].reshape(adapters * rank, -1)
        shrunk = lax.dot_general(x, table, TRANSPOSED, preferred_element_type=f32)
        placed = jnp.where(mine, shrunk, 0.0).astype(bf16)
        if part == 0:
            up = q_up_ref[...]
        else:
            begin = pl.multiple_of(head * 2 * depth + (part - 1) * depth, depth)
            up = kv_up_ref[:, pl.ds(begin, depth)]
        lora.append(ADAPTER_FACTOR * jnp.dot(placed, up, preferred_element_type=f32))
    query = jnp.dot(x, wq_ref[...], preferred_element_type=f32) + lora[0]
    query = turn(unit(query, q_gain_ref)).astype(bf16)
    kv = lax.dot_general(x, wkv_ref[...], TRANSPOSED, preferred_element_type=f32)
    raw = (kv[:, :depth] + lora[1]).astype(bf16).astype(f32)
    key = turn(unit(raw, k_gain_ref)).astype(bf16)
    value = (kv[:, depth:] + lora[2]).astype(bf16)
    keys[pl.ds(first_row, BLOCK), :] = key
    values[pl.ds(first_row, BLOCK), 0:depth] = value
    values[pl.ds(first_row, BLOCK), depth:] = jnp.broadcast_to(
        jnp.where(lane == 0, 1.0, 0.0), (BLOCK, depth)
    ).astype(bf16)

    columns = pages_ref.shape[1]
    offset = lax.rem(place, 8) * columns
    pick_row = lax.broadcasted_iota(jnp.int32, (columns, 2 * depth), 0) + offset
    pick_lane = lax.broadcasted_iota(jnp.int32, (columns, 2 * depth), 1)
    pick = jnp.where(pick_row == pick_lane, 1.0, 0.0).astype(bf16)
    across[:, pl.ds(pl.multiple_of(first_row, BLOCK), BLOCK)] = lax.dot_general(
        pick, jnp.concatenate([key, value], axis=1), TRANSPOSED, preferred_element_type=f32
    )

    def look(number, carry):
        start, lead, found, before = carry
        group = groups_s[0, number]
        lead = jnp.where(group == before, lead, start)
        found = jnp.where(start <= first_row, lead, found)
        return start + lens_s[0, number], lead, found, group

    zero = jnp.int32(0)
    found = lax.fori_loop(0, requests, look, (zero, zero, zero, jnp.int32(-1)))[2]
    acc[...] = jnp.zeros_like(acc)
    gap = lax.broadcasted_iota(jnp.int32, (BLOCK, KEY_BLOCK), 0) - lax.broadcasted_iota(
        jnp.int32, (BLOCK, KEY_BLOCK), 1
    )
    reach = rope.astype(jnp.int32)
    scale = depth**-0.5

    def over_keys(number, carry):
        begin = pl.multiple_of(number * KEY_BLOCK, KEY_BLOCK)
        scores = lax.dot_general(
            query, keys[pl.ds(begin, KEY_BLOCK), :], TRANSPOSED, preferred_element_type=f32
        )
        behind = gap + (first_row - begin)
        raised = jnp.where((behind >= 0) & (behind <= reach), jnp.exp(scores * scale), 0.0)
        acc[...] += jnp.dot(
            raised.astype(bf16), values[pl.ds(begin, KEY_BLOCK), :], preferred_element_type=f32
        )
        return carry

    lax.fori_loop(
        lax.div(found, KEY_BLOCK), (step + 1) * (BLOCK // KEY_BLOCK), over_keys, jnp.int32(0)
    )
    mixed = (acc[:, :depth] / acc[:, depth : depth + 1]).astype(bf16)
    shrunk = lax.dot_general(mixed, shrink_o_ref[...], TRANSPOSED, preferred_element_type=f32)
    placed = jnp.where(mine, ADAPTER_FACTOR * shrunk, 0.0).astype(bf16)
    width = out_ref.shape[-1]
    for begin in range(0, width, 512):
        term = jnp.dot(mixed, wo_ref[:, begin : begin + 512], preferred_element_type=f32)
        term = term + jnp.dot(
            placed, expand_ref[:, begin : begin + 512], preferred_element_type=f32
        )
        out_ref[:, begin : begin + 512] = term.astype(bf16)

    @pl.when(step == pl.num_programs(0) - 1)
    def _():
        spot_lane = lax.broadcasted_iota(jnp.int32, (columns, PAGE), 1)

        def fill(number, start):
            length = lens_s[0, number]
            for part in range(2):
                begin = start + part * PAGE
                aligned = pl.multiple_of(lax.div(begin, PAGE) * PAGE, PAGE)
                window = across[:, pl.ds(aligned, 2 * PAGE)]
                shift = lax.rem(2 * PAGE - (begin - aligned), 2 * PAGE)
                rolled = pltpu.roll(window, shift, 1)[:, :PAGE]
                kept = jnp.where(spot_lane < length - part * PAGE, rolled, 0.0)
                pages_ref[pages_s[0, number * 2 + part]] = kept.astype(bf16)
            return start + length

        lax.fori_loop(0, requests, fill, zero)


def heart(
    lengths,
    groups,
    adapter_of_request,
    adapter_slot,
    page_table,
    q_gain,
    k_gain,
    x,
    factors,
    wkv,
    query_weight,
    query_up,
    kv_up,
    w_o,
    shrink_o,
    expand_o,
):
    total, width = x.shape
    depth = query_weight.shape[1]
    requests = lengths.shape[1]
    pages = page_table.shape[1]
    columns = 2 * kv_up.shape[1] // 64
    slots = adapter_slot.shape[0]
    smem = pl.BlockSpec(memory_space=pltpu.SMEM)

    def whole(array):
        return pl.BlockSpec(
            array.shape, lambda i: (0,) * array.ndim, pipeline_mode=pl.Buffered(1)
        )

    small = (
        lengths,
        groups,
        adapter_of_request,
        adapter_slot.reshape(1, slots),
        q_gain.reshape(1, depth),
        k_gain.reshape(1, depth),
    )
    tables = (factors, wkv, query_weight, query_up, kv_up, w_o, shrink_o, expand_o)
    return pl.pallas_call(
        heart_kernel,
        grid=(total // BLOCK,),
        out_shape=(
            jax.ShapeDtypeStruct((total, width), jnp.bfloat16),
            jax.ShapeDtypeStruct((pages, columns, PAGE), jnp.bfloat16),
        ),
        in_specs=[smem, smem, smem]
        + [whole(array) for array in small]
        + [pl.BlockSpec((BLOCK, width), lambda i: (i, 0))]
        + [whole(array) for array in tables],
        out_specs=(
            pl.BlockSpec((BLOCK, width), lambda i: (i, 0)),
            pl.BlockSpec((pages, columns, PAGE), lambda i: (0, 0, 0)),
        ),
        scratch_shapes=[
            pltpu.VMEM((8, requests), jnp.float32),
            pltpu.VMEM((total, depth), jnp.bfloat16),
            pltpu.VMEM((total, 2 * depth), jnp.bfloat16),
            pltpu.VMEM((columns, total + 4 * PAGE), jnp.float32),
            pltpu.VMEM((BLOCK, 2 * depth), jnp.float32),
        ],
        compiler_params=pltpu.CompilerParams(vmem_limit_bytes=48 << 20),
    )(lengths, groups, page_table, *small, x, *tables)


def expert_apply(rows, gate_rows, up_rows, down_rows):
    gate_value = jnp.einsum("secx,efx->secf", rows, gate_rows, preferred_element_type=jnp.float32)
    up_value = jnp.einsum("secx,efx->secf", rows, up_rows, preferred_element_type=jnp.float32)
    hidden = (jax.nn.silu(gate_value) * up_value).astype(jnp.bfloat16)
    out = jnp.einsum("secf,efx->secx", hidden, down_rows, preferred_element_type=jnp.float32)
    return lax.optimization_barrier(out.astype(jnp.bfloat16))


def local(
    tokens,
    attn_gain,
    moe_gain,
    q_gain,
    k_gain,
    query_weight,
    w_kv,
    w_o,
    w_gate,
    w_up,
    w_down,
    shrink_qkv,
    shrink_o,
    query_up_factors,
    key_value_up_factors,
    expand_o,
    lengths,
    groups,
    adapter_of_request,
    adapter_slot,
    page_table,
    expert_ids,
    expert_gates,
):
    parts = lax.axis_size("tensor")
    place = lax.axis_index("tensor")
    own_rows, width = tokens.shape
    grand_total = own_rows * parts
    adapters, rank, kv_width = key_value_up_factors.shape
    x_rows, factors, wkv_all = enter(tokens, attn_gain, shrink_qkv, w_kv.transpose(1, 0, 2))
    head_width = 2 * q_gain.shape[0]
    attn_terms, kv_pages = heart(
        lengths,
        groups,
        adapter_of_request,
        adapter_slot,
        page_table,
        q_gain,
        k_gain,
        x_rows.reshape(grand_total, width),
        factors,
        wkv_all.reshape(head_width, width),
        query_weight,
        query_up_factors.reshape(adapters * rank, -1),
        key_value_up_factors.reshape(adapters * rank, kv_width),
        w_o,
        shrink_o.reshape(adapters * rank, -1),
        expand_o.reshape(adapters * rank, width),
    )
    attn_out, moe_in = middle(attn_terms.reshape(parts, own_rows, width), tokens, moe_gain)
    experts_here = w_gate.shape[0]
    own_experts = place * experts_here + jnp.arange(experts_here, dtype=jnp.int32)
    choose = expert_ids[:, :, None] == own_experts[None, None, :]
    share = expert_gates / jnp.sum(expert_gates, axis=1, keepdims=True)
    weight = jnp.sum(jnp.where(choose, share[:, :, None], 0.0), axis=1)
    hit = jnp.any(choose, axis=1).reshape(parts, own_rows, experts_here)
    weight = weight.reshape(parts, own_rows, experts_here)
    below = jnp.tril(jnp.ones((own_rows, own_rows), jnp.bfloat16))
    rank_in_block = jnp.einsum(
        "ut,ste->sue", below, hit.astype(jnp.bfloat16), preferred_element_type=jnp.float32
    )
    numbers = jnp.arange(1, CAP_DEV + 1, dtype=jnp.float32)
    picked = hit[..., None] & (rank_in_block[..., None] == numbers)
    pick = picked.astype(jnp.bfloat16)
    slot_weight = jnp.sum(jnp.where(picked, weight[..., None], 0.0), axis=1)
    rows = jnp.einsum(
        "stek,std->eskd",
        pick,
        moe_in,
        preferred_element_type=jnp.float32,
    ).astype(jnp.bfloat16)
    rows = rows.reshape(1, experts_here, parts * CAP_DEV, width)
    outputs = expert_apply(rows, w_gate, w_up, w_down)[0]
    slot_weight = slot_weight.transpose(1, 0, 2).reshape(experts_here, parts * CAP_DEV, 1)
    weighted = (outputs.astype(jnp.float32) * slot_weight).astype(jnp.bfloat16)
    moe_terms = jnp.einsum(
        "stek,eskd->std",
        pick,
        weighted.reshape(experts_here, parts, CAP_DEV, width),
        preferred_element_type=jnp.float32,
    )
    moe_total = leave(moe_terms.astype(jnp.bfloat16))
    return (attn_out, moe_total, kv_pages)


def solution(mesh):
    placed = (
        P(("dp", "tensor"), None),
        P(),
        P(),
        P(),
        P(),
        P(None, "tensor"),
        P("tensor", None, None),
        P("tensor", None),
        P("tensor", None, None),
        P("tensor", None, None),
        P("tensor", None, None),
        P("dp", None, None),
        P(None, None, "tensor"),
        P(None, None, "tensor"),
        P(),
        P(),
        P("dp", None),
        P("dp", None),
        P("dp", None),
        P(),
        P("dp", None),
        P("dp", None),
        P("dp", None),
    )
    return jax.shard_map(
        local,
        mesh=mesh,
        in_specs=placed,
        out_specs=(P(("dp", "tensor"), None), P(("dp", "tensor"), None), P("dp", "tensor", None)),
        check_vma=False,
    )
```

```python
import functools
import math
import jax, jax.numpy as jnp
from jax import lax
from jax.experimental import pallas as pl
from jax.experimental.pallas import tpu as pltpu
from jax.sharding import PartitionSpec as P

SIDE = 4
HALF = 32

def spot(z, y, core):
    return lax.rem(z, SIDE) * 8 + lax.rem(y, SIDE) * 2 + core

def whereabouts():
    me = lax.axis_index("tensor")
    return me, lax.div(me, 8), lax.rem(lax.div(me, 2), SIDE), lax.rem(me, 2)

def greet(partners):
    barrier = pltpu.get_barrier_semaphore()
    for partner in partners:
        pl.semaphore_signal(barrier, inc=1, device_id={"tensor": partner}, device_id_type=pl.DeviceIdType.MESH)
    pl.semaphore_wait(barrier, len(partners))

class Copies:
    def __init__(self, send, recv):
        self.send, self.recv, self.n, self.all = send, recv, 0, []
    def make(self, src, dst, axis, target):
        k = self.n
        self.n += 1
        copy = pltpu.make_async_remote_copy(src_ref=src, dst_ref=dst, send_sem=self.send.at[k], recv_sem=self.recv.at[k],
            device_id={axis: target}, device_id_type=pl.DeviceIdType.MESH)
        self.all.append(copy)
        return copy
    def go(self, src, dst, axis, target):
        copy = self.make(src, dst, axis, target)
        copy.start()
        return copy
    def settle(self):
        for copy in self.all:
            copy.wait_send()
        self.all = []

def gather_rows(out, z, y, core, copies, hooks=()):
    hooks = list(hooks)
    def hook():
        if hooks:
            hooks.pop(0)()
    side = spot(z, y, 1 - core)
    shared = []
    def share(block, row, rows):
        piece = out.at[block, pl.ds(row, rows)]
        shared.append(copies.go(piece, piece, "tensor", side))
    def send(block, row, rows, target):
        piece = out.at[block, pl.ds(row, rows)]
        return copies.go(piece, piece, "tensor", target)
    class Part: pass
    parts = []
    for number in range(2):
        p = Part()
        p.row = number * HALF
        if number == 0:
            p.at = lambda u, v: spot(z + v, y + u, core)
        else:
            p.at = lambda u, v: spot(z + u, y + v, core)
        parts.append(p)
    def ring_open(p, along_u, u):
        block = p.at(u, 0)
        up, down = (p.at(1, 0), p.at(3, 0)) if along_u else (p.at(0, 1), p.at(0, 3))
        return [send(block, p.row, HALF, up), send(block, p.row, HALF, down)]
    def ring_pass(p, along_u, u, opened, which):
        opened[which].wait_recv()
        off = 3 if which == 0 else 1
        block = p.at(off, 0) if along_u else p.at(u, off)
        target = (p.at(1, 0), p.at(3, 0))[which] if along_u else (p.at(0, 1), p.at(0, 3))[which]
        fwd = send(block, p.row + which * (HALF // 2), HALF // 2, target)
        share(block, p.row, HALF)
        return fwd
    me = spot(z, y, core)
    for p in parts:
        p.u = ring_open(p, True, 0)
    for p in parts:
        p.v = {0: ring_open(p, False, 0)}
    share(me, 0, 2 * HALF)
    hook()
    for which in range(2):
        for p in parts:
            p.u.append(ring_pass(p, True, 0, p.u, which))
            off = 3 if which == 0 else 1
            p.v[off] = ring_open(p, False, off)
    for which in range(2):
        for p in parts:
            p.v[0].append(ring_pass(p, False, 0, p.v[0], which))
    hook()
    for p in parts:
        p.u[2].wait_recv()
        p.u[3].wait_recv()
        share(p.at(2, 0), p.row, HALF)
        p.v[2] = ring_open(p, False, 2)
    for off in (3, 1):
        for which in range(2):
            for p in parts:
                p.v[off].append(ring_pass(p, False, off, p.v[off], which))
        for p in parts:
            done = 0 if off == 3 else 3
            p.v[done][2].wait_recv()
            p.v[done][3].wait_recv()
            share(p.at(done, 2), p.row, HALF)
        hook()
    for which in range(2):
        for p in parts:
            p.v[2].append(ring_pass(p, False, 2, p.v[2], which))
    for off in (1, 2):
        for p in parts:
            p.v[off][2].wait_recv()
            p.v[off][3].wait_recv()
            share(p.at(off, 2), p.row, HALF)
    for copy in shared:
        copy.wait_recv()

def add_rows(dst, start, rows, sources):
    for first in range(0, rows, 16):
        total = dst[pl.ds(start + first, 16)].astype(jnp.float32)
        for ref, row in sources:
            total = total + ref[pl.ds(row + first, 16)].astype(jnp.float32)
        dst[pl.ds(start + first, 16)] = total.astype(dst.dtype)

ORDER = (2, 1, 3, 0)
FIRST_COPIES = 32 + 32 + 8
SECOND_COPIES = 16 + 32 + 8


def cell(number, v, u):
    return (v, u) if number == 0 else (u, v)


def scatter_rows(acc, sib, landed, z, y, core, copies, result, ensure, arrived):
    def neighbour(number, along_v, step):
        along_z = (number == 0) == along_v
        return spot(z + step, y, core) if along_z else spot(z, y + step, core)
    def own(number, v, u):
        return acc.at[cell(number, v, u)]
    def pair(number, v, u):
        arrived(number, v, u)
        return (sib.at[cell(number, v, u)], number * HALF)
    def buf(number, u):
        return landed.at[number * 5 + u]
    ring = {}
    def far(number, along_v, u, block):
        row = number * HALF
        b = buf(number, u)
        key = (number, u)
        ring[key] = [
            copies.go(block.at[pl.ds(row, 16)], b.at[pl.ds(0, 16)], "tensor", neighbour(number, along_v, 1)),
            copies.go(block.at[pl.ds(row + 16, 16)], b.at[pl.ds(16, 16)], "tensor", neighbour(number, along_v, 3)),
        ]
    def near(number, along_v, u, block, which):
        row = number * HALF
        b = buf(number, u)
        ring[number, u].append(
            copies.go(block.at[pl.ds(row, HALF)], b.at[pl.ds(32 + 32 * which, HALF)], "tensor",
                      neighbour(number, along_v, (1, 3)[which])))
    ensure([(2, u) for u in ORDER] + [(u, 2) for u in ORDER[1:]])
    for u in ORDER:
        for number in range(2):
            block = own(number, 2, u)
            add_rows(block, number * HALF, HALF, [pair(number, 2, u)])
            far(number, True, u, block)
    ensure([(i, j) for i in ORDER[1:] for j in ORDER[1:]])
    for u in ORDER:
        for number in range(2):
            row = number * HALF
            for which in range(2):
                v = (1, 3)[which]
                block = own(number, v, u)
                other, first = pair(number, v, u)
                ring[number, u][which].wait_recv()
                for part in range(2):
                    sources = [(other, first + 16 * part)]
                    if part == which:
                        sources.append((buf(number, u), 16 * which))
                    add_rows(block, row + 16 * part, 16, sources)
                near(number, True, u, block, which)
    for u in ORDER:
        for number in range(2):
            row = number * HALF
            block = own(number, 0, u)
            source = pair(number, 0, u)
            b = buf(number, u)
            ring[number, u][2].wait_recv()
            ring[number, u][3].wait_recv()
            sources = [source, (b, 32), (b, 64)]
            last = buf(number, 4)
            if u == 2:
                add_rows(block, row, HALF, sources)
                far(number, False, 4, block)
            elif u in (1, 3):
                which = (1, 3).index(u)
                ring[number, 4][which].wait_recv()
                for part in range(2):
                    more = [(ref, r + 16 * part) for ref, r in sources]
                    if part == which:
                        more.append((last, 16 * which))
                    add_rows(block, row + 16 * part, 16, more)
                near(number, False, 4, block, which)
            else:
                ring[number, 4][2].wait_recv()
                ring[number, 4][3].wait_recv()
                for first in range(0, HALF, 16):
                    total = block[pl.ds(row + first, 16)].astype(jnp.float32)
                    for ref, r in sources + [(last, 32), (last, 64)]:
                        total = total + ref[pl.ds(r + first, 16)].astype(jnp.float32)
                    result[pl.ds(row + first, 16)] = total

def terms_from(terms, acc, sib, local, z, y, core, copies):
    side = spot(z, y, 1 - core)
    loads, shared = {}, {}
    for v in ORDER:
        for u in ORDER:
            for number in range(2):
                i, j = cell(number, v, u)
                rows = pl.ds(number * HALF, HALF)
                shared[number, v, u] = copies.go(
                    terms.at[spot(z + i, y + j, 1 - core), rows], sib.at[i, j, rows], "tensor", side
                )
                load = pltpu.make_async_copy(
                    terms.at[spot(z + i, y + j, core), rows],
                    acc.at[i, j, rows],
                    local.at[number * 16 + v * 4 + u],
                )
                load.start()
                loads[number, v, u] = load

    def arrived(number, v, u):
        loads[number, v, u].wait()
        shared[number, v, u].wait_recv()

    return (lambda cells: None), arrived


def scatter_scratch(width):
    return [
        pltpu.VMEM((4, 4, 64, width), jnp.bfloat16),
        pltpu.VMEM((4, 4, 64, width), jnp.bfloat16),
        pltpu.VMEM((10, 96, width), jnp.bfloat16),
        pltpu.SemaphoreType.DMA((32,)),
    ]

def partners(z, y, core):
    return [spot(z, y, 1 - core), spot(z + 1, y, core), spot(z + 3, y, core), spot(z, y + 1, core), spot(z, y + 3, core)]


GATHER_COPIES = 2 * 20 + 31
EXTRA_COPIES = 7 + 11
NORM_EPS = 1e-06
ROPE_BASE = 1000000.0
ADAPTER_FACTOR = 0.5
PAGE = 128
CAP_DEV = 16
VMEM_LIMIT = 62 << 20


def normalize(values, gain):
    return (
        values
        * lax.rsqrt(jnp.mean(values * values, axis=-1, keepdims=True) + NORM_EPS)
        * gain.astype(jnp.float32)
    )


def enter_kernel(
    tokens_ref, gain_ref, shrink_ref, wkv_ref, rows_ref, factors_ref, wkv_all_ref, local, send, recv
):
    me, z, y, core = whereabouts()
    group = lax.axis_index("dp")
    up, down = lax.rem(group + 1, SIDE), lax.rem(group + 3, SIDE)
    across = lax.rem(group + 2, SIDE)
    copies = Copies(send, recv)
    homes = [
        pltpu.make_async_copy(shrink_ref, factors_ref.at[pl.ds(4 * group, 4)], local.at[0]),
        pltpu.make_async_copy(wkv_ref.at[z], wkv_all_ref.at[z, y, core], local.at[1]),
    ]
    for home in homes:
        home.start()
    rows_ref[me] = normalize(tokens_ref[...].astype(jnp.float32), gain_ref[...]).astype(
        rows_ref.dtype
    )
    barrier = pltpu.get_barrier_semaphore()
    near = partners(z, y, core) + [spot(z + 2, y, core)]
    for partner in near:
        pl.semaphore_signal(
            barrier, inc=1, device_id={"tensor": partner}, device_id_type=pl.DeviceIdType.MESH
        )
    for partner in (up, down):
        pl.semaphore_signal(
            barrier, inc=1, device_id={"dp": partner}, device_id_type=pl.DeviceIdType.MESH
        )
    pl.semaphore_wait(barrier, len(near) + 2)
    side = spot(z, y, 1 - core)
    state = {}

    def open_extras():
        spread = []
        for step in (1, 3, 2):
            there = lax.rem(z + step, SIDE)
            spread.append(
                copies.go(
                    wkv_ref.at[there], wkv_all_ref.at[z, y, core], "tensor", spot(there, y, core)
                )
            )
        state["spread"] = spread
        half = factors_ref.at[pl.ds(4 * group + 2 * core, 2)]
        mine = shrink_ref.at[pl.ds(2 * core, 2)]
        state["factors"] = [copies.go(mine, half, "dp", up), copies.go(mine, half, "dp", down)]

    def kv(y_at, first=0, count=4):
        return wkv_all_ref.at[pl.ds(first, count), lax.rem(y_at, SIDE), core]

    def middle_extras():
        for copy in state["spread"]:
            copy.wait_recv()
        homes[1].wait()
        block = kv(y)
        state["kv"] = [
            copies.go(block, block, "tensor", spot(z, y + 1, core)),
            copies.go(block, block, "tensor", spot(z, y + 3, core)),
        ]
        state["shared"] = [copies.go(block, block, "tensor", side)]
        for which, (origin, target) in enumerate(((down, up), (up, down))):
            state["factors"][which].wait_recv()
            one = factors_ref.at[4 * origin + 2 * core + which]
            state["factors"].append(copies.go(one, one, "dp", target))
            both = factors_ref.at[pl.ds(4 * origin + 2 * core, 2)]
            state["shared"].append(copies.go(both, both, "tensor", side))

    def pass_extras():
        for which, (origin, target) in enumerate(((y + 3, y + 1), (y + 1, y + 3))):
            state["kv"][which].wait_recv()
            piece = kv(origin, 2 * which, 2)
            state["kv"].append(copies.go(piece, piece, "tensor", spot(z, target, core)))
            whole = kv(origin)
            state["shared"].append(copies.go(whole, whole, "tensor", side))
        state["factors"][2].wait_recv()
        state["factors"][3].wait_recv()
        both = factors_ref.at[pl.ds(4 * across + 2 * core, 2)]
        state["shared"].append(copies.go(both, both, "tensor", side))

    def close_extras():
        state["kv"][2].wait_recv()
        state["kv"][3].wait_recv()
        whole = kv(y + 2)
        state["shared"].append(copies.go(whole, whole, "tensor", side))

    open_extras()
    gather_rows(rows_ref, z, y, core, copies, [middle_extras, pass_extras, close_extras])
    for copy in state["shared"]:
        copy.wait_recv()
    homes[0].wait()
    copies.settle()
    assert copies.n == GATHER_COPIES + EXTRA_COPIES, copies.n


def enter(tokens, gain, shrink, wkv):
    rows, width = tokens.shape
    count = GATHER_COPIES + EXTRA_COPIES
    return pl.pallas_call(
        enter_kernel,
        out_shape=(
            jax.ShapeDtypeStruct((32, rows, width), jnp.bfloat16),
            jax.ShapeDtypeStruct((4 * shrink.shape[0],) + shrink.shape[1:], jnp.bfloat16),
            jax.ShapeDtypeStruct((4, 4, 2) + wkv.shape[1:], jnp.bfloat16),
        ),
        in_specs=[
            pl.BlockSpec(memory_space=pltpu.VMEM),
            pl.BlockSpec(memory_space=pltpu.VMEM),
            pl.BlockSpec(memory_space=pl.ANY),
            pl.BlockSpec(memory_space=pl.ANY),
        ],
        out_specs=(
            pl.BlockSpec(memory_space=pltpu.VMEM),
            pl.BlockSpec(memory_space=pl.ANY),
            pl.BlockSpec(memory_space=pl.ANY),
        ),
        scratch_shapes=[
            pltpu.SemaphoreType.DMA((2,)),
            pltpu.SemaphoreType.DMA((count,)),
            pltpu.SemaphoreType.DMA((count,)),
        ],
        compiler_params=pltpu.CompilerParams(
            collective_id=0, has_side_effects=True, vmem_limit_bytes=VMEM_LIMIT
        ),
    )(tokens, gain.reshape(1, width), shrink, wkv)


def late_kernel(
    terms_ref,
    tokens_ref,
    gain_ref,
    ids_ref,
    gates_ref,
    w_gate_ref,
    w_up_ref,
    w_down_ref,
    out_ref,
    moe_ref,
    acc,
    sib,
    landed,
    local,
    total,
    rows,
    gate,
    up,
    down,
    slots,
    stage,
    pick,
    mix,
    weights_sem,
    send,
    recv,
):
    me, z, y, core = whereabouts()
    side = spot(z, y, 1 - core)
    f32, bf16 = jnp.float32, jnp.bfloat16
    experts, hidden_width, width = w_gate_ref.shape
    fetches = []
    for number, (source, held) in enumerate(
        ((w_gate_ref, gate), (w_up_ref, up), (w_down_ref, down))
    ):
        for expert in range(experts):
            fetch = pltpu.make_async_copy(
                source.at[expert], held.at[expert], weights_sem.at[number * experts + expert]
            )
            fetch.start()
            fetches.append(fetch)
    greet(partners(z, y, core))
    copies = Copies(send, recv)
    ensure, arrived = terms_from(terms_ref, acc, sib, local, z, y, core, copies)

    tokens_here = ids_ref.shape[1]
    places = experts * CAP_DEV
    slot = lax.broadcasted_iota(jnp.int32, (places, 1), 0)
    expert_of = me * experts + lax.div(slot, CAP_DEV)
    gates = gates_ref[...]
    gate_sum = jnp.sum(gates, axis=0, keepdims=True)
    hit = jnp.zeros((places, tokens_here), f32)
    weight = jnp.zeros((places, tokens_here), f32)
    for choice in range(ids_ref.shape[0]):
        same = ids_ref[choice : choice + 1, :] == expert_of
        hit = hit + jnp.where(same, 1.0, 0.0)
        weight = weight + jnp.where(same, gates_ref[choice : choice + 1, :], 0.0)
    weight = weight / gate_sum
    chunk = 256
    block = 64
    above = lax.broadcasted_iota(jnp.int32, (chunk, chunk), 0)
    right = lax.broadcasted_iota(jnp.int32, (chunk, chunk), 1)
    within = lax.div(above, block) == lax.div(right, block)
    prefix = jnp.where(within & (above <= right), 1.0, 0.0).astype(bf16)
    same_row = jnp.where(above == right, 1.0, 0.0).astype(bf16)
    number_in_block = (lax.rem(slot, CAP_DEV) + 1).astype(f32)
    for begin in range(0, tokens_here, chunk):
        piece = hit[:, begin : begin + chunk]
        count = jnp.dot(piece.astype(bf16), prefix, preferred_element_type=f32)
        taken = (piece > 0.5) & (count == number_in_block)
        pick[:, begin : begin + chunk] = jnp.where(taken, 1.0, 0.0).astype(bf16)
        shares = jnp.where(taken, weight[:, begin : begin + chunk], 0.0).astype(bf16)
        mix[pl.ds(begin, chunk), :] = lax.dot_general(
            same_row, shares, (((1,), (1,)), ((), ())), preferred_element_type=f32
        ).astype(bf16)

    scatter_rows(acc, sib, landed, z, y, core, copies, total, ensure, arrived)
    summed = total[...]
    out_ref[...] = summed.astype(out_ref.dtype)
    rows[me] = normalize(tokens_ref[...].astype(f32) + summed, gain_ref[...]).astype(rows.dtype)
    gather_rows(rows, z, y, core, copies)
    copies.settle()

    group = chunk // block
    lane_block = lax.div(lax.broadcasted_iota(jnp.int32, (1, chunk), 1), block)
    for number in range(tokens_here // chunk):
        piece = pick[:, number * chunk : (number + 1) * chunk]
        spread = jnp.concatenate(
            [jnp.where(lane_block == part, piece, jnp.zeros_like(piece)) for part in range(group)],
            axis=0,
        )
        block_rows = rows[number * group : (number + 1) * group].reshape(chunk, width)
        taken_rows = jnp.dot(spread, block_rows, preferred_element_type=f32).astype(bf16)
        slots[number * group : (number + 1) * group] = taken_rows.reshape(group, places, width)

    blocks = tokens_here // block
    for expert in range(experts):
        here = slice(expert * CAP_DEV, (expert + 1) * CAP_DEV)
        taken_rows = slots[:, here, :].reshape(blocks * CAP_DEV, width)
        fetches[expert].wait()
        gated = lax.dot_general(
            taken_rows, gate[expert], (((1,), (1,)), ((), ())), preferred_element_type=f32
        )
        fetches[experts + expert].wait()
        raised = lax.dot_general(
            taken_rows, up[expert], (((1,), (1,)), ((), ())), preferred_element_type=f32
        )
        hidden = (gated / (1.0 + jnp.exp(-gated)) * raised).astype(bf16)
        fetches[2 * experts + expert].wait()
        for begin in range(0, width, 512):
            piece = jnp.dot(
                hidden, down[expert, :, begin : begin + 512], preferred_element_type=f32
            ).astype(bf16)
            slots[:, here, begin : begin + 512] = piece.reshape(blocks, CAP_DEV, 512)

    shared = {}
    waited = set()

    def combine(index):
        part = mix[pl.ds(pl.multiple_of(index * block, block), block), :]
        return jnp.dot(part, slots[index], preferred_element_type=f32).astype(bf16)

    def make(cells):
        for i, j in cells:
            if (i, j) in shared:
                continue
            stage[i, j] = combine(spot(z + i, y + j, 1 - core))
            shared[i, j] = copies.go(stage.at[i, j], sib.at[i, j], "tensor", side)
            acc[i, j] = combine(spot(z + i, y + j, core))

    def came(number, v, u):
        where = cell(number, v, u)
        make([where])
        if where not in waited:
            waited.add(where)
            shared[where].wait_recv()

    scatter_rows(acc, sib, landed, z, y, core, copies, total, make, came)
    moe_ref[...] = total[...].astype(moe_ref.dtype)
    copies.settle()
    assert copies.n == LATE_COPIES, copies.n


LATE_COPIES = FIRST_COPIES + GATHER_COPIES + SECOND_COPIES


def late(terms, tokens, gain, ids, gates, w_gate, w_up, w_down):
    rows, width = tokens.shape
    experts = w_gate.shape[0]
    places = experts * CAP_DEV
    everyone = terms.shape[0]
    vmem = pl.BlockSpec(memory_space=pltpu.VMEM)
    far = pl.BlockSpec(memory_space=pl.ANY)
    return pl.pallas_call(
        late_kernel,
        out_shape=(jax.ShapeDtypeStruct((rows, width), jnp.bfloat16),) * 2,
        in_specs=[far, vmem, vmem, vmem, vmem, far, far, far],
        out_specs=(vmem, vmem),
        scratch_shapes=scatter_scratch(width)
        + [
            pltpu.VMEM((rows, width), jnp.float32),
            pltpu.VMEM((everyone, rows, width), jnp.bfloat16),
            pltpu.VMEM(w_gate.shape, jnp.bfloat16),
            pltpu.VMEM(w_up.shape, jnp.bfloat16),
            pltpu.VMEM(w_down.shape, jnp.bfloat16),
            pltpu.VMEM((everyone, places, width), jnp.bfloat16),
            pltpu.VMEM((4, 4, rows, width), jnp.bfloat16),
            pltpu.VMEM((places, everyone * rows), jnp.bfloat16),
            pltpu.VMEM((everyone * rows, places), jnp.bfloat16),
            pltpu.SemaphoreType.DMA((3 * experts,)),
            pltpu.SemaphoreType.DMA((LATE_COPIES,)),
            pltpu.SemaphoreType.DMA((LATE_COPIES,)),
        ],
        compiler_params=pltpu.CompilerParams(
            collective_id=1, has_side_effects=True, vmem_limit_bytes=VMEM_LIMIT
        ),
    )(terms, tokens, gain.reshape(1, width), ids, gates, w_gate, w_up, w_down)


BLOCK = 512
KEY_BLOCK = 256
TRANSPOSED = (((1,), (1,)), ((), ()))


def heart_kernel(
    lens_s,
    groups_s,
    pages_s,
    lens_ref,
    groups_ref,
    adapters_ref,
    slots_ref,
    q_gain_ref,
    k_gain_ref,
    x_ref,
    factors_ref,
    wkv_ref,
    wq_ref,
    q_up_ref,
    kv_up_ref,
    wo_ref,
    shrink_o_ref,
    expand_ref,
    out_ref,
    pages_ref,
    tab,
    keys,
    values,
    across,
    acc,
):
    step = pl.program_id(0)
    place = lax.axis_index("tensor")
    head = lax.div(place, 8)
    f32, bf16 = jnp.float32, jnp.bfloat16
    requests = lens_ref.shape[1]
    adapters = slots_ref.shape[1]
    depth = wq_ref.shape[1]

    @pl.when(step == 0)
    def _():
        down = lax.broadcasted_iota(jnp.int32, (requests, requests), 0)
        over = lax.broadcasted_iota(jnp.int32, (requests, requests), 1)

        def column(row, number):
            a = lax.broadcasted_iota(jnp.int32, (number, number), 0)
            b = lax.broadcasted_iota(jnp.int32, (number, number), 1)
            return jnp.sum(
                jnp.where(a == b, jnp.broadcast_to(row, (number, number)), 0.0),
                axis=1,
                keepdims=True,
            )

        lens = lens_ref[...].astype(f32)
        groups = groups_ref[...].astype(f32)
        chosen = adapters_ref[...]
        slots = column(slots_ref[...].astype(f32), adapters)
        ends = jnp.sum(jnp.where(down <= over, column(lens, requests), 0.0), axis=0, keepdims=True)
        starts = ends - lens
        same = column(groups, requests) == groups
        firsts = jnp.min(
            jnp.where(same, column(starts, requests), 1e9), axis=0, keepdims=True
        )
        which = lax.broadcasted_iota(jnp.int32, (adapters, requests), 0)
        slot = jnp.sum(jnp.where(which == chosen, slots, 0.0), axis=0, keepdims=True)
        tab[0:1, :] = starts
        tab[1:2, :] = ends
        tab[2:3, :] = firsts
        tab[3:4, :] = slot

    first_row = step * BLOCK
    row = first_row + lax.broadcasted_iota(jnp.int32, (BLOCK, 1), 0)
    row_f = row.astype(f32)
    inside = (row_f >= tab[0:1, :]) & (row_f < tab[1:2, :])
    rope = row_f - jnp.sum(jnp.where(inside, tab[2:3, :], 0.0), axis=1, keepdims=True)
    slot = jnp.sum(jnp.where(inside, tab[3:4, :], 0.0), axis=1, keepdims=True).astype(jnp.int32)

    lane = lax.broadcasted_iota(jnp.int32, (1, depth), 1)
    half = depth // 2
    low = lane < half
    freq = jnp.exp(
        -jnp.where(low, lane, lane - half).astype(f32) * (2.0 * math.log(ROPE_BASE) / depth)
    )
    mixed_trig = jnp.sin(rope * freq + jnp.where(low, 0.5 * math.pi, 0.0))
    other_trig = pltpu.roll(mixed_trig, half, 1)
    cosine = jnp.where(low, mixed_trig, other_trig)
    sine = jnp.where(low, -other_trig, mixed_trig)

    def turn(vector):
        return vector * cosine + pltpu.roll(vector, half, 1) * sine

    def unit(vector, gain_ref):
        return (
            vector
            * lax.rsqrt(jnp.mean(vector * vector, axis=-1, keepdims=True) + NORM_EPS)
            * gain_ref[...].astype(f32)
        )

    rank = factors_ref.shape[1] // 3
    mine = slot == lax.div(lax.broadcasted_iota(jnp.int32, (1, adapters * rank), 1), rank)
    x = x_ref[...]
    lora = []
    for part in range(3):
        table = factors_ref[:, part * rank : (part + 1) * rank, :].reshape(adapters * rank, -1)
        shrunk = lax.dot_general(x, table, TRANSPOSED, preferred_element_type=f32)
        placed = jnp.where(mine, shrunk, 0.0).astype(bf16)
        if part == 0:
            up = q_up_ref[...]
        else:
            begin = pl.multiple_of(head * 2 * depth + (part - 1) * depth, depth)
            up = kv_up_ref[:, pl.ds(begin, depth)]
        lora.append(ADAPTER_FACTOR * jnp.dot(placed, up, preferred_element_type=f32))
    query = jnp.dot(x, wq_ref[...], preferred_element_type=f32) + lora[0]
    query = turn(unit(query, q_gain_ref)).astype(bf16)
    kv = lax.dot_general(x, wkv_ref[...], TRANSPOSED, preferred_element_type=f32)
    raw = (kv[:, :depth] + lora[1]).astype(bf16).astype(f32)
    key = turn(unit(raw, k_gain_ref)).astype(bf16)
    value = (kv[:, depth:] + lora[2]).astype(bf16)
    keys[pl.ds(first_row, BLOCK), :] = key
    values[pl.ds(first_row, BLOCK), 0:depth] = value
    values[pl.ds(first_row, BLOCK), depth:] = jnp.broadcast_to(
        jnp.where(lane == 0, 1.0, 0.0), (BLOCK, depth)
    ).astype(bf16)

    columns = pages_ref.shape[1]
    offset = lax.rem(place, 8) * columns
    pick_row = lax.broadcasted_iota(jnp.int32, (columns, 2 * depth), 0) + offset
    pick_lane = lax.broadcasted_iota(jnp.int32, (columns, 2 * depth), 1)
    pick = jnp.where(pick_row == pick_lane, 1.0, 0.0).astype(bf16)
    across[:, pl.ds(pl.multiple_of(first_row, BLOCK), BLOCK)] = lax.dot_general(
        pick, jnp.concatenate([key, value], axis=1), TRANSPOSED, preferred_element_type=f32
    )

    def look(number, carry):
        start, lead, found, before = carry
        group = groups_s[0, number]
        lead = jnp.where(group == before, lead, start)
        found = jnp.where(start <= first_row, lead, found)
        return start + lens_s[0, number], lead, found, group

    zero = jnp.int32(0)
    found = lax.fori_loop(0, requests, look, (zero, zero, zero, jnp.int32(-1)))[2]
    acc[...] = jnp.zeros_like(acc)
    gap = lax.broadcasted_iota(jnp.int32, (BLOCK, KEY_BLOCK), 0) - lax.broadcasted_iota(
        jnp.int32, (BLOCK, KEY_BLOCK), 1
    )
    reach = rope.astype(jnp.int32)
    scale = depth**-0.5

    def over_keys(number, carry):
        begin = pl.multiple_of(number * KEY_BLOCK, KEY_BLOCK)
        scores = lax.dot_general(
            query, keys[pl.ds(begin, KEY_BLOCK), :], TRANSPOSED, preferred_element_type=f32
        )
        behind = gap + (first_row - begin)
        raised = jnp.where((behind >= 0) & (behind <= reach), jnp.exp(scores * scale), 0.0)
        acc[...] += jnp.dot(
            raised.astype(bf16), values[pl.ds(begin, KEY_BLOCK), :], preferred_element_type=f32
        )
        return carry

    lax.fori_loop(
        lax.div(found, KEY_BLOCK), (step + 1) * (BLOCK // KEY_BLOCK), over_keys, jnp.int32(0)
    )
    mixed = (acc[:, :depth] / acc[:, depth : depth + 1]).astype(bf16)
    shrunk = lax.dot_general(mixed, shrink_o_ref[...], TRANSPOSED, preferred_element_type=f32)
    placed = jnp.where(mine, ADAPTER_FACTOR * shrunk, 0.0).astype(bf16)
    width = out_ref.shape[-1]
    for begin in range(0, width, 512):
        term = jnp.dot(mixed, wo_ref[:, begin : begin + 512], preferred_element_type=f32)
        term = term + jnp.dot(
            placed, expand_ref[:, begin : begin + 512], preferred_element_type=f32
        )
        out_ref[:, begin : begin + 512] = term.astype(bf16)

    @pl.when(step == pl.num_programs(0) - 1)
    def _():
        spot_lane = lax.broadcasted_iota(jnp.int32, (columns, PAGE), 1)

        def fill(number, start):
            length = lens_s[0, number]
            for part in range(2):
                begin = start + part * PAGE
                aligned = pl.multiple_of(lax.div(begin, PAGE) * PAGE, PAGE)
                window = across[:, pl.ds(aligned, 2 * PAGE)]
                shift = lax.rem(2 * PAGE - (begin - aligned), 2 * PAGE)
                rolled = pltpu.roll(window, shift, 1)[:, :PAGE]
                kept = jnp.where(spot_lane < length - part * PAGE, rolled, 0.0)
                pages_ref[pages_s[0, number * 2 + part]] = kept.astype(bf16)
            return start + length

        lax.fori_loop(0, requests, fill, zero)


def heart(
    lengths,
    groups,
    adapter_of_request,
    adapter_slot,
    page_table,
    q_gain,
    k_gain,
    x,
    factors,
    wkv,
    query_weight,
    query_up,
    kv_up,
    w_o,
    shrink_o,
    expand_o,
):
    total, width = x.shape
    depth = query_weight.shape[1]
    requests = lengths.shape[1]
    pages = page_table.shape[1]
    columns = 2 * kv_up.shape[1] // 64
    slots = adapter_slot.shape[0]
    smem = pl.BlockSpec(memory_space=pltpu.SMEM)

    def whole(array):
        return pl.BlockSpec(
            array.shape, lambda i: (0,) * array.ndim, pipeline_mode=pl.Buffered(1)
        )

    small = (
        lengths,
        groups,
        adapter_of_request,
        adapter_slot.reshape(1, slots),
        q_gain.reshape(1, depth),
        k_gain.reshape(1, depth),
    )
    tables = (factors, wkv, query_weight, query_up, kv_up, w_o, shrink_o, expand_o)
    return pl.pallas_call(
        heart_kernel,
        grid=(total // BLOCK,),
        out_shape=(
            jax.ShapeDtypeStruct((total, width), jnp.bfloat16),
            jax.ShapeDtypeStruct((pages, columns, PAGE), jnp.bfloat16),
        ),
        in_specs=[smem, smem, smem]
        + [whole(array) for array in small]
        + [pl.BlockSpec((BLOCK, width), lambda i: (i, 0))]
        + [whole(array) for array in tables],
        out_specs=(
            pl.BlockSpec((BLOCK, width), lambda i: (i, 0)),
            pl.BlockSpec((pages, columns, PAGE), lambda i: (0, 0, 0)),
        ),
        scratch_shapes=[
            pltpu.VMEM((8, requests), jnp.float32),
            pltpu.VMEM((total, depth), jnp.bfloat16),
            pltpu.VMEM((total, 2 * depth), jnp.bfloat16),
            pltpu.VMEM((columns, total + 4 * PAGE), jnp.float32),
            pltpu.VMEM((BLOCK, 2 * depth), jnp.float32),
        ],
        compiler_params=pltpu.CompilerParams(vmem_limit_bytes=VMEM_LIMIT),
    )(lengths, groups, page_table, *small, x, *tables)


def local(
    tokens,
    attn_gain,
    moe_gain,
    q_gain,
    k_gain,
    query_weight,
    w_kv,
    w_o,
    w_gate,
    w_up,
    w_down,
    shrink_qkv,
    shrink_o,
    query_up_factors,
    key_value_up_factors,
    expand_o,
    lengths,
    groups,
    adapter_of_request,
    adapter_slot,
    page_table,
    expert_ids,
    expert_gates,
):
    parts = lax.axis_size("tensor")
    place = lax.axis_index("tensor")
    own_rows, width = tokens.shape
    grand_total = own_rows * parts
    adapters, rank, kv_width = key_value_up_factors.shape
    x_rows, factors, wkv_all = enter(tokens, attn_gain, shrink_qkv, w_kv.transpose(1, 0, 2))
    head_width = 2 * q_gain.shape[0]
    attn_terms, kv_pages = heart(
        lengths,
        groups,
        adapter_of_request,
        adapter_slot,
        page_table,
        q_gain,
        k_gain,
        x_rows.reshape(grand_total, width),
        factors,
        wkv_all.reshape(head_width, width),
        query_weight,
        query_up_factors.reshape(adapters * rank, -1),
        key_value_up_factors.reshape(adapters * rank, kv_width),
        w_o,
        shrink_o.reshape(adapters * rank, -1),
        expand_o.reshape(adapters * rank, width),
    )
    attn_out, moe_total = late(
        attn_terms.reshape(parts, own_rows, width),
        tokens,
        moe_gain,
        expert_ids.T,
        expert_gates.T,
        w_gate,
        w_up,
        w_down,
    )
    return (attn_out, moe_total, kv_pages)


def solution(mesh):
    placed = (
        P(("dp", "tensor"), None),
        P(),
        P(),
        P(),
        P(),
        P(None, "tensor"),
        P("tensor", None, None),
        P("tensor", None),
        P("tensor", None, None),
        P("tensor", None, None),
        P("tensor", None, None),
        P("dp", None, None),
        P(None, None, "tensor"),
        P(None, None, "tensor"),
        P(),
        P(),
        P("dp", None),
        P("dp", None),
        P("dp", None),
        P(),
        P("dp", None),
        P("dp", None),
        P("dp", None),
    )
    return jax.shard_map(
        local,
        mesh=mesh,
        in_specs=placed,
        out_specs=(P(("dp", "tensor"), None), P(("dp", "tensor"), None), P("dp", "tensor", None)),
        check_vma=False,
    )
```

```python
import functools
import math
import jax, jax.numpy as jnp
from jax import lax
from jax.experimental import pallas as pl
from jax.experimental.pallas import tpu as pltpu
from jax.sharding import PartitionSpec as P

SIDE = 4
HALF = 32

def spot(z, y, core):
    return lax.rem(z, SIDE) * 8 + lax.rem(y, SIDE) * 2 + core

def whereabouts():
    me = lax.axis_index("tensor")
    return me, lax.div(me, 8), lax.rem(lax.div(me, 2), SIDE), lax.rem(me, 2)

def greet(partners):
    barrier = pltpu.get_barrier_semaphore()
    for partner in partners:
        pl.semaphore_signal(barrier, inc=1, device_id={"tensor": partner}, device_id_type=pl.DeviceIdType.MESH)
    pl.semaphore_wait(barrier, len(partners))

class Copies:
    def __init__(self, send, recv):
        self.send, self.recv, self.n, self.all = send, recv, 0, []
    def make(self, src, dst, axis, target):
        k = self.n
        self.n += 1
        copy = pltpu.make_async_remote_copy(src_ref=src, dst_ref=dst, send_sem=self.send.at[k], recv_sem=self.recv.at[k],
            device_id={axis: target}, device_id_type=pl.DeviceIdType.MESH)
        self.all.append(copy)
        return copy
    def go(self, src, dst, axis, target):
        copy = self.make(src, dst, axis, target)
        copy.start()
        return copy
    def settle(self):
        for copy in self.all:
            copy.wait_send()
        self.all = []

EARLY = ((0, 0), (0, 1), (0, 3), (1, 0), (3, 0))
MIDDLE = ((2, 0), (0, 2), (3, 3), (3, 1), (1, 3), (1, 1))
LAST = ((3, 2), (2, 3), (2, 1), (1, 2), (2, 2))
CELLS = EARLY + MIDDLE + LAST


def gather_rows(out, z, y, core, copies, hooks):
    side = spot(z, y, 1 - core)
    shared = {}
    waited = set()

    def ready(cells):
        for i, j in cells:
            for key in ((0, i, j), (1, i, j)):
                if key in shared and key not in waited:
                    waited.add(key)
                    shared[key].wait_recv()

    def hook(name):
        if name in hooks:
            hooks[name](ready)

    def share(block, row, rows, number, u, v):
        piece = out.at[block, pl.ds(row, rows)]
        where = (number, v, u) if number == 0 else (number, u, v)
        shared[where] = copies.go(piece, piece, "tensor", side)

    def send(block, row, rows, target):
        piece = out.at[block, pl.ds(row, rows)]
        return copies.go(piece, piece, "tensor", target)
    class Part: pass
    parts = []
    for number in range(2):
        p = Part()
        p.row = number * HALF
        p.number = number
        if number == 0:
            p.at = lambda u, v: spot(z + v, y + u, core)
        else:
            p.at = lambda u, v: spot(z + u, y + v, core)
        parts.append(p)
    def ring_open(p, along_u, u):
        block = p.at(u, 0)
        up, down = (p.at(1, 0), p.at(3, 0)) if along_u else (p.at(0, 1), p.at(0, 3))
        return [send(block, p.row, HALF, up), send(block, p.row, HALF, down)]
    def ring_pass(p, along_u, u, opened, which):
        opened[which].wait_recv()
        off = 3 if which == 0 else 1
        block = p.at(off, 0) if along_u else p.at(u, off)
        target = (p.at(1, 0), p.at(3, 0))[which] if along_u else (p.at(0, 1), p.at(0, 3))[which]
        fwd = send(block, p.row + which * (HALF // 2), HALF // 2, target)
        share(block, p.row, HALF, p.number, *((off, 0) if along_u else (u, off)))
        return fwd
    me = spot(z, y, core)
    for p in parts:
        p.u = ring_open(p, True, 0)
    for p in parts:
        p.v = {0: ring_open(p, False, 0)}
    share(me, 0, 2 * HALF, 0, 0, 0)
    hook("opened")
    for which in range(2):
        for p in parts:
            p.u.append(ring_pass(p, True, 0, p.u, which))
            off = 3 if which == 0 else 1
            p.v[off] = ring_open(p, False, off)
    for which in range(2):
        for p in parts:
            p.v[0].append(ring_pass(p, False, 0, p.v[0], which))
    hook("early")
    for p in parts:
        p.u[2].wait_recv()
        p.u[3].wait_recv()
        share(p.at(2, 0), p.row, HALF, p.number, 2, 0)
        p.v[2] = ring_open(p, False, 2)
    for off in (3, 1):
        for which in range(2):
            for p in parts:
                p.v[off].append(ring_pass(p, False, off, p.v[off], which))
        for p in parts:
            done = 0 if off == 3 else 3
            p.v[done][2].wait_recv()
            p.v[done][3].wait_recv()
            share(p.at(done, 2), p.row, HALF, p.number, done, 2)
        if off == 3:
            hook("third")
    for which in range(2):
        for p in parts:
            p.v[2].append(ring_pass(p, False, 2, p.v[2], which))
    hook("middle")
    for off in (1, 2):
        for p in parts:
            p.v[off][2].wait_recv()
            p.v[off][3].wait_recv()
            share(p.at(off, 2), p.row, HALF, p.number, off, 2)
    hook("last")
    ready(CELLS)
    assert len(waited) == len(shared)

def add_rows(dst, start, rows, sources):
    for first in range(0, rows, 16):
        total = dst[pl.ds(start + first, 16)].astype(jnp.float32)
        for ref, row in sources:
            total = total + ref[pl.ds(row + first, 16)].astype(jnp.float32)
        dst[pl.ds(start + first, 16)] = total.astype(dst.dtype)

ORDER = (2, 1, 3, 0)
FIRST_COPIES = 32 + 32 + 8
SECOND_COPIES = 16 + 32 + 8


def cell(number, v, u):
    return (v, u) if number == 0 else (u, v)


def scatter_rows(acc, sib, landed, z, y, core, copies, result, ensure, arrived):
    def neighbour(number, along_v, step):
        along_z = (number == 0) == along_v
        return spot(z + step, y, core) if along_z else spot(z, y + step, core)
    def own(number, v, u):
        return acc.at[cell(number, v, u)]
    def pair(number, v, u):
        arrived(number, v, u)
        return (sib.at[cell(number, v, u)], number * HALF)
    def buf(number, u):
        return landed.at[number * 5 + u]
    ring = {}
    def far(number, along_v, u, block):
        row = number * HALF
        b = buf(number, u)
        key = (number, u)
        ring[key] = [
            copies.go(block.at[pl.ds(row, 16)], b.at[pl.ds(0, 16)], "tensor", neighbour(number, along_v, 1)),
            copies.go(block.at[pl.ds(row + 16, 16)], b.at[pl.ds(16, 16)], "tensor", neighbour(number, along_v, 3)),
        ]
    def near(number, along_v, u, block, which):
        row = number * HALF
        b = buf(number, u)
        ring[number, u].append(
            copies.go(block.at[pl.ds(row, HALF)], b.at[pl.ds(32 + 32 * which, HALF)], "tensor",
                      neighbour(number, along_v, (1, 3)[which])))
    ensure([(2, u) for u in ORDER] + [(u, 2) for u in ORDER[1:]])
    for u in ORDER:
        for number in range(2):
            block = own(number, 2, u)
            add_rows(block, number * HALF, HALF, [pair(number, 2, u)])
            far(number, True, u, block)
    ensure([(i, j) for i in ORDER[1:] for j in ORDER[1:]])
    for u in ORDER:
        for number in range(2):
            row = number * HALF
            for which in range(2):
                v = (1, 3)[which]
                block = own(number, v, u)
                other, first = pair(number, v, u)
                ring[number, u][which].wait_recv()
                for part in range(2):
                    sources = [(other, first + 16 * part)]
                    if part == which:
                        sources.append((buf(number, u), 16 * which))
                    add_rows(block, row + 16 * part, 16, sources)
                near(number, True, u, block, which)
    for u in ORDER:
        for number in range(2):
            row = number * HALF
            block = own(number, 0, u)
            source = pair(number, 0, u)
            b = buf(number, u)
            ring[number, u][2].wait_recv()
            ring[number, u][3].wait_recv()
            sources = [source, (b, 32), (b, 64)]
            last = buf(number, 4)
            if u == 2:
                add_rows(block, row, HALF, sources)
                far(number, False, 4, block)
            elif u in (1, 3):
                which = (1, 3).index(u)
                ring[number, 4][which].wait_recv()
                for part in range(2):
                    more = [(ref, r + 16 * part) for ref, r in sources]
                    if part == which:
                        more.append((last, 16 * which))
                    add_rows(block, row + 16 * part, 16, more)
                near(number, False, 4, block, which)
            else:
                ring[number, 4][2].wait_recv()
                ring[number, 4][3].wait_recv()
                for first in range(0, HALF, 16):
                    total = block[pl.ds(row + first, 16)].astype(jnp.float32)
                    for ref, r in sources + [(last, 32), (last, 64)]:
                        total = total + ref[pl.ds(r + first, 16)].astype(jnp.float32)
                    result[pl.ds(row + first, 16)] = total

def terms_from(terms, acc, sib, local, z, y, core, copies):
    side = spot(z, y, 1 - core)
    loads, shared = {}, {}
    for v in ORDER:
        for u in ORDER:
            for number in range(2):
                i, j = cell(number, v, u)
                rows = pl.ds(number * HALF, HALF)
                shared[number, v, u] = copies.go(
                    terms.at[spot(z + i, y + j, 1 - core), rows], sib.at[i, j, rows], "tensor", side
                )
                load = pltpu.make_async_copy(
                    terms.at[spot(z + i, y + j, core), rows],
                    acc.at[i, j, rows],
                    local.at[number * 16 + v * 4 + u],
                )
                load.start()
                loads[number, v, u] = load

    def arrived(number, v, u):
        loads[number, v, u].wait()
        shared[number, v, u].wait_recv()

    return (lambda cells: None), arrived


def scatter_scratch(width):
    return [
        pltpu.VMEM((4, 4, 64, width), jnp.bfloat16),
        pltpu.VMEM((4, 4, 64, width), jnp.bfloat16),
        pltpu.VMEM((10, 96, width), jnp.bfloat16),
        pltpu.SemaphoreType.DMA((32,)),
    ]

def partners(z, y, core):
    return [spot(z, y, 1 - core), spot(z + 1, y, core), spot(z + 3, y, core), spot(z, y + 1, core), spot(z, y + 3, core)]


GATHER_COPIES = 2 * 20 + 31
EXTRA_COPIES = 9 + 11
NORM_EPS = 1e-06
ROPE_BASE = 1000000.0
ADAPTER_FACTOR = 0.5
PAGE = 128
CAP_DEV = 16
VMEM_LIMIT = 62 << 20


def normalize(values, gain):
    return (
        values
        * lax.rsqrt(jnp.mean(values * values, axis=-1, keepdims=True) + NORM_EPS)
        * gain.astype(jnp.float32)
    )


def enter_kernel(
    tokens_ref, gain_ref, shrink_ref, wkv_ref, rows_ref, factors_ref, wkv_all_ref, local, send, recv
):
    me, z, y, core = whereabouts()
    group = lax.axis_index("dp")
    up, down = lax.rem(group + 1, SIDE), lax.rem(group + 3, SIDE)
    across = lax.rem(group + 2, SIDE)
    copies = Copies(send, recv)
    homes = [
        pltpu.make_async_copy(shrink_ref.at[held], factors_ref.at[:, 4 * group + held], local.at[held])
        for held in range(4)
    ]
    homes.append(pltpu.make_async_copy(wkv_ref.at[z], wkv_all_ref.at[z, y, core], local.at[4]))
    for home in homes:
        home.start()
    rows_ref[me] = normalize(tokens_ref[...].astype(jnp.float32), gain_ref[...]).astype(
        rows_ref.dtype
    )
    barrier = pltpu.get_barrier_semaphore()
    near = partners(z, y, core) + [spot(z + 2, y, core)]
    for partner in near:
        pl.semaphore_signal(
            barrier, inc=1, device_id={"tensor": partner}, device_id_type=pl.DeviceIdType.MESH
        )
    for partner in (up, down):
        pl.semaphore_signal(
            barrier, inc=1, device_id={"dp": partner}, device_id_type=pl.DeviceIdType.MESH
        )
    pl.semaphore_wait(barrier, len(near) + 2)
    side = spot(z, y, 1 - core)
    state = {}

    def open_extras():
        spread = []
        for step in (1, 3, 2):
            there = lax.rem(z + step, SIDE)
            spread.append(
                copies.go(
                    wkv_ref.at[there], wkv_all_ref.at[z, y, core], "tensor", spot(there, y, core)
                )
            )
        state["spread"] = spread
        state["factors"] = [[], []]
        for held in range(2):
            slot = 2 * core + held
            for which, target in enumerate((up, down)):
                state["factors"][which].append(
                    copies.go(
                        shrink_ref.at[slot], factors_ref.at[:, 4 * group + slot], "dp", target
                    )
                )

    def kv(y_at, first=0, count=4):
        return wkv_all_ref.at[pl.ds(first, count), lax.rem(y_at, SIDE), core]

    def kv_extras(ready):
        for copy in state["spread"]:
            copy.wait_recv()
        homes[4].wait()
        block = kv(y)
        state["kv"] = [
            copies.go(block, block, "tensor", spot(z, y + 1, core)),
            copies.go(block, block, "tensor", spot(z, y + 3, core)),
        ]
        state["shared"] = [copies.go(block, block, "tensor", side)]

    def factor_extras(ready):
        state["far"] = []
        for which, (origin, target) in enumerate(((down, up), (up, down))):
            for copy in state["factors"][which]:
                copy.wait_recv()
            one = factors_ref.at[:, 4 * origin + 2 * core + which]
            state["far"].append(copies.go(one, one, "dp", target))
            both = factors_ref.at[:, pl.ds(4 * origin + 2 * core, 2)]
            state["shared"].append(copies.go(both, both, "tensor", side))
        pass_extras()

    def pass_extras():
        for which, (origin, target) in enumerate(((y + 3, y + 1), (y + 1, y + 3))):
            state["kv"][which].wait_recv()
            piece = kv(origin, 2 * which, 2)
            state["kv"].append(copies.go(piece, piece, "tensor", spot(z, target, core)))
            whole = kv(origin)
            state["shared"].append(copies.go(whole, whole, "tensor", side))

    def close_extras():
        for copy in state["far"]:
            copy.wait_recv()
        both = factors_ref.at[:, pl.ds(4 * across + 2 * core, 2)]
        state["shared"].append(copies.go(both, both, "tensor", side))
        state["kv"][2].wait_recv()
        state["kv"][3].wait_recv()
        whole = kv(y + 2)
        state["shared"].append(copies.go(whole, whole, "tensor", side))

    open_extras()
    gather_rows(
        rows_ref, z, y, core, copies, {"opened": kv_extras, "third": factor_extras}
    )
    close_extras()
    for copy in state["shared"]:
        copy.wait_recv()
    for home in homes[:4]:
        home.wait()
    copies.settle()
    assert copies.n == GATHER_COPIES + EXTRA_COPIES, copies.n


def enter(tokens, gain, shrink, wkv):
    rows, width = tokens.shape
    count = GATHER_COPIES + EXTRA_COPIES
    return pl.pallas_call(
        enter_kernel,
        out_shape=(
            jax.ShapeDtypeStruct((32, rows, width), jnp.bfloat16),
            jax.ShapeDtypeStruct((shrink.shape[1], 4 * shrink.shape[0]) + shrink.shape[2:], jnp.bfloat16),
            jax.ShapeDtypeStruct((4, 4, 2) + wkv.shape[1:], jnp.bfloat16),
        ),
        in_specs=[
            pl.BlockSpec(memory_space=pltpu.VMEM),
            pl.BlockSpec(memory_space=pltpu.VMEM),
            pl.BlockSpec(memory_space=pl.ANY),
            pl.BlockSpec(memory_space=pl.ANY),
        ],
        out_specs=(
            pl.BlockSpec(memory_space=pltpu.VMEM),
            pl.BlockSpec(memory_space=pltpu.VMEM),
            pl.BlockSpec(memory_space=pltpu.VMEM),
        ),
        scratch_shapes=[
            pltpu.SemaphoreType.DMA((5,)),
            pltpu.SemaphoreType.DMA((count,)),
            pltpu.SemaphoreType.DMA((count,)),
        ],
        compiler_params=pltpu.CompilerParams(
            collective_id=0, has_side_effects=True, vmem_limit_bytes=VMEM_LIMIT
        ),
    )(tokens, gain.reshape(1, width), shrink, wkv)


def late_kernel(
    terms_ref,
    tokens_ref,
    gain_ref,
    ids_ref,
    gates_ref,
    w_gate_ref,
    w_up_ref,
    w_down_ref,
    out_ref,
    moe_ref,
    acc,
    sib,
    landed,
    local,
    total,
    rows,
    gate,
    up,
    down,
    slots,
    stage,
    pick,
    mix,
    weights_sem,
    send,
    recv,
):
    me, z, y, core = whereabouts()
    side = spot(z, y, 1 - core)
    f32, bf16 = jnp.float32, jnp.bfloat16
    experts, hidden_width, width = w_gate_ref.shape
    fetches = []
    for number, (source, held) in enumerate(
        ((w_gate_ref, gate), (w_up_ref, up), (w_down_ref, down))
    ):
        for expert in range(experts):
            fetch = pltpu.make_async_copy(
                source.at[expert], held.at[expert], weights_sem.at[number * experts + expert]
            )
            fetch.start()
            fetches.append(fetch)
    greet(partners(z, y, core))
    copies = Copies(send, recv)
    ensure, arrived = terms_from(terms_ref, acc, sib, local, z, y, core, copies)

    tokens_here = ids_ref.shape[1]
    places = experts * CAP_DEV
    slot = lax.broadcasted_iota(jnp.int32, (places, 1), 0)
    expert_of = me * experts + lax.div(slot, CAP_DEV)
    gates = gates_ref[...]
    gate_sum = jnp.sum(gates, axis=0, keepdims=True)
    hit = jnp.zeros((places, tokens_here), f32)
    weight = jnp.zeros((places, tokens_here), f32)
    for choice in range(ids_ref.shape[0]):
        same = ids_ref[choice : choice + 1, :] == expert_of
        hit = hit + jnp.where(same, 1.0, 0.0)
        weight = weight + jnp.where(same, gates_ref[choice : choice + 1, :], 0.0)
    weight = weight / gate_sum
    chunk = 256
    block = 64
    above = lax.broadcasted_iota(jnp.int32, (chunk, chunk), 0)
    right = lax.broadcasted_iota(jnp.int32, (chunk, chunk), 1)
    within = lax.div(above, block) == lax.div(right, block)
    prefix = jnp.where(within & (above <= right), 1.0, 0.0).astype(bf16)
    same_row = jnp.where(above == right, 1.0, 0.0).astype(bf16)
    number_in_block = (lax.rem(slot, CAP_DEV) + 1).astype(f32)
    for begin in range(0, tokens_here, chunk):
        piece = hit[:, begin : begin + chunk]
        count = jnp.dot(piece.astype(bf16), prefix, preferred_element_type=f32)
        taken = (piece > 0.5) & (count == number_in_block)
        pick[:, begin : begin + chunk] = jnp.where(taken, 1.0, 0.0).astype(bf16)
        shares = jnp.where(taken, weight[:, begin : begin + chunk], 0.0).astype(bf16)
        mix[pl.ds(begin, chunk), :] = lax.dot_general(
            same_row, shares, (((1,), (1,)), ((), ())), preferred_element_type=f32
        ).astype(bf16)

    scatter_rows(acc, sib, landed, z, y, core, copies, total, ensure, arrived)
    summed = total[...]
    out_ref[...] = summed.astype(out_ref.dtype)
    rows[me] = normalize(tokens_ref[...].astype(f32) + summed, gain_ref[...]).astype(rows.dtype)
    pair_rows = 2 * block
    lane_block = lax.div(lax.broadcasted_iota(jnp.int32, (1, pair_rows), 1), block)

    def apply_experts(cells):
        first = CELLS.index(cells[0])
        for number, (i, j) in enumerate(cells):
            index = spot(z + i, y + j, 0)
            piece = pick[:, pl.ds(pl.multiple_of(index * block, pair_rows), pair_rows)]
            spread = jnp.concatenate(
                [jnp.where(lane_block == part, piece, jnp.zeros_like(piece)) for part in range(2)],
                axis=0,
            )
            taken_rows = jnp.dot(
                spread, rows[pl.ds(index, 2)].reshape(pair_rows, width), preferred_element_type=f32
            )
            slots[2 * (first + number) : 2 * (first + number) + 2] = taken_rows.astype(bf16).reshape(
                2, places, width
            )
        blocks = slice(2 * first, 2 * (first + len(cells)))
        count = 2 * len(cells)
        for expert in range(experts):
            here = slice(expert * CAP_DEV, (expert + 1) * CAP_DEV)
            taken_rows = slots[blocks, here, :].reshape(count * CAP_DEV, width)
            gated = lax.dot_general(
                taken_rows, gate[expert], (((1,), (1,)), ((), ())), preferred_element_type=f32
            )
            raised = lax.dot_general(
                taken_rows, up[expert], (((1,), (1,)), ((), ())), preferred_element_type=f32
            )
            hidden = (gated / (1.0 + jnp.exp(-gated)) * raised).astype(bf16)
            for begin in range(0, width, 512):
                piece = jnp.dot(
                    hidden, down[expert, :, begin : begin + 512], preferred_element_type=f32
                ).astype(bf16)
                slots[blocks, here, begin : begin + 512] = piece.reshape(count, CAP_DEV, 512)

    def early_experts(ready):
        for fetch in fetches:
            fetch.wait()
        ready(EARLY)
        apply_experts(EARLY)

    def middle_experts(ready):
        ready(EARLY + MIDDLE)
        apply_experts(MIDDLE)

    gather_rows(
        rows, z, y, core, copies, {"early": early_experts, "middle": middle_experts}
    )
    apply_experts(LAST)
    copies.settle()

    shared = {}
    waited = set()

    def combine(i, j, which):
        index = spot(z + i, y + j, which)
        part = mix[pl.ds(pl.multiple_of(index * block, block), block), :]
        held = slots[2 * CELLS.index((i, j)) + which]
        return jnp.dot(part, held, preferred_element_type=f32).astype(bf16)

    def make(cells):
        for i, j in cells:
            if (i, j) in shared:
                continue
            stage[i, j] = combine(i, j, 1 - core)
            shared[i, j] = copies.go(stage.at[i, j], sib.at[i, j], "tensor", side)
            acc[i, j] = combine(i, j, core)

    def came(number, v, u):
        where = cell(number, v, u)
        make([where])
        if where not in waited:
            waited.add(where)
            shared[where].wait_recv()

    scatter_rows(acc, sib, landed, z, y, core, copies, total, make, came)
    moe_ref[...] = total[...].astype(moe_ref.dtype)
    copies.settle()
    assert copies.n == LATE_COPIES, copies.n


LATE_COPIES = FIRST_COPIES + GATHER_COPIES + SECOND_COPIES


def late(terms, tokens, gain, ids, gates, w_gate, w_up, w_down):
    rows, width = tokens.shape
    experts = w_gate.shape[0]
    places = experts * CAP_DEV
    everyone = terms.shape[0]
    vmem = pl.BlockSpec(memory_space=pltpu.VMEM)
    far = pl.BlockSpec(memory_space=pl.ANY)
    return pl.pallas_call(
        late_kernel,
        out_shape=(jax.ShapeDtypeStruct((rows, width), jnp.bfloat16),) * 2,
        in_specs=[far, vmem, vmem, vmem, vmem, far, far, far],
        out_specs=(vmem, vmem),
        scratch_shapes=scatter_scratch(width)
        + [
            pltpu.VMEM((rows, width), jnp.float32),
            pltpu.VMEM((everyone, rows, width), jnp.bfloat16),
            pltpu.VMEM(w_gate.shape, jnp.bfloat16),
            pltpu.VMEM(w_up.shape, jnp.bfloat16),
            pltpu.VMEM(w_down.shape, jnp.bfloat16),
            pltpu.VMEM((everyone, places, width), jnp.bfloat16),
            pltpu.VMEM((4, 4, rows, width), jnp.bfloat16),
            pltpu.VMEM((places, everyone * rows), jnp.bfloat16),
            pltpu.VMEM((everyone * rows, places), jnp.bfloat16),
            pltpu.SemaphoreType.DMA((3 * experts,)),
            pltpu.SemaphoreType.DMA((LATE_COPIES,)),
            pltpu.SemaphoreType.DMA((LATE_COPIES,)),
        ],
        compiler_params=pltpu.CompilerParams(
            collective_id=1, has_side_effects=True, vmem_limit_bytes=VMEM_LIMIT
        ),
    )(terms, tokens, gain.reshape(1, width), ids, gates, w_gate, w_up, w_down)


BLOCK = 512
KEY_BLOCK = 256
TRANSPOSED = (((1,), (1,)), ((), ()))


def heart_kernel(
    lens_s,
    groups_s,
    pages_s,
    lens_ref,
    groups_ref,
    adapters_ref,
    slots_ref,
    q_gain_ref,
    k_gain_ref,
    x_ref,
    factors_ref,
    wkv_ref,
    wq_ref,
    q_up_ref,
    kv_up_ref,
    wo_ref,
    shrink_o_ref,
    expand_ref,
    out_ref,
    pages_ref,
    tab,
    keys,
    values,
    across,
    acc,
):
    step = pl.program_id(0)
    place = lax.axis_index("tensor")
    head = lax.div(place, 8)
    f32, bf16 = jnp.float32, jnp.bfloat16
    requests = lens_ref.shape[1]
    adapters = slots_ref.shape[1]
    depth = wq_ref.shape[1]

    @pl.when(step == 0)
    def _():
        down = lax.broadcasted_iota(jnp.int32, (requests, requests), 0)
        over = lax.broadcasted_iota(jnp.int32, (requests, requests), 1)

        def column(row, number):
            a = lax.broadcasted_iota(jnp.int32, (number, number), 0)
            b = lax.broadcasted_iota(jnp.int32, (number, number), 1)
            return jnp.sum(
                jnp.where(a == b, jnp.broadcast_to(row, (number, number)), 0.0),
                axis=1,
                keepdims=True,
            )

        lens = lens_ref[...].astype(f32)
        groups = groups_ref[...].astype(f32)
        chosen = adapters_ref[...]
        slots = column(slots_ref[...].astype(f32), adapters)
        ends = jnp.sum(jnp.where(down <= over, column(lens, requests), 0.0), axis=0, keepdims=True)
        starts = ends - lens
        same = column(groups, requests) == groups
        firsts = jnp.min(
            jnp.where(same, column(starts, requests), 1e9), axis=0, keepdims=True
        )
        which = lax.broadcasted_iota(jnp.int32, (adapters, requests), 0)
        slot = jnp.sum(jnp.where(which == chosen, slots, 0.0), axis=0, keepdims=True)
        tab[0:1, :] = starts
        tab[1:2, :] = ends
        tab[2:3, :] = firsts
        tab[3:4, :] = slot

    first_row = step * BLOCK
    row = first_row + lax.broadcasted_iota(jnp.int32, (BLOCK, 1), 0)
    row_f = row.astype(f32)
    inside = (row_f >= tab[0:1, :]) & (row_f < tab[1:2, :])
    rope = row_f - jnp.sum(jnp.where(inside, tab[2:3, :], 0.0), axis=1, keepdims=True)
    slot = jnp.sum(jnp.where(inside, tab[3:4, :], 0.0), axis=1, keepdims=True).astype(jnp.int32)

    lane = lax.broadcasted_iota(jnp.int32, (1, depth), 1)
    half = depth // 2
    low = lane < half
    freq = jnp.exp(
        -jnp.where(low, lane, lane - half).astype(f32) * (2.0 * math.log(ROPE_BASE) / depth)
    )
    mixed_trig = jnp.sin(rope * freq + jnp.where(low, 0.5 * math.pi, 0.0))
    other_trig = pltpu.roll(mixed_trig, half, 1)
    cosine = jnp.where(low, mixed_trig, other_trig)
    sine = jnp.where(low, -other_trig, mixed_trig)

    def turn(vector):
        return vector * cosine + pltpu.roll(vector, half, 1) * sine

    def unit(vector, gain_ref):
        return (
            vector
            * lax.rsqrt(jnp.mean(vector * vector, axis=-1, keepdims=True) + NORM_EPS)
            * gain_ref[...].astype(f32)
        )

    total_rank = q_up_ref.shape[0]
    rank = total_rank // adapters
    mine = slot == lax.div(lax.broadcasted_iota(jnp.int32, (1, adapters * rank), 1), rank)
    x = x_ref[...]
    lora = []
    projected = lax.dot_general(x, factors_ref[...], TRANSPOSED, preferred_element_type=f32)
    for part in range(3):
        shrunk = projected[:, part * total_rank : (part + 1) * total_rank]
        placed = jnp.where(mine, shrunk, 0.0).astype(bf16)
        if part == 0:
            up = q_up_ref[...]
        else:
            begin = pl.multiple_of(head * 2 * depth + (part - 1) * depth, depth)
            up = kv_up_ref[:, pl.ds(begin, depth)]
        lora.append(ADAPTER_FACTOR * jnp.dot(placed, up, preferred_element_type=f32))
    query = jnp.dot(x, wq_ref[...], preferred_element_type=f32) + lora[0]
    query = turn(unit(query, q_gain_ref)).astype(bf16)
    kv = lax.dot_general(x, wkv_ref[...], TRANSPOSED, preferred_element_type=f32)
    raw = (kv[:, :depth] + lora[1]).astype(bf16).astype(f32)
    key = turn(unit(raw, k_gain_ref)).astype(bf16)
    value = (kv[:, depth:] + lora[2]).astype(bf16)
    keys[pl.ds(first_row, BLOCK), :] = key
    values[pl.ds(first_row, BLOCK), 0:depth] = value
    values[pl.ds(first_row, BLOCK), depth:] = jnp.broadcast_to(
        jnp.where(lane == 0, 1.0, 0.0), (BLOCK, depth)
    ).astype(bf16)

    columns = pages_ref.shape[1]
    offset = lax.rem(place, 8) * columns
    pick_row = lax.broadcasted_iota(jnp.int32, (columns, 2 * depth), 0) + offset
    pick_lane = lax.broadcasted_iota(jnp.int32, (columns, 2 * depth), 1)
    pick = jnp.where(pick_row == pick_lane, 1.0, 0.0).astype(bf16)
    across[:, pl.ds(pl.multiple_of(first_row, BLOCK), BLOCK)] = lax.dot_general(
        pick, jnp.concatenate([key, value], axis=1), TRANSPOSED, preferred_element_type=f32
    )

    def look(number, carry):
        start, lead, found, before = carry
        group = groups_s[0, number]
        lead = jnp.where(group == before, lead, start)
        found = jnp.where(start <= first_row, lead, found)
        return start + lens_s[0, number], lead, found, group

    zero = jnp.int32(0)
    found = lax.fori_loop(0, requests, look, (zero, zero, zero, jnp.int32(-1)))[2]
    acc[...] = jnp.zeros_like(acc)
    gap = lax.broadcasted_iota(jnp.int32, (BLOCK, KEY_BLOCK), 0) - lax.broadcasted_iota(
        jnp.int32, (BLOCK, KEY_BLOCK), 1
    )
    reach = rope.astype(jnp.int32)
    scale = depth**-0.5

    def over_keys(number, carry):
        begin = pl.multiple_of(number * KEY_BLOCK, KEY_BLOCK)
        scores = lax.dot_general(
            query, keys[pl.ds(begin, KEY_BLOCK), :], TRANSPOSED, preferred_element_type=f32
        )
        behind = gap + (first_row - begin)
        raised = jnp.where((behind >= 0) & (behind <= reach), jnp.exp(scores * scale), 0.0)
        acc[...] += jnp.dot(
            raised.astype(bf16), values[pl.ds(begin, KEY_BLOCK), :], preferred_element_type=f32
        )
        return carry

    lax.fori_loop(
        lax.div(found, KEY_BLOCK), (step + 1) * (BLOCK // KEY_BLOCK), over_keys, jnp.int32(0)
    )
    mixed = (acc[:, :depth] / acc[:, depth : depth + 1]).astype(bf16)
    shrunk = lax.dot_general(mixed, shrink_o_ref[...], TRANSPOSED, preferred_element_type=f32)
    placed = jnp.where(mine, ADAPTER_FACTOR * shrunk, 0.0).astype(bf16)
    width = out_ref.shape[-1]
    for begin in range(0, width, 512):
        term = jnp.dot(mixed, wo_ref[:, begin : begin + 512], preferred_element_type=f32)
        term = term + jnp.dot(
            placed, expand_ref[:, begin : begin + 512], preferred_element_type=f32
        )
        out_ref[:, begin : begin + 512] = term.astype(bf16)

    @pl.when(step == pl.num_programs(0) - 1)
    def _():
        spot_lane = lax.broadcasted_iota(jnp.int32, (columns, PAGE), 1)

        def fill(number, start):
            length = lens_s[0, number]
            for part in range(2):
                begin = start + part * PAGE
                aligned = pl.multiple_of(lax.div(begin, PAGE) * PAGE, PAGE)
                window = across[:, pl.ds(aligned, 2 * PAGE)]
                shift = lax.rem(2 * PAGE - (begin - aligned), 2 * PAGE)
                rolled = pltpu.roll(window, shift, 1)[:, :PAGE]
                kept = jnp.where(spot_lane < length - part * PAGE, rolled, 0.0)
                pages_ref[pages_s[0, number * 2 + part]] = kept.astype(bf16)
            return start + length

        lax.fori_loop(0, requests, fill, zero)


def heart(
    lengths,
    groups,
    adapter_of_request,
    adapter_slot,
    page_table,
    q_gain,
    k_gain,
    x,
    factors,
    wkv,
    query_weight,
    query_up,
    kv_up,
    w_o,
    shrink_o,
    expand_o,
):
    total, width = x.shape
    depth = query_weight.shape[1]
    requests = lengths.shape[1]
    pages = page_table.shape[1]
    columns = 2 * kv_up.shape[1] // 64
    slots = adapter_slot.shape[0]
    smem = pl.BlockSpec(memory_space=pltpu.SMEM)

    def whole(array):
        return pl.BlockSpec(
            array.shape, lambda i: (0,) * array.ndim, pipeline_mode=pl.Buffered(1)
        )

    small = (
        lengths,
        groups,
        adapter_of_request,
        adapter_slot.reshape(1, slots),
        q_gain.reshape(1, depth),
        k_gain.reshape(1, depth),
    )
    tables = (factors, wkv, query_weight, query_up, kv_up, w_o, shrink_o, expand_o)
    return pl.pallas_call(
        heart_kernel,
        grid=(total // BLOCK,),
        out_shape=(
            jax.ShapeDtypeStruct((total, width), jnp.bfloat16),
            jax.ShapeDtypeStruct((pages, columns, PAGE), jnp.bfloat16),
        ),
        in_specs=[smem, smem, smem]
        + [whole(array) for array in small]
        + [pl.BlockSpec((BLOCK, width), lambda i: (i, 0))]
        + [whole(array) for array in tables],
        out_specs=(
            pl.BlockSpec((BLOCK, width), lambda i: (i, 0)),
            pl.BlockSpec((pages, columns, PAGE), lambda i: (0, 0, 0)),
        ),
        scratch_shapes=[
            pltpu.VMEM((8, requests), jnp.float32),
            pltpu.VMEM((total, depth), jnp.bfloat16),
            pltpu.VMEM((total, 2 * depth), jnp.bfloat16),
            pltpu.VMEM((columns, total + 4 * PAGE), jnp.float32),
            pltpu.VMEM((BLOCK, 2 * depth), jnp.float32),
        ],
        compiler_params=pltpu.CompilerParams(vmem_limit_bytes=VMEM_LIMIT),
    )(lengths, groups, page_table, *small, x, *tables)


def local(
    tokens,
    attn_gain,
    moe_gain,
    q_gain,
    k_gain,
    query_weight,
    w_kv,
    w_o,
    w_gate,
    w_up,
    w_down,
    shrink_qkv,
    shrink_o,
    query_up_factors,
    key_value_up_factors,
    expand_o,
    lengths,
    groups,
    adapter_of_request,
    adapter_slot,
    page_table,
    expert_ids,
    expert_gates,
):
    parts = lax.axis_size("tensor")
    place = lax.axis_index("tensor")
    own_rows, width = tokens.shape
    grand_total = own_rows * parts
    adapters, rank, kv_width = key_value_up_factors.shape
    x_rows, factors, wkv_all = enter(
        tokens,
        attn_gain,
        shrink_qkv.reshape(-1, 3, rank, width),
        w_kv.transpose(1, 0, 2),
    )
    head_width = 2 * q_gain.shape[0]
    attn_terms, kv_pages = heart(
        lengths,
        groups,
        adapter_of_request,
        adapter_slot,
        page_table,
        q_gain,
        k_gain,
        x_rows.reshape(grand_total, width),
        factors.reshape(-1, width),
        wkv_all.reshape(head_width, width),
        query_weight,
        query_up_factors.reshape(adapters * rank, -1),
        key_value_up_factors.reshape(adapters * rank, kv_width),
        w_o,
        shrink_o.reshape(adapters * rank, -1),
        expand_o.reshape(adapters * rank, width),
    )
    attn_out, moe_total = late(
        attn_terms.reshape(parts, own_rows, width),
        tokens,
        moe_gain,
        expert_ids.T,
        expert_gates.T,
        w_gate,
        w_up,
        w_down,
    )
    return (attn_out, moe_total, kv_pages)


def solution(mesh):
    placed = (
        P(("dp", "tensor"), None),
        P(),
        P(),
        P(),
        P(),
        P(None, "tensor"),
        P("tensor", None, None),
        P("tensor", None),
        P("tensor", None, None),
        P("tensor", None, None),
        P("tensor", None, None),
        P("dp", None, None),
        P(None, None, "tensor"),
        P(None, None, "tensor"),
        P(),
        P(),
        P("dp", None),
        P("dp", None),
        P("dp", None),
        P(),
        P("dp", None),
        P("dp", None),
        P("dp", None),
    )
    return jax.shard_map(
        local,
        mesh=mesh,
        in_specs=placed,
        out_specs=(P(("dp", "tensor"), None), P(("dp", "tensor"), None), P("dp", "tensor", None)),
        check_vma=False,
    )
```

```python
import functools
import math
import jax, jax.numpy as jnp
from jax import lax
from jax.experimental import pallas as pl
from jax.experimental.pallas import tpu as pltpu
from jax.sharding import PartitionSpec as P

SIDE = 4
HALF = 32

def spot(z, y, core):
    return lax.rem(z, SIDE) * 8 + lax.rem(y, SIDE) * 2 + core

def whereabouts():
    me = lax.axis_index("tensor")
    return me, lax.div(me, 8), lax.rem(lax.div(me, 2), SIDE), lax.rem(me, 2)

def greet(partners):
    barrier = pltpu.get_barrier_semaphore()
    for partner in partners:
        pl.semaphore_signal(barrier, inc=1, device_id={"tensor": partner}, device_id_type=pl.DeviceIdType.MESH)
    pl.semaphore_wait(barrier, len(partners))

class Copies:
    def __init__(self, send, recv):
        self.send, self.recv, self.n, self.all = send, recv, 0, []
    def make(self, src, dst, axis, target):
        k = self.n
        self.n += 1
        copy = pltpu.make_async_remote_copy(src_ref=src, dst_ref=dst, send_sem=self.send.at[k], recv_sem=self.recv.at[k],
            device_id={axis: target}, device_id_type=pl.DeviceIdType.MESH)
        self.all.append(copy)
        return copy
    def go(self, src, dst, axis, target):
        copy = self.make(src, dst, axis, target)
        copy.start()
        return copy
    def settle(self):
        for copy in self.all:
            copy.wait_send()
        self.all = []

EARLY = ((0, 0), (0, 1), (0, 3), (1, 0), (3, 0))
MIDDLE = ((2, 0), (0, 2), (3, 3), (3, 1), (1, 3), (1, 1))
LAST = ((3, 2), (2, 3), (2, 1), (1, 2), (2, 2))
CELLS = EARLY + MIDDLE + LAST


def gather_rows(out, z, y, core, copies, hooks):
    side = spot(z, y, 1 - core)
    shared = {}
    waited = set()

    def ready(cells):
        for i, j in cells:
            for key in ((0, i, j), (1, i, j)):
                if key in shared and key not in waited:
                    waited.add(key)
                    shared[key].wait_recv()

    def hook(name):
        if name in hooks:
            hooks[name](ready)

    def share(block, row, rows, number, u, v):
        piece = out.at[block, pl.ds(row, rows)]
        where = (number, v, u) if number == 0 else (number, u, v)
        shared[where] = copies.go(piece, piece, "tensor", side)

    def send(block, row, rows, target):
        piece = out.at[block, pl.ds(row, rows)]
        return copies.go(piece, piece, "tensor", target)
    class Part: pass
    parts = []
    for number in range(2):
        p = Part()
        p.row = number * HALF
        p.number = number
        if number == 0:
            p.at = lambda u, v: spot(z + v, y + u, core)
        else:
            p.at = lambda u, v: spot(z + u, y + v, core)
        parts.append(p)
    def ring_open(p, along_u, u):
        block = p.at(u, 0)
        up, down = (p.at(1, 0), p.at(3, 0)) if along_u else (p.at(0, 1), p.at(0, 3))
        return [send(block, p.row, HALF, up), send(block, p.row, HALF, down)]
    def ring_pass(p, along_u, u, opened, which):
        opened[which].wait_recv()
        off = 3 if which == 0 else 1
        block = p.at(off, 0) if along_u else p.at(u, off)
        target = (p.at(1, 0), p.at(3, 0))[which] if along_u else (p.at(0, 1), p.at(0, 3))[which]
        fwd = send(block, p.row + which * (HALF // 2), HALF // 2, target)
        share(block, p.row, HALF, p.number, *((off, 0) if along_u else (u, off)))
        return fwd
    me = spot(z, y, core)
    for p in parts:
        p.u = ring_open(p, True, 0)
    for p in parts:
        p.v = {0: ring_open(p, False, 0)}
    share(me, 0, 2 * HALF, 0, 0, 0)
    hook("opened")
    for which in range(2):
        for p in parts:
            p.u.append(ring_pass(p, True, 0, p.u, which))
            off = 3 if which == 0 else 1
            p.v[off] = ring_open(p, False, off)
    for which in range(2):
        for p in parts:
            p.v[0].append(ring_pass(p, False, 0, p.v[0], which))
    hook("early")
    for p in parts:
        p.u[2].wait_recv()
        p.u[3].wait_recv()
        share(p.at(2, 0), p.row, HALF, p.number, 2, 0)
        p.v[2] = ring_open(p, False, 2)
    for off in (3, 1):
        for which in range(2):
            for p in parts:
                p.v[off].append(ring_pass(p, False, off, p.v[off], which))
        for p in parts:
            done = 0 if off == 3 else 3
            p.v[done][2].wait_recv()
            p.v[done][3].wait_recv()
            share(p.at(done, 2), p.row, HALF, p.number, done, 2)
        if off == 3:
            hook("third")
    for which in range(2):
        for p in parts:
            p.v[2].append(ring_pass(p, False, 2, p.v[2], which))
    hook("middle")
    for off in (1, 2):
        for p in parts:
            p.v[off][2].wait_recv()
            p.v[off][3].wait_recv()
            share(p.at(off, 2), p.row, HALF, p.number, off, 2)
    hook("last")
    ready(CELLS)
    assert len(waited) == len(shared)

def add_rows(dst, start, rows, sources):
    for first in range(0, rows, 16):
        total = dst[pl.ds(start + first, 16)].astype(jnp.float32)
        for ref, row in sources:
            total = total + ref[pl.ds(row + first, 16)].astype(jnp.float32)
        dst[pl.ds(start + first, 16)] = total.astype(dst.dtype)

ORDER = (2, 1, 3, 0)
FIRST_COPIES = 32 + 32 + 8
SECOND_COPIES = 16 + 32 + 8


def cell(number, v, u):
    return (v, u) if number == 0 else (u, v)


def scatter_rows(acc, sib, landed, z, y, core, copies, result, ensure, arrived):
    def neighbour(number, along_v, step):
        along_z = (number == 0) == along_v
        return spot(z + step, y, core) if along_z else spot(z, y + step, core)
    def own(number, v, u):
        return acc.at[cell(number, v, u)]
    def pair(number, v, u):
        arrived(number, v, u)
        return (sib.at[cell(number, v, u)], number * HALF)
    def buf(number, u):
        return landed.at[number * 5 + u]
    ring = {}
    def far(number, along_v, u, block):
        row = number * HALF
        b = buf(number, u)
        key = (number, u)
        ring[key] = [
            copies.go(block.at[pl.ds(row, 16)], b.at[pl.ds(0, 16)], "tensor", neighbour(number, along_v, 1)),
            copies.go(block.at[pl.ds(row + 16, 16)], b.at[pl.ds(16, 16)], "tensor", neighbour(number, along_v, 3)),
        ]
    def near(number, along_v, u, block, which):
        row = number * HALF
        b = buf(number, u)
        ring[number, u].append(
            copies.go(block.at[pl.ds(row, HALF)], b.at[pl.ds(32 + 32 * which, HALF)], "tensor",
                      neighbour(number, along_v, (1, 3)[which])))
    ensure([(2, u) for u in ORDER] + [(u, 2) for u in ORDER[1:]])
    for u in ORDER:
        for number in range(2):
            block = own(number, 2, u)
            add_rows(block, number * HALF, HALF, [pair(number, 2, u)])
            far(number, True, u, block)
    ensure([(i, j) for i in ORDER[1:] for j in ORDER[1:]])
    for u in ORDER:
        for number in range(2):
            row = number * HALF
            for which in range(2):
                v = (1, 3)[which]
                block = own(number, v, u)
                other, first = pair(number, v, u)
                ring[number, u][which].wait_recv()
                for part in range(2):
                    sources = [(other, first + 16 * part)]
                    if part == which:
                        sources.append((buf(number, u), 16 * which))
                    add_rows(block, row + 16 * part, 16, sources)
                near(number, True, u, block, which)
    for u in ORDER:
        for number in range(2):
            row = number * HALF
            block = own(number, 0, u)
            source = pair(number, 0, u)
            b = buf(number, u)
            ring[number, u][2].wait_recv()
            ring[number, u][3].wait_recv()
            sources = [source, (b, 32), (b, 64)]
            last = buf(number, 4)
            if u == 2:
                add_rows(block, row, HALF, sources)
                far(number, False, 4, block)
            elif u in (1, 3):
                which = (1, 3).index(u)
                ring[number, 4][which].wait_recv()
                for part in range(2):
                    more = [(ref, r + 16 * part) for ref, r in sources]
                    if part == which:
                        more.append((last, 16 * which))
                    add_rows(block, row + 16 * part, 16, more)
                near(number, False, 4, block, which)
            else:
                ring[number, 4][2].wait_recv()
                ring[number, 4][3].wait_recv()
                for first in range(0, HALF, 16):
                    total = block[pl.ds(row + first, 16)].astype(jnp.float32)
                    for ref, r in sources + [(last, 32), (last, 64)]:
                        total = total + ref[pl.ds(r + first, 16)].astype(jnp.float32)
                    result[pl.ds(row + first, 16)] = total

def terms_from(terms, acc, sib, local, z, y, core, copies):
    side = spot(z, y, 1 - core)
    loads, shared = {}, {}
    for v in ORDER:
        for u in ORDER:
            for number in range(2):
                i, j = cell(number, v, u)
                rows = pl.ds(number * HALF, HALF)
                shared[number, v, u] = copies.go(
                    terms.at[spot(z + i, y + j, 1 - core), rows], sib.at[i, j, rows], "tensor", side
                )
                load = pltpu.make_async_copy(
                    terms.at[spot(z + i, y + j, core), rows],
                    acc.at[i, j, rows],
                    local.at[number * 16 + v * 4 + u],
                )
                load.start()
                loads[number, v, u] = load

    def arrived(number, v, u):
        loads[number, v, u].wait()
        shared[number, v, u].wait_recv()

    return (lambda cells: None), arrived


def scatter_scratch(width):
    return [
        pltpu.VMEM((4, 4, 64, width), jnp.bfloat16),
        pltpu.VMEM((4, 4, 64, width), jnp.bfloat16),
        pltpu.VMEM((10, 96, width), jnp.bfloat16),
        pltpu.SemaphoreType.DMA((32,)),
    ]

def partners(z, y, core):
    return [spot(z, y, 1 - core), spot(z + 1, y, core), spot(z + 3, y, core), spot(z, y + 1, core), spot(z, y + 3, core)]


GATHER_COPIES = 2 * 20 + 31
EXTRA_COPIES = 9 + 11
NORM_EPS = 1e-06
ROPE_BASE = 1000000.0
ADAPTER_FACTOR = 0.5
PAGE = 128
CAP_DEV = 16
VMEM_LIMIT = 62 << 20


def normalize(values, gain):
    return (
        values
        * lax.rsqrt(jnp.mean(values * values, axis=-1, keepdims=True) + NORM_EPS)
        * gain.astype(jnp.float32)
    )


def front_kernel(
    lens_ref,
    groups_ref,
    adapters_ref,
    slots_ref,
    q_gain_ref,
    k_gain_ref,
    gain_ref,
    tokens_ref,
    shrink_ref,
    wkv_ref,
    wq_far,
    q_up_far,
    kv_up_far,
    wo_far,
    shrink_o_far,
    expand_far,
    terms_ref,
    across,
    rows_ref,
    factors_ref,
    wkv_all_ref,
    wkv_held,
    wq_ref,
    q_up_ref,
    kv_up_ref,
    out_table,
    shrink_o_ref,
    tab,
    trig,
    queries,
    keys,
    values,
    acc,
    stage,
    fetch_sem,
    store_sem,
    local,
    send,
    recv,
):
    me, z, y, core = whereabouts()
    group = lax.axis_index("dp")
    up, down = lax.rem(group + 1, SIDE), lax.rem(group + 3, SIDE)
    opposite = lax.rem(group + 2, SIDE)
    copies = Copies(send, recv)
    homes = [
        pltpu.make_async_copy(shrink_ref.at[held], factors_ref.at[:, 4 * group + held], local.at[held])
        for held in range(4)
    ]
    homes.append(pltpu.make_async_copy(wkv_ref.at[z], wkv_all_ref.at[z, y, core], local.at[4]))
    for home in homes:
        home.start()
    depth = wq_ref.shape[1]
    fetches = []
    for number, (far, held) in enumerate(
        (
            (wq_far, wq_ref),
            (q_up_far, q_up_ref),
            (kv_up_far, kv_up_ref),
            (shrink_o_far, shrink_o_ref),
            (wo_far, out_table.at[pl.ds(0, depth)]),
            (expand_far, out_table.at[pl.ds(depth, expand_far.shape[0])]),
        )
    ):
        fetch = pltpu.make_async_copy(far, held, fetch_sem.at[number])
        fetch.start()
        fetches.append(fetch)
    rows_ref[me] = normalize(tokens_ref[...].astype(jnp.float32), gain_ref[...]).astype(
        rows_ref.dtype
    )
    barrier = pltpu.get_barrier_semaphore()
    near = partners(z, y, core) + [spot(z + 2, y, core)]
    for partner in near:
        pl.semaphore_signal(
            barrier, inc=1, device_id={"tensor": partner}, device_id_type=pl.DeviceIdType.MESH
        )
    for partner in (up, down):
        pl.semaphore_signal(
            barrier, inc=1, device_id={"dp": partner}, device_id_type=pl.DeviceIdType.MESH
        )
    pl.semaphore_wait(barrier, len(near) + 2)
    side = spot(z, y, 1 - core)
    state = {}

    def open_extras():
        spread = []
        for step in (1, 3, 2):
            there = lax.rem(z + step, SIDE)
            spread.append(
                copies.go(
                    wkv_ref.at[there], wkv_all_ref.at[z, y, core], "tensor", spot(there, y, core)
                )
            )
        state["spread"] = spread
        state["factors"] = [[], []]
        for held in range(2):
            slot = 2 * core + held
            for which, target in enumerate((up, down)):
                state["factors"][which].append(
                    copies.go(
                        shrink_ref.at[slot], factors_ref.at[:, 4 * group + slot], "dp", target
                    )
                )

    def kv(y_at, first=0, count=4):
        return wkv_all_ref.at[pl.ds(first, count), lax.rem(y_at, SIDE), core]

    def kv_extras(ready):
        for copy in state["spread"]:
            copy.wait_recv()
        homes[4].wait()
        block = kv(y)
        state["kv"] = [
            copies.go(block, block, "tensor", spot(z, y + 1, core)),
            copies.go(block, block, "tensor", spot(z, y + 3, core)),
        ]
        state["shared"] = [copies.go(block, block, "tensor", side)]

    def factor_extras(ready):
        state["far"] = []
        for which, (origin, target) in enumerate(((down, up), (up, down))):
            for copy in state["factors"][which]:
                copy.wait_recv()
            one = factors_ref.at[:, 4 * origin + 2 * core + which]
            state["far"].append(copies.go(one, one, "dp", target))
            both = factors_ref.at[:, pl.ds(4 * origin + 2 * core, 2)]
            state["shared"].append(copies.go(both, both, "tensor", side))
        pass_extras()

    def pass_extras():
        for which, (origin, target) in enumerate(((y + 3, y + 1), (y + 1, y + 3))):
            state["kv"][which].wait_recv()
            piece = kv(origin, 2 * which, 2)
            state["kv"].append(copies.go(piece, piece, "tensor", spot(z, target, core)))
            whole = kv(origin)
            state["shared"].append(copies.go(whole, whole, "tensor", side))

    def close_extras():
        for copy in state["far"]:
            copy.wait_recv()
        both = factors_ref.at[:, pl.ds(4 * opposite + 2 * core, 2)]
        state["shared"].append(copies.go(both, both, "tensor", side))
        state["kv"][2].wait_recv()
        state["kv"][3].wait_recv()
        whole = kv(y + 2)
        state["shared"].append(copies.go(whole, whole, "tensor", side))

    f32, bf16 = jnp.float32, jnp.bfloat16
    head = z
    requests = lens_ref.shape[1]
    adapters = slots_ref.shape[1]
    width = rows_ref.shape[-1]
    total = rows_ref.shape[0] * rows_ref.shape[1]
    half = depth // 2
    lane = lax.broadcasted_iota(jnp.int32, (1, depth), 1)
    low = lane < half
    total_rank = q_up_ref.shape[0]
    rank_lane = lax.div(
        lax.broadcasted_iota(jnp.int32, (1, total_rank), 1), total_rank // adapters
    ).astype(f32)

    def build_tables():
        down_ = lax.broadcasted_iota(jnp.int32, (requests, requests), 0)
        over = lax.broadcasted_iota(jnp.int32, (requests, requests), 1)

        def column(row, number):
            p = lax.broadcasted_iota(jnp.int32, (number, number), 0)
            q = lax.broadcasted_iota(jnp.int32, (number, number), 1)
            return jnp.sum(
                jnp.where(p == q, jnp.broadcast_to(row, (number, number)), 0.0),
                axis=1,
                keepdims=True,
            )

        lens = lens_ref[...].astype(f32)
        groups = groups_ref[...].astype(f32)
        slots = column(slots_ref[...].astype(f32), adapters)
        ends = jnp.sum(jnp.where(down_ <= over, column(lens, requests), 0.0), axis=0, keepdims=True)
        starts = ends - lens
        same = column(groups, requests) == groups
        firsts = jnp.min(jnp.where(same, column(starts, requests), 1e9), axis=0, keepdims=True)
        which = lax.broadcasted_iota(jnp.int32, (adapters, requests), 0)
        slot = jnp.sum(jnp.where(which == adapters_ref[...], slots, 0.0), axis=0, keepdims=True)
        tab[0:1, :] = starts
        tab[1:2, :] = ends
        tab[2:3, :] = firsts
        tab[3:4, :] = slot

    def look_up(row, which):
        row_f = row.astype(f32)
        inside = (row_f >= tab[0:1, :]) & (row_f < tab[1:2, :])
        return jnp.sum(jnp.where(inside, tab[which : which + 1, :], 0.0), axis=1, keepdims=True)

    def natural(first, count):
        return first + lax.broadcasted_iota(jnp.int32, (count, 1), 0)

    def turns(first, count):
        freq = jnp.exp(
            -jnp.where(low, lane, lane - half).astype(f32) * (2.0 * math.log(ROPE_BASE) / depth)
        )

        def some(number, carry):
            begin = pl.multiple_of(first + number * PAGE, PAGE)
            row = natural(begin, PAGE)
            rope = row.astype(f32) - look_up(row, 2)
            trig[pl.ds(begin, PAGE), :] = jnp.sin(
                rope * freq + jnp.where(low, 0.5 * math.pi, 0.0)
            )
            return carry

        lax.fori_loop(0, count // PAGE, some, jnp.int32(0))

    def unit(vector, norm_ref):
        return (
            vector
            * lax.rsqrt(jnp.mean(vector * vector, axis=-1, keepdims=True) + NORM_EPS)
            * norm_ref[...].astype(f32)
        )

    columns = across.shape[0]

    def project(cells):
        pair = 2 * rows_ref.shape[1]
        bases = [
            pl.multiple_of(spot(z + i, y + j, 0) * rows_ref.shape[1], pair) for i, j in cells
        ]
        x = jnp.concatenate(
            [rows_ref[pl.ds(spot(z + i, y + j, 0), 2)].reshape(pair, width) for i, j in cells],
            axis=0,
        )
        slot = jnp.concatenate([look_up(natural(base, pair), 3) for base in bases], axis=0)
        mixed_trig = jnp.concatenate([trig[pl.ds(base, pair), :] for base in bases], axis=0)
        other_trig = pltpu.roll(mixed_trig, half, 1)
        cosine = jnp.where(low, mixed_trig, other_trig)
        sine = jnp.where(low, -other_trig, mixed_trig)

        def turn(vector):
            return vector * cosine + pltpu.roll(vector, half, 1) * sine

        mine = slot == rank_lane
        projected = lax.dot_general(
            x, factors_ref[...].reshape(3 * total_rank, width), TRANSPOSED, preferred_element_type=f32
        )
        lora = []
        for part in range(3):
            shrunk = projected[:, part * total_rank : (part + 1) * total_rank]
            placed = jnp.where(mine, shrunk, 0.0).astype(bf16)
            if part == 0:
                up_table = q_up_ref[...]
            else:
                begin = pl.multiple_of(head * 2 * depth + (part - 1) * depth, depth)
                up_table = kv_up_ref[:, pl.ds(begin, depth)]
            lora.append(
                ADAPTER_FACTOR * jnp.dot(placed, up_table, preferred_element_type=f32)
            )
        query = jnp.dot(x, wq_ref[...], preferred_element_type=f32) + lora[0]
        query = turn(unit(query, q_gain_ref)).astype(bf16)
        both = lax.dot_general(x, wkv_held[...], TRANSPOSED, preferred_element_type=f32)
        raw = (both[:, :depth] + lora[1]).astype(bf16).astype(f32)
        key = turn(unit(raw, k_gain_ref)).astype(bf16)
        value = (both[:, depth:] + lora[2]).astype(bf16)
        offset = lax.rem(me, 8) * columns
        pick_row = lax.broadcasted_iota(jnp.int32, (columns, 2 * depth), 0) + offset
        pick_lane = lax.broadcasted_iota(jnp.int32, (columns, 2 * depth), 1)
        pick = jnp.where(pick_row == pick_lane, 1.0, 0.0).astype(bf16)
        turned = lax.dot_general(
            pick, jnp.concatenate([key, value], axis=1), TRANSPOSED, preferred_element_type=f32
        )
        for number, base in enumerate(bases):
            here = slice(number * pair, (number + 1) * pair)
            queries[pl.ds(base, pair), :] = query[here]
            keys[pl.ds(base, pair), :] = key[here]
            values[pl.ds(base, pair), 0:depth] = value[here]
            across[:, pl.ds(base, pair)] = turned[:, here]

    def opened(ready):
        kv_extras(ready)
        build_tables()
        turns(0, 512)

    def early(ready):
        turns(512, 512)

    def third(ready):
        factor_extras(ready)
        turns(1024, 512)
        turns(1536, 512)
        values[:, depth:] = jnp.broadcast_to(
            jnp.where(lane == 0, 1.0, 0.0), (total, depth)
        ).astype(bf16)
        across[:, total:] = jnp.zeros((columns, across.shape[1] - total), f32)

    def middle(ready):
        close_extras()
        for copy in state["shared"]:
            copy.wait_recv()
        for home in homes[:4]:
            home.wait()
        for fetch in fetches:
            fetch.wait()
        wkv_held[...] = (
            wkv_all_ref[...].astype(f32).reshape(wkv_held.shape).astype(bf16)
        )
        ready(EARLY)
        project(EARLY)

    def last(ready):
        ready(EARLY + MIDDLE)
        project(MIDDLE)

    open_extras()
    gather_rows(
        rows_ref,
        z,
        y,
        core,
        copies,
        {"opened": opened, "early": early, "third": third, "middle": middle, "last": last},
    )
    project(LAST)

    gap = lax.broadcasted_iota(jnp.int32, (BLOCK, KEY_BLOCK), 0) - lax.broadcasted_iota(
        jnp.int32, (BLOCK, KEY_BLOCK), 1
    )
    scale = depth**-0.5

    def store(step):
        return pltpu.make_async_copy(
            stage.at[step],
            terms_ref.at[pl.ds(pl.multiple_of(step * BLOCK, BLOCK), BLOCK)],
            store_sem.at[step],
        )

    def attend(step, carry):
        first_row = pl.multiple_of(step * BLOCK, BLOCK)
        row = natural(first_row, BLOCK)
        reach = (row.astype(f32) - look_up(row, 2)).astype(jnp.int32)
        mine = look_up(row, 3) == rank_lane
        query = queries[pl.ds(first_row, BLOCK), :]
        acc[...] = jnp.zeros_like(acc)

        def over_keys(number, carry):
            begin = pl.multiple_of(number * KEY_BLOCK, KEY_BLOCK)
            scores = lax.dot_general(
                query, keys[pl.ds(begin, KEY_BLOCK), :], TRANSPOSED, preferred_element_type=f32
            )
            behind = gap + (first_row - begin)
            raised = jnp.where((behind >= 0) & (behind <= reach), jnp.exp(scores * scale), 0.0)
            acc[...] += jnp.dot(
                raised.astype(bf16), values[pl.ds(begin, KEY_BLOCK), :], preferred_element_type=f32
            )
            return carry

        lax.fori_loop(0, (step + 1) * (BLOCK // KEY_BLOCK), over_keys, jnp.int32(0))
        mixed = (acc[:, :depth] / acc[:, depth : depth + 1]).astype(bf16)
        shrunk = lax.dot_general(mixed, shrink_o_ref[...], TRANSPOSED, preferred_element_type=f32)
        placed = jnp.where(mine, ADAPTER_FACTOR * shrunk, 0.0).astype(bf16)
        joined = jnp.concatenate([mixed, placed], axis=1)
        for begin in range(0, width, 512):
            stage[step, :, begin : begin + 512] = jnp.dot(
                joined, out_table[:, begin : begin + 512], preferred_element_type=f32
            ).astype(bf16)
        store(step).start()
        return carry

    lax.fori_loop(0, total // BLOCK, attend, jnp.int32(0))
    for step in range(total // BLOCK):
        store(step).wait()
    copies.settle()
    assert copies.n == GATHER_COPIES + EXTRA_COPIES, copies.n


def pages_kernel(lens_s, pages_s, across, pages_ref):
    columns = pages_ref.shape[1]
    spot_lane = lax.broadcasted_iota(jnp.int32, (columns, PAGE), 1)

    def fill(number, start):
        length = lens_s[0, number]
        for part in range(2):
            begin = start + part * PAGE
            aligned = pl.multiple_of(lax.div(begin, PAGE) * PAGE, PAGE)
            window = across[:, pl.ds(aligned, 2 * PAGE)]
            shift = lax.rem(2 * PAGE - (begin - aligned), 2 * PAGE)
            rolled = pltpu.roll(window, shift, 1)[:, :PAGE]
            kept = jnp.where(spot_lane < length - part * PAGE, rolled, 0.0)
            pages_ref[pages_s[0, number * 2 + part]] = kept.astype(jnp.bfloat16)
        return start + length

    lax.fori_loop(0, lens_s.shape[1], fill, jnp.int32(0))


BLOCK = 512
KEY_BLOCK = 256
TRANSPOSED = (((1,), (1,)), ((), ()))


def front(
    lengths,
    groups,
    adapter_of_request,
    adapter_slot,
    page_table,
    q_gain,
    k_gain,
    gain,
    tokens,
    shrink,
    wkv,
    query_weight,
    query_up,
    kv_up,
    w_o,
    shrink_o,
    expand_o,
):
    rows, width = tokens.shape
    total = 32 * rows
    depth = query_weight.shape[1]
    columns = kv_up.shape[1] // 32
    pages = page_table.shape[1]
    count = GATHER_COPIES + EXTRA_COPIES
    vmem = pl.BlockSpec(memory_space=pltpu.VMEM)
    smem = pl.BlockSpec(memory_space=pltpu.SMEM)
    far = pl.BlockSpec(memory_space=pl.ANY)
    bf16, f32 = jnp.bfloat16, jnp.float32
    terms, across = pl.pallas_call(
        front_kernel,
        out_shape=(
            jax.ShapeDtypeStruct((total, width), bf16),
            jax.ShapeDtypeStruct((columns, total + 4 * PAGE), f32),
        ),
        in_specs=[vmem] * 8 + [far] * 8,
        out_specs=(far, vmem),
        scratch_shapes=[
            pltpu.VMEM((32, rows, width), bf16),
            pltpu.VMEM((shrink.shape[1], 4 * shrink.shape[0]) + shrink.shape[2:], bf16),
            pltpu.VMEM((4, 4, 2) + wkv.shape[1:], bf16),
            pltpu.VMEM((2 * depth, width), bf16),
            pltpu.VMEM(query_weight.shape, bf16),
            pltpu.VMEM(query_up.shape, bf16),
            pltpu.VMEM(kv_up.shape, bf16),
            pltpu.VMEM((w_o.shape[0] + expand_o.shape[0], width), bf16),
            pltpu.VMEM(shrink_o.shape, bf16),
            pltpu.VMEM((8, lengths.shape[1]), f32),
            pltpu.VMEM((total, depth), f32),
            pltpu.VMEM((total, depth), bf16),
            pltpu.VMEM((total, depth), bf16),
            pltpu.VMEM((total, 2 * depth), bf16),
            pltpu.VMEM((BLOCK, 2 * depth), f32),
            pltpu.VMEM((total // BLOCK, BLOCK, width), bf16),
            pltpu.SemaphoreType.DMA((6,)),
            pltpu.SemaphoreType.DMA((total // BLOCK,)),
            pltpu.SemaphoreType.DMA((5,)),
            pltpu.SemaphoreType.DMA((count,)),
            pltpu.SemaphoreType.DMA((count,)),
        ],
        compiler_params=pltpu.CompilerParams(
            collective_id=0, has_side_effects=True, vmem_limit_bytes=VMEM_LIMIT
        ),
    )(
        lengths,
        groups,
        adapter_of_request,
        adapter_slot.reshape(1, -1),
        q_gain.reshape(1, depth),
        k_gain.reshape(1, depth),
        gain.reshape(1, width),
        tokens,
        shrink,
        wkv,
        query_weight,
        query_up,
        kv_up,
        w_o,
        shrink_o,
        expand_o,
    )
    kv_pages = pl.pallas_call(
        pages_kernel,
        out_shape=jax.ShapeDtypeStruct((pages, columns, PAGE), bf16),
        in_specs=[smem, smem, vmem],
        out_specs=vmem,
        compiler_params=pltpu.CompilerParams(vmem_limit_bytes=VMEM_LIMIT),
    )(lengths, page_table, across)
    return terms, kv_pages


def late_kernel(
    terms_ref,
    tokens_ref,
    gain_ref,
    ids_ref,
    gates_ref,
    w_gate_ref,
    w_up_ref,
    w_down_ref,
    out_ref,
    moe_ref,
    acc,
    sib,
    landed,
    local,
    total,
    rows,
    gate,
    up,
    down,
    slots,
    stage,
    pick,
    mix,
    weights_sem,
    send,
    recv,
):
    me, z, y, core = whereabouts()
    side = spot(z, y, 1 - core)
    f32, bf16 = jnp.float32, jnp.bfloat16
    experts, hidden_width, width = w_gate_ref.shape
    fetches = []
    for number, (source, held) in enumerate(
        ((w_gate_ref, gate), (w_up_ref, up), (w_down_ref, down))
    ):
        for expert in range(experts):
            fetch = pltpu.make_async_copy(
                source.at[expert], held.at[expert], weights_sem.at[number * experts + expert]
            )
            fetch.start()
            fetches.append(fetch)
    greet(partners(z, y, core))
    copies = Copies(send, recv)
    ensure, arrived = terms_from(terms_ref, acc, sib, local, z, y, core, copies)

    tokens_here = ids_ref.shape[1]
    places = experts * CAP_DEV
    slot = lax.broadcasted_iota(jnp.int32, (places, 1), 0)
    expert_of = me * experts + lax.div(slot, CAP_DEV)
    gates = gates_ref[...]
    gate_sum = jnp.sum(gates, axis=0, keepdims=True)
    hit = jnp.zeros((places, tokens_here), f32)
    weight = jnp.zeros((places, tokens_here), f32)
    for choice in range(ids_ref.shape[0]):
        same = ids_ref[choice : choice + 1, :] == expert_of
        hit = hit + jnp.where(same, 1.0, 0.0)
        weight = weight + jnp.where(same, gates_ref[choice : choice + 1, :], 0.0)
    weight = weight / gate_sum
    chunk = 256
    block = 64
    above = lax.broadcasted_iota(jnp.int32, (chunk, chunk), 0)
    right = lax.broadcasted_iota(jnp.int32, (chunk, chunk), 1)
    within = lax.div(above, block) == lax.div(right, block)
    prefix = jnp.where(within & (above <= right), 1.0, 0.0).astype(bf16)
    same_row = jnp.where(above == right, 1.0, 0.0).astype(bf16)
    number_in_block = (lax.rem(slot, CAP_DEV) + 1).astype(f32)
    for begin in range(0, tokens_here, chunk):
        piece = hit[:, begin : begin + chunk]
        count = jnp.dot(piece.astype(bf16), prefix, preferred_element_type=f32)
        taken = (piece > 0.5) & (count == number_in_block)
        pick[:, begin : begin + chunk] = jnp.where(taken, 1.0, 0.0).astype(bf16)
        shares = jnp.where(taken, weight[:, begin : begin + chunk], 0.0).astype(bf16)
        mix[pl.ds(begin, chunk), :] = lax.dot_general(
            same_row, shares, (((1,), (1,)), ((), ())), preferred_element_type=f32
        ).astype(bf16)

    scatter_rows(acc, sib, landed, z, y, core, copies, total, ensure, arrived)
    summed = total[...]
    out_ref[...] = summed.astype(out_ref.dtype)
    rows[me] = normalize(tokens_ref[...].astype(f32) + summed, gain_ref[...]).astype(rows.dtype)
    pair_rows = 2 * block
    lane_block = lax.div(lax.broadcasted_iota(jnp.int32, (1, pair_rows), 1), block)

    def apply_experts(cells):
        first = CELLS.index(cells[0])
        for number, (i, j) in enumerate(cells):
            index = spot(z + i, y + j, 0)
            piece = pick[:, pl.ds(pl.multiple_of(index * block, pair_rows), pair_rows)]
            spread = jnp.concatenate(
                [jnp.where(lane_block == part, piece, jnp.zeros_like(piece)) for part in range(2)],
                axis=0,
            )
            taken_rows = jnp.dot(
                spread, rows[pl.ds(index, 2)].reshape(pair_rows, width), preferred_element_type=f32
            )
            slots[2 * (first + number) : 2 * (first + number) + 2] = taken_rows.astype(bf16).reshape(
                2, places, width
            )
        blocks = slice(2 * first, 2 * (first + len(cells)))
        count = 2 * len(cells)

        def one_expert(expert, carry):
            here = pl.ds(pl.multiple_of(expert * CAP_DEV, CAP_DEV), CAP_DEV)
            taken_rows = slots[blocks, here, :].reshape(count * CAP_DEV, width)
            gated = lax.dot_general(
                taken_rows, gate[expert], TRANSPOSED, preferred_element_type=f32
            )
            raised = lax.dot_general(taken_rows, up[expert], TRANSPOSED, preferred_element_type=f32)
            hidden = (gated / (1.0 + jnp.exp(-gated)) * raised).astype(bf16)
            for begin in range(0, width, 512):
                piece = jnp.dot(
                    hidden, down[expert, :, begin : begin + 512], preferred_element_type=f32
                ).astype(bf16)
                slots[blocks, here, begin : begin + 512] = piece.reshape(count, CAP_DEV, 512)
            return carry

        lax.fori_loop(0, experts, one_expert, jnp.int32(0))

    def early_experts(ready):
        for fetch in fetches:
            fetch.wait()
        ready(EARLY)
        apply_experts(EARLY)

    def middle_experts(ready):
        ready(EARLY + MIDDLE)
        apply_experts(MIDDLE)

    gather_rows(
        rows, z, y, core, copies, {"early": early_experts, "middle": middle_experts}
    )
    apply_experts(LAST)
    copies.settle()

    shared = {}
    waited = set()

    def combine(i, j, which):
        index = spot(z + i, y + j, which)
        part = mix[pl.ds(pl.multiple_of(index * block, block), block), :]
        held = slots[2 * CELLS.index((i, j)) + which]
        return jnp.dot(part, held, preferred_element_type=f32).astype(bf16)

    def make(cells):
        for i, j in cells:
            if (i, j) in shared:
                continue
            stage[i, j] = combine(i, j, 1 - core)
            shared[i, j] = copies.go(stage.at[i, j], sib.at[i, j], "tensor", side)
            acc[i, j] = combine(i, j, core)

    def came(number, v, u):
        where = cell(number, v, u)
        make([where])
        if where not in waited:
            waited.add(where)
            shared[where].wait_recv()

    scatter_rows(acc, sib, landed, z, y, core, copies, total, make, came)
    moe_ref[...] = total[...].astype(moe_ref.dtype)
    copies.settle()
    assert copies.n == LATE_COPIES, copies.n


LATE_COPIES = FIRST_COPIES + GATHER_COPIES + SECOND_COPIES


def late(terms, tokens, gain, ids, gates, w_gate, w_up, w_down):
    rows, width = tokens.shape
    experts = w_gate.shape[0]
    places = experts * CAP_DEV
    everyone = terms.shape[0]
    vmem = pl.BlockSpec(memory_space=pltpu.VMEM)
    far = pl.BlockSpec(memory_space=pl.ANY)
    return pl.pallas_call(
        late_kernel,
        out_shape=(jax.ShapeDtypeStruct((rows, width), jnp.bfloat16),) * 2,
        in_specs=[far, vmem, vmem, vmem, vmem, far, far, far],
        out_specs=(vmem, vmem),
        scratch_shapes=scatter_scratch(width)
        + [
            pltpu.VMEM((rows, width), jnp.float32),
            pltpu.VMEM((everyone, rows, width), jnp.bfloat16),
            pltpu.VMEM(w_gate.shape, jnp.bfloat16),
            pltpu.VMEM(w_up.shape, jnp.bfloat16),
            pltpu.VMEM(w_down.shape, jnp.bfloat16),
            pltpu.VMEM((everyone, places, width), jnp.bfloat16),
            pltpu.VMEM((4, 4, rows, width), jnp.bfloat16),
            pltpu.VMEM((places, everyone * rows), jnp.bfloat16),
            pltpu.VMEM((everyone * rows, places), jnp.bfloat16),
            pltpu.SemaphoreType.DMA((3 * experts,)),
            pltpu.SemaphoreType.DMA((LATE_COPIES,)),
            pltpu.SemaphoreType.DMA((LATE_COPIES,)),
        ],
        compiler_params=pltpu.CompilerParams(
            collective_id=1, has_side_effects=True, vmem_limit_bytes=VMEM_LIMIT
        ),
    )(terms, tokens, gain.reshape(1, width), ids, gates, w_gate, w_up, w_down)


def local(
    tokens,
    attn_gain,
    moe_gain,
    q_gain,
    k_gain,
    query_weight,
    w_kv,
    w_o,
    w_gate,
    w_up,
    w_down,
    shrink_qkv,
    shrink_o,
    query_up_factors,
    key_value_up_factors,
    expand_o,
    lengths,
    groups,
    adapter_of_request,
    adapter_slot,
    page_table,
    expert_ids,
    expert_gates,
):
    parts = lax.axis_size("tensor")
    place = lax.axis_index("tensor")
    own_rows, width = tokens.shape
    grand_total = own_rows * parts
    adapters, rank, kv_width = key_value_up_factors.shape
    attn_terms, kv_pages = front(
        lengths,
        groups,
        adapter_of_request,
        adapter_slot,
        page_table,
        q_gain,
        k_gain,
        attn_gain,
        tokens,
        shrink_qkv.reshape(-1, 3, rank, width),
        w_kv.transpose(1, 0, 2),
        query_weight,
        query_up_factors.reshape(adapters * rank, -1),
        key_value_up_factors.reshape(adapters * rank, kv_width),
        w_o,
        shrink_o.reshape(adapters * rank, -1),
        expand_o.reshape(adapters * rank, width),
    )
    attn_out, moe_total = late(
        attn_terms.reshape(parts, own_rows, width),
        tokens,
        moe_gain,
        expert_ids.T,
        expert_gates.T,
        w_gate,
        w_up,
        w_down,
    )
    return (attn_out, moe_total, kv_pages)


def solution(mesh):
    placed = (
        P(("dp", "tensor"), None),
        P(),
        P(),
        P(),
        P(),
        P(None, "tensor"),
        P("tensor", None, None),
        P("tensor", None),
        P("tensor", None, None),
        P("tensor", None, None),
        P("tensor", None, None),
        P("dp", None, None),
        P(None, None, "tensor"),
        P(None, None, "tensor"),
        P(),
        P(),
        P("dp", None),
        P("dp", None),
        P("dp", None),
        P(),
        P("dp", None),
        P("dp", None),
        P("dp", None),
    )
    return jax.shard_map(
        local,
        mesh=mesh,
        in_specs=placed,
        out_specs=(P(("dp", "tensor"), None), P(("dp", "tensor"), None), P("dp", "tensor", None)),
        check_vma=False,
    )
```

```python
import functools
import math
import jax, jax.numpy as jnp
from jax import lax
from jax.experimental import pallas as pl
from jax.experimental.pallas import tpu as pltpu
from jax.sharding import PartitionSpec as P

SIDE = 4
HALF = 32

def spot(z, y, core):
    return lax.rem(z, SIDE) * 8 + lax.rem(y, SIDE) * 2 + core

def whereabouts():
    me = lax.axis_index("tensor")
    return me, lax.div(me, 8), lax.rem(lax.div(me, 2), SIDE), lax.rem(me, 2)

def greet(partners):
    barrier = pltpu.get_barrier_semaphore()
    for partner in partners:
        pl.semaphore_signal(barrier, inc=1, device_id={"tensor": partner}, device_id_type=pl.DeviceIdType.MESH)
    pl.semaphore_wait(barrier, len(partners))

class Copies:
    def __init__(self, send, recv):
        self.send, self.recv, self.n, self.all = send, recv, 0, []
    def make(self, src, dst, axis, target):
        k = self.n
        self.n += 1
        copy = pltpu.make_async_remote_copy(src_ref=src, dst_ref=dst, send_sem=self.send.at[k], recv_sem=self.recv.at[k],
            device_id={axis: target}, device_id_type=pl.DeviceIdType.MESH)
        self.all.append(copy)
        return copy
    def go(self, src, dst, axis, target):
        copy = self.make(src, dst, axis, target)
        copy.start()
        return copy
    def settle(self):
        for copy in self.all:
            copy.wait_send()
        self.all = []

EARLY = ((0, 0), (0, 1), (0, 3), (1, 0), (3, 0))
MIDDLE = ((2, 0), (0, 2), (3, 3), (3, 1), (1, 3), (1, 1))
LAST = ((3, 2), (2, 3), (2, 1), (1, 2), (2, 2))
CELLS = EARLY + MIDDLE + LAST
FAR = ((2, 2), (2, 1), (1, 2), (2, 3), (3, 2), (2, 0), (0, 2))
NEAR = ((1, 1), (3, 1), (1, 3), (3, 3))
SLOT_CELLS = EARLY + FAR + NEAR


def gather_rows(out, z, y, core, copies, hooks):
    side = spot(z, y, 1 - core)
    shared = {}
    waited = set()

    def ready(cells):
        for i, j in cells:
            for key in ((0, i, j), (1, i, j)):
                if key in shared and key not in waited:
                    waited.add(key)
                    shared[key].wait_recv()

    def hook(name):
        if name in hooks:
            hooks[name](ready)

    def share(block, row, rows, number, u, v):
        piece = out.at[block, pl.ds(row, rows)]
        where = (number, v, u) if number == 0 else (number, u, v)
        shared[where] = copies.go(piece, piece, "tensor", side)

    def send(block, row, rows, target):
        piece = out.at[block, pl.ds(row, rows)]
        return copies.go(piece, piece, "tensor", target)
    class Part: pass
    parts = []
    for number in range(2):
        p = Part()
        p.row = number * HALF
        p.number = number
        if number == 0:
            p.at = lambda u, v: spot(z + v, y + u, core)
        else:
            p.at = lambda u, v: spot(z + u, y + v, core)
        parts.append(p)
    def ring_open(p, along_u, u):
        block = p.at(u, 0)
        up, down = (p.at(1, 0), p.at(3, 0)) if along_u else (p.at(0, 1), p.at(0, 3))
        return [send(block, p.row, HALF, up), send(block, p.row, HALF, down)]
    def ring_pass(p, along_u, u, opened, which):
        opened[which].wait_recv()
        off = 3 if which == 0 else 1
        block = p.at(off, 0) if along_u else p.at(u, off)
        target = (p.at(1, 0), p.at(3, 0))[which] if along_u else (p.at(0, 1), p.at(0, 3))[which]
        fwd = send(block, p.row + which * (HALF // 2), HALF // 2, target)
        share(block, p.row, HALF, p.number, *((off, 0) if along_u else (u, off)))
        return fwd
    me = spot(z, y, core)
    for p in parts:
        p.u = ring_open(p, True, 0)
    for p in parts:
        p.v = {0: ring_open(p, False, 0)}
    share(me, 0, 2 * HALF, 0, 0, 0)
    hook("opened")
    for which in range(2):
        for p in parts:
            p.u.append(ring_pass(p, True, 0, p.u, which))
            off = 3 if which == 0 else 1
            p.v[off] = ring_open(p, False, off)
    for which in range(2):
        for p in parts:
            p.v[0].append(ring_pass(p, False, 0, p.v[0], which))
    hook("early")
    for p in parts:
        p.u[2].wait_recv()
        p.u[3].wait_recv()
        share(p.at(2, 0), p.row, HALF, p.number, 2, 0)
        p.v[2] = ring_open(p, False, 2)
    hook("wide")
    for off in (3, 1):
        for which in range(2):
            for p in parts:
                p.v[off].append(ring_pass(p, False, off, p.v[off], which))
        for p in parts:
            done = 0 if off == 3 else 3
            p.v[done][2].wait_recv()
            p.v[done][3].wait_recv()
            share(p.at(done, 2), p.row, HALF, p.number, done, 2)
        if off == 3:
            hook("third")
    hook("fourth")
    for which in range(2):
        for p in parts:
            p.v[2].append(ring_pass(p, False, 2, p.v[2], which))
    hook("middle")
    for off in (1, 2):
        for p in parts:
            p.v[off][2].wait_recv()
            p.v[off][3].wait_recv()
            share(p.at(off, 2), p.row, HALF, p.number, off, 2)
    hook("last")
    ready(CELLS)
    assert len(waited) == len(shared)

def add_rows(dst, start, rows, sources):
    for first in range(0, rows, 16):
        total = dst[pl.ds(start + first, 16)].astype(jnp.float32)
        for ref, row in sources:
            total = total + ref[pl.ds(row + first, 16)].astype(jnp.float32)
        dst[pl.ds(start + first, 16)] = total.astype(dst.dtype)

ORDER = (2, 1, 3, 0)
FIRST_COPIES = 32 + 32 + 8
SECOND_COPIES = 16 + 32 + 8


def cell(number, v, u):
    return (v, u) if number == 0 else (u, v)


def scatter_rows(
    acc, sib, landed, z, y, core, copies, result, ensure, arrived, between=lambda: None
):
    def neighbour(number, along_v, step):
        along_z = (number == 0) == along_v
        return spot(z + step, y, core) if along_z else spot(z, y + step, core)
    def own(number, v, u):
        return acc.at[cell(number, v, u)]
    def pair(number, v, u):
        arrived(number, v, u)
        return (sib.at[cell(number, v, u)], number * HALF)
    def buf(number, u):
        return landed.at[number * 5 + u]
    ring = {}
    def far(number, along_v, u, block):
        row = number * HALF
        b = buf(number, u)
        key = (number, u)
        ring[key] = [
            copies.go(block.at[pl.ds(row, 16)], b.at[pl.ds(0, 16)], "tensor", neighbour(number, along_v, 1)),
            copies.go(block.at[pl.ds(row + 16, 16)], b.at[pl.ds(16, 16)], "tensor", neighbour(number, along_v, 3)),
        ]
    def near(number, along_v, u, block, which):
        row = number * HALF
        b = buf(number, u)
        ring[number, u].append(
            copies.go(block.at[pl.ds(row, HALF)], b.at[pl.ds(32 + 32 * which, HALF)], "tensor",
                      neighbour(number, along_v, (1, 3)[which])))
    coming = [(2, 2)] + [where for u in ORDER[1:] for where in ((2, u), (u, 2))]
    ensure(coming[:3])
    for u in ORDER:
        for number in range(2):
            ensure(coming[: 2 * ORDER.index(u) + number + 3])
            block = own(number, 2, u)
            add_rows(block, number * HALF, HALF, [pair(number, 2, u)])
            far(number, True, u, block)
    ensure(coming)
    between()
    coming = [cell(number, v, u) for u in ORDER for number in range(2) for v in (1, 3)]
    for u in ORDER:
        for number in range(2):
            row = number * HALF
            for which in range(2):
                v = (1, 3)[which]
                ensure(coming[: 4 * ORDER.index(u) + 2 * number + which + 4])
                block = own(number, v, u)
                other, first = pair(number, v, u)
                ring[number, u][which].wait_recv()
                for part in range(2):
                    sources = [(other, first + 16 * part)]
                    if part == which:
                        sources.append((buf(number, u), 16 * which))
                    add_rows(block, row + 16 * part, 16, sources)
                near(number, True, u, block, which)
    for u in ORDER:
        for number in range(2):
            row = number * HALF
            block = own(number, 0, u)
            source = pair(number, 0, u)
            b = buf(number, u)
            ring[number, u][2].wait_recv()
            ring[number, u][3].wait_recv()
            sources = [source, (b, 32), (b, 64)]
            last = buf(number, 4)
            if u == 2:
                add_rows(block, row, HALF, sources)
                far(number, False, 4, block)
            elif u in (1, 3):
                which = (1, 3).index(u)
                ring[number, 4][which].wait_recv()
                for part in range(2):
                    more = [(ref, r + 16 * part) for ref, r in sources]
                    if part == which:
                        more.append((last, 16 * which))
                    add_rows(block, row + 16 * part, 16, more)
                near(number, False, 4, block, which)
            else:
                ring[number, 4][2].wait_recv()
                ring[number, 4][3].wait_recv()
                for first in range(0, HALF, 16):
                    total = block[pl.ds(row + first, 16)].astype(jnp.float32)
                    for ref, r in sources + [(last, 32), (last, 64)]:
                        total = total + ref[pl.ds(r + first, 16)].astype(jnp.float32)
                    result[pl.ds(row + first, 16)] = total

def terms_from(terms, acc, sib, local, z, y, core, copies):
    side = spot(z, y, 1 - core)
    loads, shared = {}, {}
    for v in ORDER:
        for u in ORDER:
            for number in range(2):
                i, j = cell(number, v, u)
                rows = pl.ds(number * HALF, HALF)
                shared[number, v, u] = copies.go(
                    terms.at[spot(z + i, y + j, 1 - core), rows], sib.at[i, j, rows], "tensor", side
                )
                load = pltpu.make_async_copy(
                    terms.at[spot(z + i, y + j, core), rows],
                    acc.at[i, j, rows],
                    local.at[number * 16 + v * 4 + u],
                )
                load.start()
                loads[number, v, u] = load

    def arrived(number, v, u):
        loads[number, v, u].wait()
        shared[number, v, u].wait_recv()

    return (lambda cells: None), arrived


def scatter_scratch(width):
    return [
        pltpu.VMEM((4, 4, 64, width), jnp.bfloat16),
        pltpu.VMEM((4, 4, 64, width), jnp.bfloat16),
        pltpu.VMEM((10, 96, width), jnp.bfloat16),
        pltpu.SemaphoreType.DMA((32,)),
    ]

def partners(z, y, core):
    return [spot(z, y, 1 - core), spot(z + 1, y, core), spot(z + 3, y, core), spot(z, y + 1, core), spot(z, y + 3, core)]


GATHER_COPIES = 2 * 20 + 31
EXTRA_COPIES = 9 + 11
NORM_EPS = 1e-06
ROPE_BASE = 1000000.0
ADAPTER_FACTOR = 0.5
PAGE = 128
CAP_DEV = 16
VMEM_LIMIT = 62 << 20


def normalize(values, gain):
    return (
        values
        * lax.rsqrt(jnp.mean(values * values, axis=-1, keepdims=True) + NORM_EPS)
        * gain.astype(jnp.float32)
    )


def front_kernel(
    lens_ref,
    groups_ref,
    adapters_ref,
    slots_ref,
    q_gain_ref,
    k_gain_ref,
    gain_ref,
    tokens_ref,
    shrink_ref,
    wkv_ref,
    wq_far,
    q_up_far,
    kv_up_far,
    wo_far,
    shrink_o_far,
    expand_far,
    terms_ref,
    across,
    rows_ref,
    factors_ref,
    wkv_all_ref,
    wkv_held,
    wq_ref,
    q_up_ref,
    kv_up_ref,
    out_table,
    shrink_o_ref,
    tab,
    trig,
    queries,
    keys,
    values,
    acc,
    stage,
    fetch_sem,
    store_sem,
    local,
    send,
    recv,
):
    me, z, y, core = whereabouts()
    group = lax.axis_index("dp")
    up, down = lax.rem(group + 1, SIDE), lax.rem(group + 3, SIDE)
    opposite = lax.rem(group + 2, SIDE)
    copies = Copies(send, recv)
    homes = [
        pltpu.make_async_copy(shrink_ref.at[held], factors_ref.at[:, 4 * group + held], local.at[held])
        for held in range(4)
    ]
    homes.append(pltpu.make_async_copy(wkv_ref.at[z], wkv_all_ref.at[z, y, core], local.at[4]))
    for home in homes:
        home.start()
    depth = wq_ref.shape[1]
    fetches = []
    for number, (far, held) in enumerate(
        (
            (wq_far, wq_ref),
            (q_up_far, q_up_ref),
            (kv_up_far, kv_up_ref),
            (shrink_o_far, shrink_o_ref),
            (wo_far, out_table.at[pl.ds(0, depth)]),
            (expand_far, out_table.at[pl.ds(depth, expand_far.shape[0])]),
        )
    ):
        fetch = pltpu.make_async_copy(far, held, fetch_sem.at[number])
        fetch.start()
        fetches.append(fetch)
    rows_ref[me] = normalize(tokens_ref[...].astype(jnp.float32), gain_ref[...]).astype(
        rows_ref.dtype
    )
    barrier = pltpu.get_barrier_semaphore()
    near = partners(z, y, core) + [spot(z + 2, y, core)]
    for partner in near:
        pl.semaphore_signal(
            barrier, inc=1, device_id={"tensor": partner}, device_id_type=pl.DeviceIdType.MESH
        )
    for partner in (up, down):
        pl.semaphore_signal(
            barrier, inc=1, device_id={"dp": partner}, device_id_type=pl.DeviceIdType.MESH
        )
    pl.semaphore_wait(barrier, len(near) + 2)
    side = spot(z, y, 1 - core)
    state = {}

    def open_extras():
        spread = []
        for step in (1, 3, 2):
            there = lax.rem(z + step, SIDE)
            spread.append(
                copies.go(
                    wkv_ref.at[there], wkv_all_ref.at[z, y, core], "tensor", spot(there, y, core)
                )
            )
        state["spread"] = spread
        state["factors"] = [[], []]
        for held in range(2):
            slot = 2 * core + held
            for which, target in enumerate((up, down)):
                state["factors"][which].append(
                    copies.go(
                        shrink_ref.at[slot], factors_ref.at[:, 4 * group + slot], "dp", target
                    )
                )

    def kv(y_at, first=0, count=4):
        return wkv_all_ref.at[pl.ds(first, count), lax.rem(y_at, SIDE), core]

    def kv_extras(ready):
        for copy in state["spread"]:
            copy.wait_recv()
        homes[4].wait()
        block = kv(y)
        state["kv"] = [
            copies.go(block, block, "tensor", spot(z, y + 1, core)),
            copies.go(block, block, "tensor", spot(z, y + 3, core)),
        ]
        state["shared"] = [copies.go(block, block, "tensor", side)]

    def factor_extras(ready):
        state["far"] = []
        for which, (origin, target) in enumerate(((down, up), (up, down))):
            for copy in state["factors"][which]:
                copy.wait_recv()
            one = factors_ref.at[:, 4 * origin + 2 * core + which]
            state["far"].append(copies.go(one, one, "dp", target))
            both = factors_ref.at[:, pl.ds(4 * origin + 2 * core, 2)]
            state["shared"].append(copies.go(both, both, "tensor", side))
        pass_extras()

    def pass_extras():
        for which, (origin, target) in enumerate(((y + 3, y + 1), (y + 1, y + 3))):
            state["kv"][which].wait_recv()
            piece = kv(origin, 2 * which, 2)
            state["kv"].append(copies.go(piece, piece, "tensor", spot(z, target, core)))
            whole = kv(origin)
            state["shared"].append(copies.go(whole, whole, "tensor", side))

    def close_extras():
        for copy in state["far"]:
            copy.wait_recv()
        both = factors_ref.at[:, pl.ds(4 * opposite + 2 * core, 2)]
        state["shared"].append(copies.go(both, both, "tensor", side))
        state["kv"][2].wait_recv()
        state["kv"][3].wait_recv()
        whole = kv(y + 2)
        state["shared"].append(copies.go(whole, whole, "tensor", side))

    f32, bf16 = jnp.float32, jnp.bfloat16
    head = z
    requests = lens_ref.shape[1]
    adapters = slots_ref.shape[1]
    width = rows_ref.shape[-1]
    total = rows_ref.shape[0] * rows_ref.shape[1]
    half = depth // 2
    lane = lax.broadcasted_iota(jnp.int32, (1, depth), 1)
    low = lane < half
    total_rank = q_up_ref.shape[0]
    rank_lane = lax.div(
        lax.broadcasted_iota(jnp.int32, (1, total_rank), 1), total_rank // adapters
    ).astype(f32)

    def build_tables():
        down_ = lax.broadcasted_iota(jnp.int32, (requests, requests), 0)
        over = lax.broadcasted_iota(jnp.int32, (requests, requests), 1)

        def column(row, number):
            p = lax.broadcasted_iota(jnp.int32, (number, number), 0)
            q = lax.broadcasted_iota(jnp.int32, (number, number), 1)
            return jnp.sum(
                jnp.where(p == q, jnp.broadcast_to(row, (number, number)), 0.0),
                axis=1,
                keepdims=True,
            )

        lens = lens_ref[...].astype(f32)
        groups = groups_ref[...].astype(f32)
        slots = column(slots_ref[...].astype(f32), adapters)
        ends = jnp.sum(jnp.where(down_ <= over, column(lens, requests), 0.0), axis=0, keepdims=True)
        starts = ends - lens
        same = column(groups, requests) == groups
        firsts = jnp.min(jnp.where(same, column(starts, requests), 1e9), axis=0, keepdims=True)
        which = lax.broadcasted_iota(jnp.int32, (adapters, requests), 0)
        slot = jnp.sum(jnp.where(which == adapters_ref[...], slots, 0.0), axis=0, keepdims=True)
        tab[0:1, :] = starts
        tab[1:2, :] = ends
        tab[2:3, :] = firsts
        tab[3:4, :] = slot

    def look_up(row, which):
        row_f = row.astype(f32)
        inside = (row_f >= tab[0:1, :]) & (row_f < tab[1:2, :])
        return jnp.sum(jnp.where(inside, tab[which : which + 1, :], 0.0), axis=1, keepdims=True)

    def natural(first, count):
        return first + lax.broadcasted_iota(jnp.int32, (count, 1), 0)

    def turns(first, count):
        freq = jnp.exp(
            -jnp.where(low, lane, lane - half).astype(f32) * (2.0 * math.log(ROPE_BASE) / depth)
        )

        def some(number, carry):
            begin = pl.multiple_of(first + number * PAGE, PAGE)
            row = natural(begin, PAGE)
            rope = row.astype(f32) - look_up(row, 2)
            trig[pl.ds(begin, PAGE), :] = jnp.sin(
                rope * freq + jnp.where(low, 0.5 * math.pi, 0.0)
            )
            return carry

        lax.fori_loop(0, count // PAGE, some, jnp.int32(0))

    def unit(vector, norm_ref):
        return (
            vector
            * lax.rsqrt(jnp.mean(vector * vector, axis=-1, keepdims=True) + NORM_EPS)
            * norm_ref[...].astype(f32)
        )

    columns = across.shape[0]

    def project(cells):
        pair = 2 * rows_ref.shape[1]
        bases = [
            pl.multiple_of(spot(z + i, y + j, 0) * rows_ref.shape[1], pair) for i, j in cells
        ]
        x = jnp.concatenate(
            [rows_ref[pl.ds(spot(z + i, y + j, 0), 2)].reshape(pair, width) for i, j in cells],
            axis=0,
        )
        slot = jnp.concatenate([look_up(natural(base, pair), 3) for base in bases], axis=0)
        mixed_trig = jnp.concatenate([trig[pl.ds(base, pair), :] for base in bases], axis=0)
        other_trig = pltpu.roll(mixed_trig, half, 1)
        cosine = jnp.where(low, mixed_trig, other_trig)
        sine = jnp.where(low, -other_trig, mixed_trig)

        def turn(vector):
            return vector * cosine + pltpu.roll(vector, half, 1) * sine

        mine = slot == rank_lane
        projected = lax.dot_general(
            x, factors_ref[...].reshape(3 * total_rank, width), TRANSPOSED, preferred_element_type=f32
        )
        lora = []
        for part in range(3):
            shrunk = projected[:, part * total_rank : (part + 1) * total_rank]
            placed = jnp.where(mine, shrunk, 0.0).astype(bf16)
            if part == 0:
                up_table = q_up_ref[...]
            else:
                begin = pl.multiple_of(head * 2 * depth + (part - 1) * depth, depth)
                up_table = kv_up_ref[:, pl.ds(begin, depth)]
            lora.append(
                ADAPTER_FACTOR * jnp.dot(placed, up_table, preferred_element_type=f32)
            )
        query = jnp.dot(x, wq_ref[...], preferred_element_type=f32) + lora[0]
        query = turn(unit(query, q_gain_ref)).astype(bf16)
        both = lax.dot_general(x, wkv_held[...], TRANSPOSED, preferred_element_type=f32)
        raw = (both[:, :depth] + lora[1]).astype(bf16).astype(f32)
        key = turn(unit(raw, k_gain_ref)).astype(bf16)
        value = (both[:, depth:] + lora[2]).astype(bf16)
        offset = lax.rem(me, 8) * columns
        pick_row = lax.broadcasted_iota(jnp.int32, (columns, 2 * depth), 0) + offset
        pick_lane = lax.broadcasted_iota(jnp.int32, (columns, 2 * depth), 1)
        pick = jnp.where(pick_row == pick_lane, 1.0, 0.0).astype(bf16)
        turned = lax.dot_general(
            pick, jnp.concatenate([key, value], axis=1), TRANSPOSED, preferred_element_type=f32
        )
        for number, base in enumerate(bases):
            here = slice(number * pair, (number + 1) * pair)
            queries[pl.ds(base, pair), :] = query[here]
            keys[pl.ds(base, pair), :] = key[here]
            values[pl.ds(base, pair), 0:depth] = value[here]
            across[:, pl.ds(base, pair)] = turned[:, here]

    def opened(ready):
        kv_extras(ready)
        build_tables()
        turns(0, 512)

    def early(ready):
        turns(512, 512)

    def third(ready):
        factor_extras(ready)
        turns(1024, 512)
        turns(1536, 512)
        values[:, depth:] = jnp.broadcast_to(
            jnp.where(lane == 0, 1.0, 0.0), (total, depth)
        ).astype(bf16)
        across[:, total:] = jnp.zeros((columns, across.shape[1] - total), f32)

    def middle(ready):
        close_extras()
        for copy in state["shared"]:
            copy.wait_recv()
        for home in homes[:4]:
            home.wait()
        for fetch in fetches:
            fetch.wait()
        wkv_held[...] = (
            wkv_all_ref[...].astype(f32).reshape(wkv_held.shape).astype(bf16)
        )
        ready(EARLY)
        project(EARLY)

    def last(ready):
        ready(EARLY + MIDDLE)
        project(MIDDLE)

    open_extras()
    gather_rows(
        rows_ref,
        z,
        y,
        core,
        copies,
        {"opened": opened, "early": early, "third": third, "middle": middle, "last": last},
    )
    project(LAST)

    gap = lax.broadcasted_iota(jnp.int32, (BLOCK, KEY_BLOCK), 0) - lax.broadcasted_iota(
        jnp.int32, (BLOCK, KEY_BLOCK), 1
    )
    scale = depth**-0.5

    def store(step):
        return pltpu.make_async_copy(
            stage.at[step],
            terms_ref.at[pl.ds(pl.multiple_of(step * BLOCK, BLOCK), BLOCK)],
            store_sem.at[step],
        )

    def attend(step, carry):
        first_row = pl.multiple_of(step * BLOCK, BLOCK)
        row = natural(first_row, BLOCK)
        reach = (row.astype(f32) - look_up(row, 2)).astype(jnp.int32)
        mine = look_up(row, 3) == rank_lane
        query = queries[pl.ds(first_row, BLOCK), :]
        acc[...] = jnp.zeros_like(acc)

        def over_keys(number, carry):
            begin = pl.multiple_of(number * KEY_BLOCK, KEY_BLOCK)
            scores = lax.dot_general(
                query, keys[pl.ds(begin, KEY_BLOCK), :], TRANSPOSED, preferred_element_type=f32
            )
            behind = gap + (first_row - begin)
            raised = jnp.where((behind >= 0) & (behind <= reach), jnp.exp(scores * scale), 0.0)
            acc[...] += jnp.dot(
                raised.astype(bf16), values[pl.ds(begin, KEY_BLOCK), :], preferred_element_type=f32
            )
            return carry

        lax.fori_loop(0, (step + 1) * (BLOCK // KEY_BLOCK), over_keys, jnp.int32(0))
        mixed = (acc[:, :depth] / acc[:, depth : depth + 1]).astype(bf16)
        shrunk = lax.dot_general(mixed, shrink_o_ref[...], TRANSPOSED, preferred_element_type=f32)
        placed = jnp.where(mine, ADAPTER_FACTOR * shrunk, 0.0).astype(bf16)
        joined = jnp.concatenate([mixed, placed], axis=1)
        for begin in range(0, width, 512):
            stage[step, :, begin : begin + 512] = jnp.dot(
                joined, out_table[:, begin : begin + 512], preferred_element_type=f32
            ).astype(bf16)
        store(step).start()
        return carry

    lax.fori_loop(0, total // BLOCK, attend, jnp.int32(0))
    for step in range(total // BLOCK):
        store(step).wait()
    copies.settle()
    assert copies.n == GATHER_COPIES + EXTRA_COPIES, copies.n


def final_kernel(lens_s, pages_s, across, attn_ref, moe_ref, attn_out, moe_out, pages_ref):
    attn_out[...] = attn_ref[...]
    moe_out[...] = moe_ref[...]
    columns = pages_ref.shape[1]
    spot_lane = lax.broadcasted_iota(jnp.int32, (columns, PAGE), 1)

    def fill(number, start):
        length = lens_s[0, number]
        for part in range(2):
            begin = start + part * PAGE
            aligned = pl.multiple_of(lax.div(begin, PAGE) * PAGE, PAGE)
            window = across[:, pl.ds(aligned, 2 * PAGE)]
            shift = lax.rem(2 * PAGE - (begin - aligned), 2 * PAGE)
            rolled = pltpu.roll(window, shift, 1)[:, :PAGE]
            kept = jnp.where(spot_lane < length - part * PAGE, rolled, 0.0)
            pages_ref[pages_s[0, number * 2 + part]] = kept.astype(jnp.bfloat16)
        return start + length

    lax.fori_loop(0, lens_s.shape[1], fill, jnp.int32(0))


BLOCK = 512
KEY_BLOCK = 256
TRANSPOSED = (((1,), (1,)), ((), ()))


def front(
    lengths,
    groups,
    adapter_of_request,
    adapter_slot,
    q_gain,
    k_gain,
    gain,
    tokens,
    shrink,
    wkv,
    query_weight,
    query_up,
    kv_up,
    w_o,
    shrink_o,
    expand_o,
):
    rows, width = tokens.shape
    total = 32 * rows
    depth = query_weight.shape[1]
    columns = kv_up.shape[1] // 32
    count = GATHER_COPIES + EXTRA_COPIES
    vmem = pl.BlockSpec(memory_space=pltpu.VMEM)
    far = pl.BlockSpec(memory_space=pl.ANY)
    bf16, f32 = jnp.bfloat16, jnp.float32
    terms, across = pl.pallas_call(
        front_kernel,
        out_shape=(
            jax.ShapeDtypeStruct((total, width), bf16),
            jax.ShapeDtypeStruct((columns, total + 4 * PAGE), f32),
        ),
        in_specs=[vmem] * 8 + [far] * 8,
        out_specs=(far, vmem),
        scratch_shapes=[
            pltpu.VMEM((32, rows, width), bf16),
            pltpu.VMEM((shrink.shape[1], 4 * shrink.shape[0]) + shrink.shape[2:], bf16),
            pltpu.VMEM((4, 4, 2) + wkv.shape[1:], bf16),
            pltpu.VMEM((2 * depth, width), bf16),
            pltpu.VMEM(query_weight.shape, bf16),
            pltpu.VMEM(query_up.shape, bf16),
            pltpu.VMEM(kv_up.shape, bf16),
            pltpu.VMEM((w_o.shape[0] + expand_o.shape[0], width), bf16),
            pltpu.VMEM(shrink_o.shape, bf16),
            pltpu.VMEM((8, lengths.shape[1]), f32),
            pltpu.VMEM((total, depth), f32),
            pltpu.VMEM((total, depth), bf16),
            pltpu.VMEM((total, depth), bf16),
            pltpu.VMEM((total, 2 * depth), bf16),
            pltpu.VMEM((BLOCK, 2 * depth), f32),
            pltpu.VMEM((total // BLOCK, BLOCK, width), bf16),
            pltpu.SemaphoreType.DMA((6,)),
            pltpu.SemaphoreType.DMA((total // BLOCK,)),
            pltpu.SemaphoreType.DMA((5,)),
            pltpu.SemaphoreType.DMA((count,)),
            pltpu.SemaphoreType.DMA((count,)),
        ],
        compiler_params=pltpu.CompilerParams(
            collective_id=0, has_side_effects=True, vmem_limit_bytes=VMEM_LIMIT
        ),
    )(
        lengths,
        groups,
        adapter_of_request,
        adapter_slot.reshape(1, -1),
        q_gain.reshape(1, depth),
        k_gain.reshape(1, depth),
        gain,
        tokens,
        shrink,
        wkv,
        query_weight,
        query_up,
        kv_up,
        w_o,
        shrink_o,
        expand_o,
    )
    return terms, across


def final(lengths, page_table, across, attn, moe):
    pages = page_table.shape[1]
    vmem = pl.BlockSpec(memory_space=pltpu.VMEM)
    smem = pl.BlockSpec(memory_space=pltpu.SMEM)
    return pl.pallas_call(
        final_kernel,
        out_shape=(
            jax.ShapeDtypeStruct(attn.shape, attn.dtype),
            jax.ShapeDtypeStruct(moe.shape, moe.dtype),
            jax.ShapeDtypeStruct((pages, across.shape[0], PAGE), jnp.bfloat16),
        ),
        in_specs=[smem, smem, vmem, vmem, vmem],
        out_specs=(vmem, vmem, vmem),
        compiler_params=pltpu.CompilerParams(vmem_limit_bytes=VMEM_LIMIT),
    )(lengths, page_table, across, attn, moe)


def late_kernel(
    terms_ref,
    tokens_ref,
    gain_ref,
    ids_ref,
    gates_ref,
    w_gate_ref,
    w_up_ref,
    w_down_ref,
    out_ref,
    moe_ref,
    acc,
    sib,
    landed,
    local,
    total,
    rows,
    gate,
    up,
    down,
    slots,
    stage,
    pick,
    mix,
    weights_sem,
    send,
    recv,
):
    me, z, y, core = whereabouts()
    side = spot(z, y, 1 - core)
    f32, bf16 = jnp.float32, jnp.bfloat16
    experts, hidden_width, width = w_gate_ref.shape
    fetches = []
    for number, (source, held) in enumerate(
        ((w_gate_ref, gate), (w_up_ref, up), (w_down_ref, down))
    ):
        for expert in range(experts):
            fetch = pltpu.make_async_copy(
                source.at[expert], held.at[expert], weights_sem.at[number * experts + expert]
            )
            fetch.start()
            fetches.append(fetch)
    greet(partners(z, y, core))
    copies = Copies(send, recv)
    ensure, arrived = terms_from(terms_ref, acc, sib, local, z, y, core, copies)

    tokens_here = ids_ref.shape[1]
    places = experts * CAP_DEV
    slot = lax.broadcasted_iota(jnp.int32, (places, 1), 0)
    expert_of = me * experts + lax.div(slot, CAP_DEV)
    gates = gates_ref[...]
    gate_sum = jnp.sum(gates, axis=0, keepdims=True)
    hit = jnp.zeros((places, tokens_here), f32)
    weight = jnp.zeros((places, tokens_here), f32)
    for choice in range(ids_ref.shape[0]):
        same = ids_ref[choice : choice + 1, :] == expert_of
        hit = hit + jnp.where(same, 1.0, 0.0)
        weight = weight + jnp.where(same, gates_ref[choice : choice + 1, :], 0.0)
    weight = weight / gate_sum
    chunk = 256
    block = 64
    above = lax.broadcasted_iota(jnp.int32, (chunk, chunk), 0)
    right = lax.broadcasted_iota(jnp.int32, (chunk, chunk), 1)
    within = lax.div(above, block) == lax.div(right, block)
    prefix = jnp.where(within & (above <= right), 1.0, 0.0).astype(bf16)
    same_row = jnp.where(above == right, 1.0, 0.0).astype(bf16)
    number_in_block = (lax.rem(slot, CAP_DEV) + 1).astype(f32)
    for begin in range(0, tokens_here, chunk):
        piece = hit[:, begin : begin + chunk]
        count = jnp.dot(piece.astype(bf16), prefix, preferred_element_type=f32)
        taken = (piece > 0.5) & (count == number_in_block)
        pick[:, begin : begin + chunk] = jnp.where(taken, 1.0, 0.0).astype(bf16)
        shares = jnp.where(taken, weight[:, begin : begin + chunk], 0.0).astype(bf16)
        mix[pl.ds(begin, chunk), :] = lax.dot_general(
            same_row, shares, (((1,), (1,)), ((), ())), preferred_element_type=f32
        ).astype(bf16)

    scatter_rows(acc, sib, landed, z, y, core, copies, total, ensure, arrived)
    summed = total[...]
    out_ref[...] = summed.astype(out_ref.dtype)
    rows[me] = normalize(tokens_ref[...].astype(f32) + summed, gain_ref[...]).astype(rows.dtype)
    pair_rows = 2 * block
    lane_block = lax.div(lax.broadcasted_iota(jnp.int32, (1, pair_rows), 1), block)

    def apply_experts(cells):
        first = SLOT_CELLS.index(cells[0])
        for number, (i, j) in enumerate(cells):
            index = spot(z + i, y + j, 0)
            piece = pick[:, pl.ds(pl.multiple_of(index * block, pair_rows), pair_rows)]
            spread = jnp.concatenate(
                [jnp.where(lane_block == part, piece, jnp.zeros_like(piece)) for part in range(2)],
                axis=0,
            )
            taken_rows = jnp.dot(
                spread, rows[pl.ds(index, 2)].reshape(pair_rows, width), preferred_element_type=f32
            )
            slots[2 * (first + number) : 2 * (first + number) + 2] = taken_rows.astype(bf16).reshape(
                2, places, width
            )
        blocks = slice(2 * first, 2 * (first + len(cells)))
        count = 2 * len(cells)

        def one_expert(expert, carry):
            here = pl.ds(pl.multiple_of(expert * CAP_DEV, CAP_DEV), CAP_DEV)
            taken_rows = slots[blocks, here, :].reshape(count * CAP_DEV, width)
            gated = lax.dot_general(
                taken_rows, gate[expert], TRANSPOSED, preferred_element_type=f32
            )
            raised = lax.dot_general(taken_rows, up[expert], TRANSPOSED, preferred_element_type=f32)
            hidden = (gated / (1.0 + jnp.exp(-gated)) * raised).astype(bf16)
            for begin in range(0, width, 512):
                piece = jnp.dot(
                    hidden, down[expert, :, begin : begin + 512], preferred_element_type=f32
                ).astype(bf16)
                slots[blocks, here, begin : begin + 512] = piece.reshape(count, CAP_DEV, 512)
            return carry

        lax.fori_loop(0, experts, one_expert, jnp.int32(0))

    def early_experts(ready):
        for fetch in fetches:
            fetch.wait()
        ready(EARLY)
        apply_experts(EARLY)

    gather_rows(rows, z, y, core, copies, {"wide": early_experts})
    copies.settle()
    apply_experts(FAR)

    shared = {}
    waited = set()

    def combine(i, j, which):
        index = spot(z + i, y + j, which)
        part = mix[pl.ds(pl.multiple_of(index * block, block), block), :]
        held = slots[2 * SLOT_CELLS.index((i, j)) + which]
        return jnp.dot(part, held, preferred_element_type=f32).astype(bf16)

    def make(cells):
        for i, j in cells:
            if (i, j) in shared:
                continue
            stage[i, j] = combine(i, j, 1 - core)
            shared[i, j] = copies.go(stage.at[i, j], sib.at[i, j], "tensor", side)
            acc[i, j] = combine(i, j, core)

    def came(number, v, u):
        where = cell(number, v, u)
        make([where])
        if where not in waited:
            waited.add(where)
            shared[where].wait_recv()

    scatter_rows(acc, sib, landed, z, y, core, copies, total, make, came, lambda: apply_experts(NEAR))
    moe_ref[...] = total[...].astype(moe_ref.dtype)
    copies.settle()
    assert copies.n == LATE_COPIES, copies.n


LATE_COPIES = FIRST_COPIES + GATHER_COPIES + SECOND_COPIES


def late(terms, tokens, gain, ids, gates, w_gate, w_up, w_down):
    rows, width = tokens.shape
    experts = w_gate.shape[0]
    places = experts * CAP_DEV
    everyone = terms.shape[0]
    vmem = pl.BlockSpec(memory_space=pltpu.VMEM)
    far = pl.BlockSpec(memory_space=pl.ANY)
    return pl.pallas_call(
        late_kernel,
        out_shape=(jax.ShapeDtypeStruct((rows, width), jnp.bfloat16),) * 2,
        in_specs=[far, vmem, vmem, vmem, vmem, far, far, far],
        out_specs=(vmem, vmem),
        scratch_shapes=scatter_scratch(width)
        + [
            pltpu.VMEM((rows, width), jnp.float32),
            pltpu.VMEM((everyone, rows, width), jnp.bfloat16),
            pltpu.VMEM(w_gate.shape, jnp.bfloat16),
            pltpu.VMEM(w_up.shape, jnp.bfloat16),
            pltpu.VMEM(w_down.shape, jnp.bfloat16),
            pltpu.VMEM((everyone, places, width), jnp.bfloat16),
            pltpu.VMEM((4, 4, rows, width), jnp.bfloat16),
            pltpu.VMEM((places, everyone * rows), jnp.bfloat16),
            pltpu.VMEM((everyone * rows, places), jnp.bfloat16),
            pltpu.SemaphoreType.DMA((3 * experts,)),
            pltpu.SemaphoreType.DMA((LATE_COPIES,)),
            pltpu.SemaphoreType.DMA((LATE_COPIES,)),
        ],
        compiler_params=pltpu.CompilerParams(
            collective_id=1, has_side_effects=True, vmem_limit_bytes=VMEM_LIMIT
        ),
    )(terms, tokens, gain, ids, gates, w_gate, w_up, w_down)


def local(
    tokens,
    attn_gain,
    moe_gain,
    q_gain,
    k_gain,
    query_weight,
    w_kv,
    w_o,
    w_gate,
    w_up,
    w_down,
    shrink_qkv,
    shrink_o,
    query_up_factors,
    key_value_up_factors,
    expand_o,
    lengths,
    groups,
    adapter_of_request,
    adapter_slot,
    page_table,
    expert_ids,
    expert_gates,
):
    parts = lax.axis_size("tensor")
    place = lax.axis_index("tensor")
    own_rows, width = tokens.shape
    grand_total = own_rows * parts
    adapters, rank, kv_width = key_value_up_factors.shape
    attn_terms, across = front(
        lengths,
        groups,
        adapter_of_request,
        adapter_slot,
        q_gain,
        k_gain,
        attn_gain,
        tokens,
        shrink_qkv.reshape(-1, 3, rank, width),
        w_kv.transpose(1, 0, 2),
        query_weight,
        query_up_factors.reshape(adapters * rank, -1),
        key_value_up_factors.reshape(adapters * rank, kv_width),
        w_o,
        shrink_o.reshape(adapters * rank, -1),
        expand_o.reshape(adapters * rank, width),
    )
    attn, moe = late(
        attn_terms.reshape(parts, own_rows, width),
        tokens,
        moe_gain,
        expert_ids.T,
        expert_gates.T,
        w_gate,
        w_up,
        w_down,
    )
    return tuple(final(lengths, page_table, across, attn, moe))


def solution(mesh):
    placed = (
        P(("dp", "tensor"), None),
        P(),
        P(),
        P(),
        P(),
        P(None, "tensor"),
        P("tensor", None, None),
        P("tensor", None),
        P("tensor", None, None),
        P("tensor", None, None),
        P("tensor", None, None),
        P("dp", None, None),
        P(None, None, "tensor"),
        P(None, None, "tensor"),
        P(),
        P(),
        P("dp", None),
        P("dp", None),
        P("dp", None),
        P(),
        P("dp", None),
        P("dp", None),
        P("dp", None),
    )
    return jax.shard_map(
        local,
        mesh=mesh,
        in_specs=placed,
        out_specs=(P(("dp", "tensor"), None), P(("dp", "tensor"), None), P("dp", "tensor", None)),
        check_vma=False,
    )
```

```python
import functools
import math
import jax, jax.numpy as jnp
from jax import lax
from jax.experimental import pallas as pl
from jax.experimental.pallas import tpu as pltpu
from jax.sharding import PartitionSpec as P

SIDE = 4
HALF = 32

def spot(z, y, core):
    return lax.rem(z, SIDE) * 8 + lax.rem(y, SIDE) * 2 + core

def whereabouts():
    me = lax.axis_index("tensor")
    return me, lax.div(me, 8), lax.rem(lax.div(me, 2), SIDE), lax.rem(me, 2)

def greet(partners):
    barrier = pltpu.get_barrier_semaphore()
    for partner in partners:
        pl.semaphore_signal(barrier, inc=1, device_id={"tensor": partner}, device_id_type=pl.DeviceIdType.MESH)
    pl.semaphore_wait(barrier, len(partners))

class Copies:
    def __init__(self, send, recv):
        self.send, self.recv, self.n, self.all = send, recv, 0, []
    def make(self, src, dst, axis, target):
        k = self.n
        self.n += 1
        copy = pltpu.make_async_remote_copy(src_ref=src, dst_ref=dst, send_sem=self.send.at[k], recv_sem=self.recv.at[k],
            device_id={axis: target}, device_id_type=pl.DeviceIdType.MESH)
        self.all.append(copy)
        return copy
    def go(self, src, dst, axis, target):
        copy = self.make(src, dst, axis, target)
        copy.start()
        return copy
    def settle(self):
        for copy in self.all:
            copy.wait_send()
        self.all = []

EARLY = ((0, 0), (0, 1), (0, 3), (1, 0), (3, 0))
MIDDLE = ((2, 0), (0, 2), (3, 3), (3, 1), (1, 3), (1, 1))
LAST = ((3, 2), (2, 3), (2, 1), (1, 2), (2, 2))
CELLS = EARLY + MIDDLE + LAST


def gather_rows(out, z, y, core, copies, hooks):
    side = spot(z, y, 1 - core)
    shared = {}
    waited = set()

    def ready(cells):
        for i, j in cells:
            for key in ((0, i, j), (1, i, j)):
                if key in shared and key not in waited:
                    waited.add(key)
                    shared[key].wait_recv()

    def hook(name):
        if name in hooks:
            hooks[name](ready)

    def share(block, row, rows, number, u, v):
        piece = out.at[block, pl.ds(row, rows)]
        where = (number, v, u) if number == 0 else (number, u, v)
        shared[where] = copies.go(piece, piece, "tensor", side)

    def send(block, row, rows, target):
        piece = out.at[block, pl.ds(row, rows)]
        return copies.go(piece, piece, "tensor", target)
    class Part: pass
    parts = []
    for number in range(2):
        p = Part()
        p.row = number * HALF
        p.number = number
        if number == 0:
            p.at = lambda u, v: spot(z + v, y + u, core)
        else:
            p.at = lambda u, v: spot(z + u, y + v, core)
        parts.append(p)
    def ring_open(p, along_u, u):
        block = p.at(u, 0)
        up, down = (p.at(1, 0), p.at(3, 0)) if along_u else (p.at(0, 1), p.at(0, 3))
        return [send(block, p.row, HALF, up), send(block, p.row, HALF, down)]
    def ring_pass(p, along_u, u, opened, which):
        opened[which].wait_recv()
        off = 3 if which == 0 else 1
        block = p.at(off, 0) if along_u else p.at(u, off)
        target = (p.at(1, 0), p.at(3, 0))[which] if along_u else (p.at(0, 1), p.at(0, 3))[which]
        fwd = send(block, p.row + which * (HALF // 2), HALF // 2, target)
        share(block, p.row, HALF, p.number, *((off, 0) if along_u else (u, off)))
        return fwd
    me = spot(z, y, core)
    for p in parts:
        p.u = ring_open(p, True, 0)
    for p in parts:
        p.v = {0: ring_open(p, False, 0)}
    share(me, 0, 2 * HALF, 0, 0, 0)
    hook("opened")
    for which in range(2):
        for p in parts:
            p.u.append(ring_pass(p, True, 0, p.u, which))
            off = 3 if which == 0 else 1
            p.v[off] = ring_open(p, False, off)
    for which in range(2):
        for p in parts:
            p.v[0].append(ring_pass(p, False, 0, p.v[0], which))
    hook("early")
    for p in parts:
        p.u[2].wait_recv()
        p.u[3].wait_recv()
        share(p.at(2, 0), p.row, HALF, p.number, 2, 0)
        p.v[2] = ring_open(p, False, 2)
    hook("wide")
    for off in (3, 1):
        for which in range(2):
            for p in parts:
                p.v[off].append(ring_pass(p, False, off, p.v[off], which))
        for p in parts:
            done = 0 if off == 3 else 3
            p.v[done][2].wait_recv()
            p.v[done][3].wait_recv()
            share(p.at(done, 2), p.row, HALF, p.number, done, 2)
        if off == 3:
            hook("third")
    hook("fourth")
    for which in range(2):
        for p in parts:
            p.v[2].append(ring_pass(p, False, 2, p.v[2], which))
    hook("middle")
    for off in (1, 2):
        for p in parts:
            p.v[off][2].wait_recv()
            p.v[off][3].wait_recv()
            share(p.at(off, 2), p.row, HALF, p.number, off, 2)
    hook("last")
    ready(CELLS)
    assert len(waited) == len(shared)

def add_rows(dst, start, rows, sources):
    for first in range(0, rows, 16):
        total = dst[pl.ds(start + first, 16)].astype(jnp.float32)
        for ref, row in sources:
            total = total + ref[pl.ds(row + first, 16)].astype(jnp.float32)
        dst[pl.ds(start + first, 16)] = total.astype(dst.dtype)

ORDER = (2, 1, 3, 0)
FIRST_COPIES = 32 + 32 + 8
SECOND_COPIES = 16 + 32 + 8


def cell(number, v, u):
    return (v, u) if number == 0 else (u, v)


def scatter_rows(
    acc, sib, landed, z, y, core, copies, result, ensure, arrived
):
    def neighbour(number, along_v, step):
        along_z = (number == 0) == along_v
        return spot(z + step, y, core) if along_z else spot(z, y + step, core)
    def own(number, v, u):
        return acc.at[cell(number, v, u)]
    def pair(number, v, u):
        arrived(number, v, u)
        return (sib.at[cell(number, v, u)], number * HALF)
    def buf(number, u):
        return landed.at[number * 5 + u]
    ring = {}
    def far(number, along_v, u, block):
        row = number * HALF
        b = buf(number, u)
        key = (number, u)
        ring[key] = [
            copies.go(block.at[pl.ds(row, 16)], b.at[pl.ds(0, 16)], "tensor", neighbour(number, along_v, 1)),
            copies.go(block.at[pl.ds(row + 16, 16)], b.at[pl.ds(16, 16)], "tensor", neighbour(number, along_v, 3)),
        ]
    def near(number, along_v, u, block, which):
        row = number * HALF
        b = buf(number, u)
        ring[number, u].append(
            copies.go(block.at[pl.ds(row, HALF)], b.at[pl.ds(32 + 32 * which, HALF)], "tensor",
                      neighbour(number, along_v, (1, 3)[which])))
    coming = [(2, 2)] + [where for u in ORDER[1:] for where in ((2, u), (u, 2))]
    ensure(coming[:3])
    for u in ORDER:
        for number in range(2):
            ensure(coming[: 2 * ORDER.index(u) + number + 3])
            block = own(number, 2, u)
            add_rows(block, number * HALF, HALF, [pair(number, 2, u)])
            far(number, True, u, block)
    ensure(coming)
    coming = [cell(number, v, u) for u in ORDER for number in range(2) for v in (1, 3)]
    for u in ORDER:
        for number in range(2):
            row = number * HALF
            for which in range(2):
                v = (1, 3)[which]
                ensure(coming[: 4 * ORDER.index(u) + 2 * number + which + 4])
                block = own(number, v, u)
                other, first = pair(number, v, u)
                ring[number, u][which].wait_recv()
                for part in range(2):
                    sources = [(other, first + 16 * part)]
                    if part == which:
                        sources.append((buf(number, u), 16 * which))
                    add_rows(block, row + 16 * part, 16, sources)
                near(number, True, u, block, which)
    for u in ORDER:
        for number in range(2):
            row = number * HALF
            block = own(number, 0, u)
            source = pair(number, 0, u)
            b = buf(number, u)
            ring[number, u][2].wait_recv()
            ring[number, u][3].wait_recv()
            sources = [source, (b, 32), (b, 64)]
            last = buf(number, 4)
            if u == 2:
                add_rows(block, row, HALF, sources)
                far(number, False, 4, block)
            elif u in (1, 3):
                which = (1, 3).index(u)
                ring[number, 4][which].wait_recv()
                for part in range(2):
                    more = [(ref, r + 16 * part) for ref, r in sources]
                    if part == which:
                        more.append((last, 16 * which))
                    add_rows(block, row + 16 * part, 16, more)
                near(number, False, 4, block, which)
            else:
                ring[number, 4][2].wait_recv()
                ring[number, 4][3].wait_recv()
                for first in range(0, HALF, 16):
                    total = block[pl.ds(row + first, 16)].astype(jnp.float32)
                    for ref, r in sources + [(last, 32), (last, 64)]:
                        total = total + ref[pl.ds(r + first, 16)].astype(jnp.float32)
                    result[pl.ds(row + first, 16)] = total

def terms_from(terms, acc, sib, local, z, y, core, copies):
    side = spot(z, y, 1 - core)
    loads, shared = {}, {}
    for v in ORDER:
        for u in ORDER:
            for number in range(2):
                i, j = cell(number, v, u)
                rows = pl.ds(number * HALF, HALF)
                shared[number, v, u] = copies.go(
                    terms.at[spot(z + i, y + j, 1 - core), rows], sib.at[i, j, rows], "tensor", side
                )
                load = pltpu.make_async_copy(
                    terms.at[spot(z + i, y + j, core), rows],
                    acc.at[i, j, rows],
                    local.at[number * 16 + v * 4 + u],
                )
                load.start()
                loads[number, v, u] = load

    def arrived(number, v, u):
        loads[number, v, u].wait()
        shared[number, v, u].wait_recv()

    return (lambda cells: None), arrived


def scatter_scratch(width):
    return [
        pltpu.VMEM((4, 4, 64, width), jnp.bfloat16),
        pltpu.VMEM((4, 4, 64, width), jnp.bfloat16),
        pltpu.VMEM((10, 96, width), jnp.bfloat16),
        pltpu.SemaphoreType.DMA((32,)),
    ]

def partners(z, y, core):
    return [spot(z, y, 1 - core), spot(z + 1, y, core), spot(z + 3, y, core), spot(z, y + 1, core), spot(z, y + 3, core)]


GATHER_COPIES = 2 * 20 + 31
EXTRA_COPIES = 9 + 11
NORM_EPS = 1e-06
ROPE_BASE = 1000000.0
ADAPTER_FACTOR = 0.5
PAGE = 128
CAP_DEV = 16
VMEM_LIMIT = 62 << 20


def normalize(values, gain):
    return (
        values
        * lax.rsqrt(jnp.mean(values * values, axis=-1, keepdims=True) + NORM_EPS)
        * gain.astype(jnp.float32)
    )


def front_kernel(
    lens_ref,
    groups_ref,
    adapters_ref,
    slots_ref,
    q_gain_ref,
    k_gain_ref,
    gain_ref,
    tokens_ref,
    shrink_ref,
    wkv_ref,
    wq_far,
    q_up_far,
    kv_up_far,
    wo_far,
    shrink_o_far,
    expand_far,
    terms_ref,
    across,
    rows_ref,
    factors_ref,
    wkv_all_ref,
    wkv_held,
    wq_ref,
    q_up_ref,
    kv_up_ref,
    out_table,
    shrink_o_ref,
    tab,
    trig,
    queries,
    keys,
    values,
    acc,
    stage,
    fetch_sem,
    store_sem,
    local,
    send,
    recv,
):
    me, z, y, core = whereabouts()
    group = lax.axis_index("dp")
    up, down = lax.rem(group + 1, SIDE), lax.rem(group + 3, SIDE)
    opposite = lax.rem(group + 2, SIDE)
    copies = Copies(send, recv)
    homes = [
        pltpu.make_async_copy(shrink_ref.at[held], factors_ref.at[:, 4 * group + held], local.at[held])
        for held in range(4)
    ]
    homes.append(pltpu.make_async_copy(wkv_ref.at[z], wkv_all_ref.at[z, y, core], local.at[4]))
    for home in homes:
        home.start()
    depth = wq_ref.shape[1]
    fetches = []
    for number, (far, held) in enumerate(
        (
            (wq_far, wq_ref),
            (q_up_far, q_up_ref),
            (kv_up_far, kv_up_ref),
            (shrink_o_far, shrink_o_ref),
            (wo_far, out_table.at[pl.ds(0, depth)]),
            (expand_far, out_table.at[pl.ds(depth, expand_far.shape[0])]),
        )
    ):
        fetch = pltpu.make_async_copy(far, held, fetch_sem.at[number])
        fetch.start()
        fetches.append(fetch)
    rows_ref[me] = normalize(tokens_ref[...].astype(jnp.float32), gain_ref[...]).astype(
        rows_ref.dtype
    )
    barrier = pltpu.get_barrier_semaphore()
    near = partners(z, y, core) + [spot(z + 2, y, core)]
    for partner in near:
        pl.semaphore_signal(
            barrier, inc=1, device_id={"tensor": partner}, device_id_type=pl.DeviceIdType.MESH
        )
    for partner in (up, down):
        pl.semaphore_signal(
            barrier, inc=1, device_id={"dp": partner}, device_id_type=pl.DeviceIdType.MESH
        )
    pl.semaphore_wait(barrier, len(near) + 2)
    side = spot(z, y, 1 - core)
    state = {}

    def open_extras():
        spread = []
        for step in (1, 3, 2):
            there = lax.rem(z + step, SIDE)
            spread.append(
                copies.go(
                    wkv_ref.at[there], wkv_all_ref.at[z, y, core], "tensor", spot(there, y, core)
                )
            )
        state["spread"] = spread
        state["factors"] = [[], []]
        for held in range(2):
            slot = 2 * core + held
            for which, target in enumerate((up, down)):
                state["factors"][which].append(
                    copies.go(
                        shrink_ref.at[slot], factors_ref.at[:, 4 * group + slot], "dp", target
                    )
                )

    def kv(y_at, first=0, count=4):
        return wkv_all_ref.at[pl.ds(first, count), lax.rem(y_at, SIDE), core]

    def kv_extras(ready):
        for copy in state["spread"]:
            copy.wait_recv()
        homes[4].wait()
        block = kv(y)
        state["kv"] = [
            copies.go(block, block, "tensor", spot(z, y + 1, core)),
            copies.go(block, block, "tensor", spot(z, y + 3, core)),
        ]
        state["shared"] = [copies.go(block, block, "tensor", side)]

    def factor_extras(ready):
        state["far"] = []
        for which, (origin, target) in enumerate(((down, up), (up, down))):
            for copy in state["factors"][which]:
                copy.wait_recv()
            one = factors_ref.at[:, 4 * origin + 2 * core + which]
            state["far"].append(copies.go(one, one, "dp", target))
            both = factors_ref.at[:, pl.ds(4 * origin + 2 * core, 2)]
            state["shared"].append(copies.go(both, both, "tensor", side))
        pass_extras()

    def pass_extras():
        for which, (origin, target) in enumerate(((y + 3, y + 1), (y + 1, y + 3))):
            state["kv"][which].wait_recv()
            piece = kv(origin, 2 * which, 2)
            state["kv"].append(copies.go(piece, piece, "tensor", spot(z, target, core)))
            whole = kv(origin)
            state["shared"].append(copies.go(whole, whole, "tensor", side))

    def close_extras():
        for copy in state["far"]:
            copy.wait_recv()
        both = factors_ref.at[:, pl.ds(4 * opposite + 2 * core, 2)]
        state["shared"].append(copies.go(both, both, "tensor", side))
        state["kv"][2].wait_recv()
        state["kv"][3].wait_recv()
        whole = kv(y + 2)
        state["shared"].append(copies.go(whole, whole, "tensor", side))

    f32, bf16 = jnp.float32, jnp.bfloat16
    head = z
    requests = lens_ref.shape[1]
    adapters = slots_ref.shape[1]
    width = rows_ref.shape[-1]
    total = rows_ref.shape[0] * rows_ref.shape[1]
    half = depth // 2
    lane = lax.broadcasted_iota(jnp.int32, (1, depth), 1)
    low = lane < half
    total_rank = q_up_ref.shape[0]
    rank_lane = lax.div(
        lax.broadcasted_iota(jnp.int32, (1, total_rank), 1), total_rank // adapters
    ).astype(f32)

    def build_tables():
        down_ = lax.broadcasted_iota(jnp.int32, (requests, requests), 0)
        over = lax.broadcasted_iota(jnp.int32, (requests, requests), 1)

        def column(row, number):
            p = lax.broadcasted_iota(jnp.int32, (number, number), 0)
            q = lax.broadcasted_iota(jnp.int32, (number, number), 1)
            return jnp.sum(
                jnp.where(p == q, jnp.broadcast_to(row, (number, number)), 0.0),
                axis=1,
                keepdims=True,
            )

        lens = lens_ref[...].astype(f32)
        groups = groups_ref[...].astype(f32)
        slots = column(slots_ref[...].astype(f32), adapters)
        ends = jnp.sum(jnp.where(down_ <= over, column(lens, requests), 0.0), axis=0, keepdims=True)
        starts = ends - lens
        same = column(groups, requests) == groups
        firsts = jnp.min(jnp.where(same, column(starts, requests), 1e9), axis=0, keepdims=True)
        which = lax.broadcasted_iota(jnp.int32, (adapters, requests), 0)
        slot = jnp.sum(jnp.where(which == adapters_ref[...], slots, 0.0), axis=0, keepdims=True)
        tab[0:1, :] = starts
        tab[1:2, :] = ends
        tab[2:3, :] = firsts
        tab[3:4, :] = slot

    def look_up(row, which):
        row_f = row.astype(f32)
        inside = (row_f >= tab[0:1, :]) & (row_f < tab[1:2, :])
        return jnp.sum(jnp.where(inside, tab[which : which + 1, :], 0.0), axis=1, keepdims=True)

    def natural(first, count):
        return first + lax.broadcasted_iota(jnp.int32, (count, 1), 0)

    def turns(first, count):
        freq = jnp.exp(
            -jnp.where(low, lane, lane - half).astype(f32) * (2.0 * math.log(ROPE_BASE) / depth)
        )

        def some(number, carry):
            begin = pl.multiple_of(first + number * PAGE, PAGE)
            row = natural(begin, PAGE)
            rope = row.astype(f32) - look_up(row, 2)
            trig[pl.ds(begin, PAGE), :] = jnp.sin(
                rope * freq + jnp.where(low, 0.5 * math.pi, 0.0)
            )
            return carry

        lax.fori_loop(0, count // PAGE, some, jnp.int32(0))

    def unit(vector, norm_ref):
        return (
            vector
            * lax.rsqrt(jnp.mean(vector * vector, axis=-1, keepdims=True) + NORM_EPS)
            * norm_ref[...].astype(f32)
        )

    columns = across.shape[0]

    def project(cells):
        pair = 2 * rows_ref.shape[1]
        bases = [
            pl.multiple_of(spot(z + i, y + j, 0) * rows_ref.shape[1], pair) for i, j in cells
        ]
        x = jnp.concatenate(
            [rows_ref[pl.ds(spot(z + i, y + j, 0), 2)].reshape(pair, width) for i, j in cells],
            axis=0,
        )
        slot = jnp.concatenate([look_up(natural(base, pair), 3) for base in bases], axis=0)
        mixed_trig = jnp.concatenate([trig[pl.ds(base, pair), :] for base in bases], axis=0)
        other_trig = pltpu.roll(mixed_trig, half, 1)
        cosine = jnp.where(low, mixed_trig, other_trig)
        sine = jnp.where(low, -other_trig, mixed_trig)

        def turn(vector):
            return vector * cosine + pltpu.roll(vector, half, 1) * sine

        mine = slot == rank_lane
        projected = lax.dot_general(
            x, factors_ref[...].reshape(3 * total_rank, width), TRANSPOSED, preferred_element_type=f32
        )
        lora = []
        for part in range(3):
            shrunk = projected[:, part * total_rank : (part + 1) * total_rank]
            placed = jnp.where(mine, shrunk, 0.0).astype(bf16)
            if part == 0:
                up_table = q_up_ref[...]
            else:
                begin = pl.multiple_of(head * 2 * depth + (part - 1) * depth, depth)
                up_table = kv_up_ref[:, pl.ds(begin, depth)]
            lora.append(
                ADAPTER_FACTOR * jnp.dot(placed, up_table, preferred_element_type=f32)
            )
        query = jnp.dot(x, wq_ref[...], preferred_element_type=f32) + lora[0]
        query = turn(unit(query, q_gain_ref)).astype(bf16)
        both = lax.dot_general(x, wkv_held[...], TRANSPOSED, preferred_element_type=f32)
        raw = (both[:, :depth] + lora[1]).astype(bf16).astype(f32)
        key = turn(unit(raw, k_gain_ref)).astype(bf16)
        value = (both[:, depth:] + lora[2]).astype(bf16)
        offset = lax.rem(me, 8) * columns
        pick_row = lax.broadcasted_iota(jnp.int32, (columns, 2 * depth), 0) + offset
        pick_lane = lax.broadcasted_iota(jnp.int32, (columns, 2 * depth), 1)
        pick = jnp.where(pick_row == pick_lane, 1.0, 0.0).astype(bf16)
        turned = lax.dot_general(
            pick, jnp.concatenate([key, value], axis=1), TRANSPOSED, preferred_element_type=f32
        )
        for number, base in enumerate(bases):
            here = slice(number * pair, (number + 1) * pair)
            queries[pl.ds(base, pair), :] = query[here]
            keys[pl.ds(base, pair), :] = key[here]
            values[pl.ds(base, pair), 0:depth] = value[here]
            across[:, pl.ds(base, pair)] = turned[:, here]

    def opened(ready):
        kv_extras(ready)
        build_tables()
        turns(0, 512)

    def early(ready):
        turns(512, 512)

    def third(ready):
        factor_extras(ready)
        turns(1024, 512)
        turns(1536, 512)
        values[:, depth:] = jnp.broadcast_to(
            jnp.where(lane == 0, 1.0, 0.0), (total, depth)
        ).astype(bf16)
        across[:, total:] = jnp.zeros((columns, across.shape[1] - total), f32)

    def middle(ready):
        close_extras()
        for copy in state["shared"]:
            copy.wait_recv()
        for home in homes[:4]:
            home.wait()
        for fetch in fetches:
            fetch.wait()
        wkv_held[...] = (
            wkv_all_ref[...].astype(f32).reshape(wkv_held.shape).astype(bf16)
        )
        ready(EARLY)
        project(EARLY)

    def last(ready):
        ready(EARLY + MIDDLE)
        project(MIDDLE)

    open_extras()
    gather_rows(
        rows_ref,
        z,
        y,
        core,
        copies,
        {"opened": opened, "early": early, "third": third, "middle": middle, "last": last},
    )
    project(LAST)

    gap = lax.broadcasted_iota(jnp.int32, (BLOCK, KEY_BLOCK), 0) - lax.broadcasted_iota(
        jnp.int32, (BLOCK, KEY_BLOCK), 1
    )
    scale = depth**-0.5

    def store(step):
        return pltpu.make_async_copy(
            stage.at[step],
            terms_ref.at[pl.ds(pl.multiple_of(step * BLOCK, BLOCK), BLOCK)],
            store_sem.at[step],
        )

    def attend(step, carry):
        first_row = pl.multiple_of(step * BLOCK, BLOCK)
        row = natural(first_row, BLOCK)
        reach = (row.astype(f32) - look_up(row, 2)).astype(jnp.int32)
        mine = look_up(row, 3) == rank_lane
        query = queries[pl.ds(first_row, BLOCK), :]
        acc[...] = jnp.zeros_like(acc)

        def over_keys(number, carry):
            begin = pl.multiple_of(number * KEY_BLOCK, KEY_BLOCK)
            scores = lax.dot_general(
                query, keys[pl.ds(begin, KEY_BLOCK), :], TRANSPOSED, preferred_element_type=f32
            )
            behind = gap + (first_row - begin)
            raised = jnp.where((behind >= 0) & (behind <= reach), jnp.exp(scores * scale), 0.0)
            acc[...] += jnp.dot(
                raised.astype(bf16), values[pl.ds(begin, KEY_BLOCK), :], preferred_element_type=f32
            )
            return carry

        lax.fori_loop(0, (step + 1) * (BLOCK // KEY_BLOCK), over_keys, jnp.int32(0))
        mixed = (acc[:, :depth] / acc[:, depth : depth + 1]).astype(bf16)
        shrunk = lax.dot_general(mixed, shrink_o_ref[...], TRANSPOSED, preferred_element_type=f32)
        placed = jnp.where(mine, ADAPTER_FACTOR * shrunk, 0.0).astype(bf16)
        joined = jnp.concatenate([mixed, placed], axis=1)
        for begin in range(0, width, 512):
            stage[step, :, begin : begin + 512] = jnp.dot(
                joined, out_table[:, begin : begin + 512], preferred_element_type=f32
            ).astype(bf16)
        store(step).start()
        return carry

    lax.fori_loop(0, total // BLOCK, attend, jnp.int32(0))
    for step in range(total // BLOCK):
        store(step).wait()
    copies.settle()
    assert copies.n == GATHER_COPIES + EXTRA_COPIES, copies.n


def final_kernel(lens_s, pages_s, across, attn_ref, moe_ref, attn_out, moe_out, pages_ref):
    attn_out[...] = attn_ref[...]
    moe_out[...] = moe_ref[...]
    columns = pages_ref.shape[1]
    spot_lane = lax.broadcasted_iota(jnp.int32, (columns, PAGE), 1)

    def fill(number, start):
        length = lens_s[0, number]
        for part in range(2):
            begin = start + part * PAGE
            aligned = pl.multiple_of(lax.div(begin, PAGE) * PAGE, PAGE)
            window = across[:, pl.ds(aligned, 2 * PAGE)]
            shift = lax.rem(2 * PAGE - (begin - aligned), 2 * PAGE)
            rolled = pltpu.roll(window, shift, 1)[:, :PAGE]
            kept = jnp.where(spot_lane < length - part * PAGE, rolled, 0.0)
            pages_ref[pages_s[0, number * 2 + part]] = kept.astype(jnp.bfloat16)
        return start + length

    lax.fori_loop(0, lens_s.shape[1], fill, jnp.int32(0))


BLOCK = 512
KEY_BLOCK = 512
TRANSPOSED = (((1,), (1,)), ((), ()))


def front(
    lengths,
    groups,
    adapter_of_request,
    adapter_slot,
    q_gain,
    k_gain,
    gain,
    tokens,
    shrink,
    wkv,
    query_weight,
    query_up,
    kv_up,
    w_o,
    shrink_o,
    expand_o,
):
    rows, width = tokens.shape
    total = 32 * rows
    depth = query_weight.shape[1]
    columns = kv_up.shape[1] // 32
    count = GATHER_COPIES + EXTRA_COPIES
    vmem = pl.BlockSpec(memory_space=pltpu.VMEM)
    far = pl.BlockSpec(memory_space=pl.ANY)
    bf16, f32 = jnp.bfloat16, jnp.float32
    terms, across = pl.pallas_call(
        front_kernel,
        out_shape=(
            jax.ShapeDtypeStruct((total, width), bf16),
            jax.ShapeDtypeStruct((columns, total + 4 * PAGE), f32),
        ),
        in_specs=[vmem] * 8 + [far] * 8,
        out_specs=(far, vmem),
        scratch_shapes=[
            pltpu.VMEM((32, rows, width), bf16),
            pltpu.VMEM((shrink.shape[1], 4 * shrink.shape[0]) + shrink.shape[2:], bf16),
            pltpu.VMEM((4, 4, 2) + wkv.shape[1:], bf16),
            pltpu.VMEM((2 * depth, width), bf16),
            pltpu.VMEM(query_weight.shape, bf16),
            pltpu.VMEM(query_up.shape, bf16),
            pltpu.VMEM(kv_up.shape, bf16),
            pltpu.VMEM((w_o.shape[0] + expand_o.shape[0], width), bf16),
            pltpu.VMEM(shrink_o.shape, bf16),
            pltpu.VMEM((8, lengths.shape[1]), f32),
            pltpu.VMEM((total, depth), f32),
            pltpu.VMEM((total, depth), bf16),
            pltpu.VMEM((total, depth), bf16),
            pltpu.VMEM((total, 2 * depth), bf16),
            pltpu.VMEM((BLOCK, 2 * depth), f32),
            pltpu.VMEM((total // BLOCK, BLOCK, width), bf16),
            pltpu.SemaphoreType.DMA((6,)),
            pltpu.SemaphoreType.DMA((total // BLOCK,)),
            pltpu.SemaphoreType.DMA((5,)),
            pltpu.SemaphoreType.DMA((count,)),
            pltpu.SemaphoreType.DMA((count,)),
        ],
        compiler_params=pltpu.CompilerParams(
            collective_id=0, has_side_effects=True, vmem_limit_bytes=VMEM_LIMIT
        ),
    )(
        lengths,
        groups,
        adapter_of_request,
        adapter_slot.reshape(1, -1),
        q_gain.reshape(1, depth),
        k_gain.reshape(1, depth),
        gain,
        tokens,
        shrink,
        wkv,
        query_weight,
        query_up,
        kv_up,
        w_o,
        shrink_o,
        expand_o,
    )
    return terms, across


def final(lengths, page_table, across, attn, moe):
    pages = page_table.shape[1]
    vmem = pl.BlockSpec(memory_space=pltpu.VMEM)
    smem = pl.BlockSpec(memory_space=pltpu.SMEM)
    return pl.pallas_call(
        final_kernel,
        out_shape=(
            jax.ShapeDtypeStruct(attn.shape, attn.dtype),
            jax.ShapeDtypeStruct(moe.shape, moe.dtype),
            jax.ShapeDtypeStruct((pages, across.shape[0], PAGE), jnp.bfloat16),
        ),
        in_specs=[smem, smem, vmem, vmem, vmem],
        out_specs=(vmem, vmem, vmem),
        compiler_params=pltpu.CompilerParams(vmem_limit_bytes=VMEM_LIMIT),
    )(lengths, page_table, across, attn, moe)


def late_kernel(
    terms_ref,
    tokens_ref,
    gain_ref,
    ids_ref,
    gates_ref,
    w_gate_ref,
    w_up_ref,
    w_down_ref,
    out_ref,
    moe_ref,
    acc,
    sib,
    landed,
    local,
    total,
    rows,
    gate,
    up,
    down,
    slots,
    stage,
    pick,
    mix,
    weights_sem,
    send,
    recv,
):
    me, z, y, core = whereabouts()
    side = spot(z, y, 1 - core)
    f32, bf16 = jnp.float32, jnp.bfloat16
    experts, hidden_width, width = w_gate_ref.shape
    fetches = []
    for number, (source, held) in enumerate(
        ((w_gate_ref, gate), (w_up_ref, up), (w_down_ref, down))
    ):
        for expert in range(experts):
            fetch = pltpu.make_async_copy(
                source.at[expert], held.at[expert], weights_sem.at[number * experts + expert]
            )
            fetch.start()
            fetches.append(fetch)
    greet(partners(z, y, core))
    copies = Copies(send, recv)
    ensure, arrived = terms_from(terms_ref, acc, sib, local, z, y, core, copies)

    tokens_here = ids_ref.shape[1]
    places = experts * CAP_DEV
    slot = lax.broadcasted_iota(jnp.int32, (places, 1), 0)
    expert_of = me * experts + lax.div(slot, CAP_DEV)
    gates = gates_ref[...]
    gate_sum = jnp.sum(gates, axis=0, keepdims=True)
    hit = jnp.zeros((places, tokens_here), f32)
    weight = jnp.zeros((places, tokens_here), f32)
    for choice in range(ids_ref.shape[0]):
        same = ids_ref[choice : choice + 1, :] == expert_of
        hit = hit + jnp.where(same, 1.0, 0.0)
        weight = weight + jnp.where(same, gates_ref[choice : choice + 1, :], 0.0)
    weight = weight / gate_sum
    chunk = 256
    block = 64
    above = lax.broadcasted_iota(jnp.int32, (chunk, chunk), 0)
    right = lax.broadcasted_iota(jnp.int32, (chunk, chunk), 1)
    within = lax.div(above, block) == lax.div(right, block)
    prefix = jnp.where(within & (above <= right), 1.0, 0.0).astype(bf16)
    same_row = jnp.where(above == right, 1.0, 0.0).astype(bf16)
    number_in_block = (lax.rem(slot, CAP_DEV) + 1).astype(f32)
    for begin in range(0, tokens_here, chunk):
        piece = hit[:, begin : begin + chunk]
        count = jnp.dot(piece.astype(bf16), prefix, preferred_element_type=f32)
        taken = (piece > 0.5) & (count == number_in_block)
        pick[:, begin : begin + chunk] = jnp.where(taken, 1.0, 0.0).astype(bf16)
        shares = jnp.where(taken, weight[:, begin : begin + chunk], 0.0).astype(bf16)
        mix[pl.ds(begin, chunk), :] = lax.dot_general(
            same_row, shares, (((1,), (1,)), ((), ())), preferred_element_type=f32
        ).astype(bf16)

    scatter_rows(acc, sib, landed, z, y, core, copies, total, ensure, arrived)
    summed = total[...]
    out_ref[...] = summed.astype(out_ref.dtype)
    rows[me] = normalize(tokens_ref[...].astype(f32) + summed, gain_ref[...]).astype(rows.dtype)
    pair_rows = 2 * block
    lane_block = lax.div(lax.broadcasted_iota(jnp.int32, (1, pair_rows), 1), block)

    def apply_experts(cells):
        first = CELLS.index(cells[0])
        for number, (i, j) in enumerate(cells):
            index = spot(z + i, y + j, 0)
            piece = pick[:, pl.ds(pl.multiple_of(index * block, pair_rows), pair_rows)]
            spread = jnp.concatenate(
                [jnp.where(lane_block == part, piece, jnp.zeros_like(piece)) for part in range(2)],
                axis=0,
            )
            taken_rows = jnp.dot(
                spread, rows[pl.ds(index, 2)].reshape(pair_rows, width), preferred_element_type=f32
            )
            slots[2 * (first + number) : 2 * (first + number) + 2] = taken_rows.astype(bf16).reshape(
                2, places, width
            )
        blocks = slice(2 * first, 2 * (first + len(cells)))
        count = 2 * len(cells)

        def one_expert(expert):
            here = slice(expert * CAP_DEV, (expert + 1) * CAP_DEV)
            taken_rows = slots[blocks, here, :].reshape(count * CAP_DEV, width)
            gated = lax.dot_general(
                taken_rows, gate[expert], TRANSPOSED, preferred_element_type=f32
            )
            raised = lax.dot_general(taken_rows, up[expert], TRANSPOSED, preferred_element_type=f32)
            hidden = (gated / (1.0 + jnp.exp(-gated)) * raised).astype(bf16)
            for begin in range(0, width, 512):
                piece = jnp.dot(
                    hidden, down[expert, :, begin : begin + 512], preferred_element_type=f32
                ).astype(bf16)
                slots[blocks, here, begin : begin + 512] = piece.reshape(count, CAP_DEV, 512)

        for expert in range(experts):
            one_expert(expert)

    gather_rows(rows, z, y, core, copies, {})
    copies.settle()
    for fetch in fetches:
        fetch.wait()
    apply_experts(CELLS)

    shared = {}
    waited = set()

    def combine(i, j, which):
        index = spot(z + i, y + j, which)
        part = mix[pl.ds(pl.multiple_of(index * block, block), block), :]
        held = slots[2 * CELLS.index((i, j)) + which]
        return jnp.dot(part, held, preferred_element_type=f32).astype(bf16)

    def make(cells):
        for i, j in cells:
            if (i, j) in shared:
                continue
            stage[i, j] = combine(i, j, 1 - core)
            shared[i, j] = copies.go(stage.at[i, j], sib.at[i, j], "tensor", side)
            acc[i, j] = combine(i, j, core)

    def came(number, v, u):
        where = cell(number, v, u)
        make([where])
        if where not in waited:
            waited.add(where)
            shared[where].wait_recv()

    scatter_rows(acc, sib, landed, z, y, core, copies, total, make, came)
    moe_ref[...] = total[...].astype(moe_ref.dtype)
    copies.settle()
    assert copies.n == LATE_COPIES, copies.n


LATE_COPIES = FIRST_COPIES + GATHER_COPIES + SECOND_COPIES


def late(terms, tokens, gain, ids, gates, w_gate, w_up, w_down):
    rows, width = tokens.shape
    experts = w_gate.shape[0]
    places = experts * CAP_DEV
    everyone = terms.shape[0]
    vmem = pl.BlockSpec(memory_space=pltpu.VMEM)
    far = pl.BlockSpec(memory_space=pl.ANY)
    return pl.pallas_call(
        late_kernel,
        out_shape=(jax.ShapeDtypeStruct((rows, width), jnp.bfloat16),) * 2,
        in_specs=[far, vmem, vmem, vmem, vmem, far, far, far],
        out_specs=(vmem, vmem),
        scratch_shapes=scatter_scratch(width)
        + [
            pltpu.VMEM((rows, width), jnp.float32),
            pltpu.VMEM((everyone, rows, width), jnp.bfloat16),
            pltpu.VMEM(w_gate.shape, jnp.bfloat16),
            pltpu.VMEM(w_up.shape, jnp.bfloat16),
            pltpu.VMEM(w_down.shape, jnp.bfloat16),
            pltpu.VMEM((everyone, places, width), jnp.bfloat16),
            pltpu.VMEM((4, 4, rows, width), jnp.bfloat16),
            pltpu.VMEM((places, everyone * rows), jnp.bfloat16),
            pltpu.VMEM((everyone * rows, places), jnp.bfloat16),
            pltpu.SemaphoreType.DMA((3 * experts,)),
            pltpu.SemaphoreType.DMA((LATE_COPIES,)),
            pltpu.SemaphoreType.DMA((LATE_COPIES,)),
        ],
        compiler_params=pltpu.CompilerParams(
            collective_id=1, has_side_effects=True, vmem_limit_bytes=VMEM_LIMIT
        ),
    )(terms, tokens, gain, ids, gates, w_gate, w_up, w_down)


def local(
    tokens,
    attn_gain,
    moe_gain,
    q_gain,
    k_gain,
    query_weight,
    w_kv,
    w_o,
    w_gate,
    w_up,
    w_down,
    shrink_qkv,
    shrink_o,
    query_up_factors,
    key_value_up_factors,
    expand_o,
    lengths,
    groups,
    adapter_of_request,
    adapter_slot,
    page_table,
    expert_ids,
    expert_gates,
):
    parts = lax.axis_size("tensor")
    place = lax.axis_index("tensor")
    own_rows, width = tokens.shape
    grand_total = own_rows * parts
    adapters, rank, kv_width = key_value_up_factors.shape
    attn_terms, across = front(
        lengths,
        groups,
        adapter_of_request,
        adapter_slot,
        q_gain,
        k_gain,
        attn_gain,
        tokens,
        shrink_qkv.reshape(-1, 3, rank, width),
        w_kv.transpose(1, 0, 2),
        query_weight,
        query_up_factors.reshape(adapters * rank, -1),
        key_value_up_factors.reshape(adapters * rank, kv_width),
        w_o,
        shrink_o.reshape(adapters * rank, -1),
        expand_o.reshape(adapters * rank, width),
    )
    attn, moe = late(
        attn_terms.reshape(parts, own_rows, width),
        tokens,
        moe_gain,
        expert_ids.T,
        expert_gates.T,
        w_gate,
        w_up,
        w_down,
    )
    return tuple(final(lengths, page_table, across, attn, moe))


def solution(mesh):
    placed = (
        P(("dp", "tensor"), None),
        P(),
        P(),
        P(),
        P(),
        P(None, "tensor"),
        P("tensor", None, None),
        P("tensor", None),
        P("tensor", None, None),
        P("tensor", None, None),
        P("tensor", None, None),
        P("dp", None, None),
        P(None, None, "tensor"),
        P(None, None, "tensor"),
        P(),
        P(),
        P("dp", None),
        P("dp", None),
        P("dp", None),
        P(),
        P("dp", None),
        P("dp", None),
        P("dp", None),
    )
    return jax.shard_map(
        local,
        mesh=mesh,
        in_specs=placed,
        out_specs=(P(("dp", "tensor"), None), P(("dp", "tensor"), None), P("dp", "tensor", None)),
        check_vma=False,
    )
```

```python
import functools
import math
import jax, jax.numpy as jnp
from jax import lax
from jax.experimental import pallas as pl
from jax.experimental.pallas import tpu as pltpu
from jax.sharding import PartitionSpec as P

SIDE = 4
HALF = 32

def spot(z, y, core):
    return lax.rem(z, SIDE) * 8 + lax.rem(y, SIDE) * 2 + core

def whereabouts():
    me = lax.axis_index("tensor")
    return me, lax.div(me, 8), lax.rem(lax.div(me, 2), SIDE), lax.rem(me, 2)

def greet(partners):
    barrier = pltpu.get_barrier_semaphore()
    for partner in partners:
        pl.semaphore_signal(barrier, inc=1, device_id={"tensor": partner}, device_id_type=pl.DeviceIdType.MESH)
    pl.semaphore_wait(barrier, len(partners))

class Copies:
    def __init__(self, send, recv):
        self.send, self.recv, self.n, self.all = send, recv, 0, []
    def make(self, src, dst, axis, target):
        k = self.n
        self.n += 1
        copy = pltpu.make_async_remote_copy(src_ref=src, dst_ref=dst, send_sem=self.send.at[k], recv_sem=self.recv.at[k],
            device_id={axis: target}, device_id_type=pl.DeviceIdType.MESH)
        self.all.append(copy)
        return copy
    def go(self, src, dst, axis, target):
        copy = self.make(src, dst, axis, target)
        copy.start()
        return copy
    def settle(self):
        for copy in self.all:
            copy.wait_send()
        self.all = []

EARLY = ((0, 0), (0, 1), (0, 3), (1, 0), (3, 0))
MIDDLE = ((2, 0), (0, 2), (3, 3), (3, 1), (1, 3), (1, 1))
LAST = ((3, 2), (2, 3), (2, 1), (1, 2), (2, 2))
CELLS = EARLY + MIDDLE + LAST


def gather_rows(out, z, y, core, copies, hooks):
    side = spot(z, y, 1 - core)
    shared = {}
    waited = set()

    def ready(cells):
        for i, j in cells:
            for key in ((0, i, j), (1, i, j)):
                if key in shared and key not in waited:
                    waited.add(key)
                    shared[key].wait_recv()

    def hook(name):
        if name in hooks:
            hooks[name](ready)

    def share(block, row, rows, number, u, v):
        piece = out.at[block, pl.ds(row, rows)]
        where = (number, v, u) if number == 0 else (number, u, v)
        shared[where] = copies.go(piece, piece, "tensor", side)

    def send(block, row, rows, target):
        piece = out.at[block, pl.ds(row, rows)]
        return copies.go(piece, piece, "tensor", target)
    class Part: pass
    parts = []
    for number in range(2):
        p = Part()
        p.row = number * HALF
        p.number = number
        if number == 0:
            p.at = lambda u, v: spot(z + v, y + u, core)
        else:
            p.at = lambda u, v: spot(z + u, y + v, core)
        parts.append(p)
    def ring_open(p, along_u, u):
        block = p.at(u, 0)
        up, down = (p.at(1, 0), p.at(3, 0)) if along_u else (p.at(0, 1), p.at(0, 3))
        return [send(block, p.row, HALF, up), send(block, p.row, HALF, down)]
    def ring_pass(p, along_u, u, opened, which):
        opened[which].wait_recv()
        off = 3 if which == 0 else 1
        block = p.at(off, 0) if along_u else p.at(u, off)
        target = (p.at(1, 0), p.at(3, 0))[which] if along_u else (p.at(0, 1), p.at(0, 3))[which]
        fwd = send(block, p.row + which * (HALF // 2), HALF // 2, target)
        share(block, p.row, HALF, p.number, *((off, 0) if along_u else (u, off)))
        return fwd
    me = spot(z, y, core)
    for p in parts:
        p.u = ring_open(p, True, 0)
    for p in parts:
        p.v = {0: ring_open(p, False, 0)}
    share(me, 0, 2 * HALF, 0, 0, 0)
    hook("opened")
    for which in range(2):
        for p in parts:
            p.u.append(ring_pass(p, True, 0, p.u, which))
            off = 3 if which == 0 else 1
            p.v[off] = ring_open(p, False, off)
    for which in range(2):
        for p in parts:
            p.v[0].append(ring_pass(p, False, 0, p.v[0], which))
    hook("early")
    for p in parts:
        p.u[2].wait_recv()
        p.u[3].wait_recv()
        share(p.at(2, 0), p.row, HALF, p.number, 2, 0)
        p.v[2] = ring_open(p, False, 2)
    hook("wide")
    for off in (3, 1):
        for which in range(2):
            for p in parts:
                p.v[off].append(ring_pass(p, False, off, p.v[off], which))
        for p in parts:
            done = 0 if off == 3 else 3
            p.v[done][2].wait_recv()
            p.v[done][3].wait_recv()
            share(p.at(done, 2), p.row, HALF, p.number, done, 2)
        if off == 3:
            hook("third")
    hook("fourth")
    for which in range(2):
        for p in parts:
            p.v[2].append(ring_pass(p, False, 2, p.v[2], which))
    hook("middle")
    for off in (1, 2):
        for p in parts:
            p.v[off][2].wait_recv()
            p.v[off][3].wait_recv()
            share(p.at(off, 2), p.row, HALF, p.number, off, 2)
    hook("last")
    ready(CELLS)
    assert len(waited) == len(shared)

def add_rows(dst, start, rows, sources):
    for first in range(0, rows, 16):
        total = dst[pl.ds(start + first, 16)].astype(jnp.float32)
        for ref, row in sources:
            total = total + ref[pl.ds(row + first, 16)].astype(jnp.float32)
        dst[pl.ds(start + first, 16)] = total.astype(dst.dtype)

ORDER = (2, 1, 3, 0)
FIRST_COPIES = 32 + 32 + 8
SECOND_COPIES = 16 + 32 + 8


def cell(number, v, u):
    return (v, u) if number == 0 else (u, v)


def scatter_rows(
    acc, sib, landed, z, y, core, copies, result, ensure, arrived
):
    def neighbour(number, along_v, step):
        along_z = (number == 0) == along_v
        return spot(z + step, y, core) if along_z else spot(z, y + step, core)
    def own(number, v, u):
        return acc.at[cell(number, v, u)]
    def pair(number, v, u):
        arrived(number, v, u)
        return (sib.at[cell(number, v, u)], number * HALF)
    def buf(number, u):
        return landed.at[number * 5 + u]
    ring = {}
    def far(number, along_v, u, block):
        row = number * HALF
        b = buf(number, u)
        key = (number, u)
        ring[key] = [
            copies.go(block.at[pl.ds(row, 16)], b.at[pl.ds(0, 16)], "tensor", neighbour(number, along_v, 1)),
            copies.go(block.at[pl.ds(row + 16, 16)], b.at[pl.ds(16, 16)], "tensor", neighbour(number, along_v, 3)),
        ]
    def near(number, along_v, u, block, which):
        row = number * HALF
        b = buf(number, u)
        ring[number, u].append(
            copies.go(block.at[pl.ds(row, HALF)], b.at[pl.ds(32 + 32 * which, HALF)], "tensor",
                      neighbour(number, along_v, (1, 3)[which])))
    coming = [(2, 2)] + [where for u in ORDER[1:] for where in ((2, u), (u, 2))]
    ensure(coming[:5])
    for u in ORDER:
        for number in range(2):
            ensure(coming[: 2 * ORDER.index(u) + number + 5])
            block = own(number, 2, u)
            add_rows(block, number * HALF, HALF, [pair(number, 2, u)])
            far(number, True, u, block)
    ensure(coming)
    coming = [cell(number, v, u) for u in ORDER for number in range(2) for v in (1, 3)]
    for u in ORDER:
        for number in range(2):
            row = number * HALF
            for which in range(2):
                v = (1, 3)[which]
                ensure(coming[: 4 * ORDER.index(u) + 2 * number + which + 4])
                block = own(number, v, u)
                other, first = pair(number, v, u)
                ring[number, u][which].wait_recv()
                for part in range(2):
                    sources = [(other, first + 16 * part)]
                    if part == which:
                        sources.append((buf(number, u), 16 * which))
                    add_rows(block, row + 16 * part, 16, sources)
                near(number, True, u, block, which)
    for u in ORDER:
        for number in range(2):
            row = number * HALF
            block = own(number, 0, u)
            source = pair(number, 0, u)
            b = buf(number, u)
            ring[number, u][2].wait_recv()
            ring[number, u][3].wait_recv()
            sources = [source, (b, 32), (b, 64)]
            last = buf(number, 4)
            if u == 2:
                add_rows(block, row, HALF, sources)
                far(number, False, 4, block)
            elif u in (1, 3):
                which = (1, 3).index(u)
                ring[number, 4][which].wait_recv()
                for part in range(2):
                    more = [(ref, r + 16 * part) for ref, r in sources]
                    if part == which:
                        more.append((last, 16 * which))
                    add_rows(block, row + 16 * part, 16, more)
                near(number, False, 4, block, which)
            else:
                ring[number, 4][2].wait_recv()
                ring[number, 4][3].wait_recv()
                for first in range(0, HALF, 16):
                    total = block[pl.ds(row + first, 16)].astype(jnp.float32)
                    for ref, r in sources + [(last, 32), (last, 64)]:
                        total = total + ref[pl.ds(r + first, 16)].astype(jnp.float32)
                    result[pl.ds(row + first, 16)] = total

def terms_from(terms, acc, sib, local, z, y, core, copies):
    side = spot(z, y, 1 - core)
    loads, shared = {}, {}
    for v in ORDER:
        for u in ORDER:
            for number in range(2):
                i, j = cell(number, v, u)
                rows = pl.ds(number * HALF, HALF)
                shared[number, v, u] = copies.go(
                    terms.at[spot(z + i, y + j, 1 - core), rows], sib.at[i, j, rows], "tensor", side
                )
                load = pltpu.make_async_copy(
                    terms.at[spot(z + i, y + j, core), rows],
                    acc.at[i, j, rows],
                    local.at[number * 16 + v * 4 + u],
                )
                load.start()
                loads[number, v, u] = load

    def arrived(number, v, u):
        loads[number, v, u].wait()
        shared[number, v, u].wait_recv()

    return (lambda cells: None), arrived


def scatter_scratch(width):
    return [
        pltpu.VMEM((4, 4, 64, width), jnp.bfloat16),
        pltpu.VMEM((4, 4, 64, width), jnp.bfloat16),
        pltpu.VMEM((10, 96, width), jnp.bfloat16),
        pltpu.SemaphoreType.DMA((32,)),
    ]

def partners(z, y, core):
    return [spot(z, y, 1 - core), spot(z + 1, y, core), spot(z + 3, y, core), spot(z, y + 1, core), spot(z, y + 3, core)]


GATHER_COPIES = 2 * 20 + 31
EXTRA_COPIES = 9 + 11
NORM_EPS = 1e-06
ROPE_BASE = 1000000.0
ADAPTER_FACTOR = 0.5
PAGE = 128
CAP_DEV = 16
VMEM_LIMIT = 62 << 20


def normalize(values, gain):
    return (
        values
        * lax.rsqrt(jnp.mean(values * values, axis=-1, keepdims=True) + NORM_EPS)
        * gain.astype(jnp.float32)
    )


def front_kernel(
    lens_ref,
    groups_ref,
    adapters_ref,
    slots_ref,
    q_gain_ref,
    k_gain_ref,
    gain_ref,
    tokens_ref,
    shrink_ref,
    wkv_ref,
    wq_far,
    q_up_far,
    kv_up_far,
    wo_far,
    shrink_o_far,
    expand_far,
    terms_ref,
    across,
    rows_ref,
    factors_ref,
    wkv_all_ref,
    wkv_held,
    wq_ref,
    q_up_ref,
    kv_up_ref,
    out_table,
    shrink_o_ref,
    tab,
    trig,
    queries,
    keys,
    values,
    acc,
    stage,
    fetch_sem,
    store_sem,
    local,
    send,
    recv,
):
    me, z, y, core = whereabouts()
    group = lax.axis_index("dp")
    up, down = lax.rem(group + 1, SIDE), lax.rem(group + 3, SIDE)
    opposite = lax.rem(group + 2, SIDE)
    copies = Copies(send, recv)
    homes = [
        pltpu.make_async_copy(shrink_ref.at[held], factors_ref.at[:, 4 * group + held], local.at[held])
        for held in range(4)
    ]
    homes.append(pltpu.make_async_copy(wkv_ref.at[z], wkv_all_ref.at[z, y, core], local.at[4]))
    for home in homes:
        home.start()
    depth = wq_ref.shape[1]
    fetches = []
    for number, (far, held) in enumerate(
        (
            (wq_far, wq_ref),
            (q_up_far, q_up_ref),
            (kv_up_far, kv_up_ref),
            (shrink_o_far, shrink_o_ref),
            (wo_far, out_table.at[pl.ds(0, depth)]),
            (expand_far, out_table.at[pl.ds(depth, expand_far.shape[0])]),
        )
    ):
        fetch = pltpu.make_async_copy(far, held, fetch_sem.at[number])
        fetch.start()
        fetches.append(fetch)
    rows_ref[me] = normalize(tokens_ref[...].astype(jnp.float32), gain_ref[...]).astype(
        rows_ref.dtype
    )
    barrier = pltpu.get_barrier_semaphore()
    near = partners(z, y, core) + [spot(z + 2, y, core)]
    for partner in near:
        pl.semaphore_signal(
            barrier, inc=1, device_id={"tensor": partner}, device_id_type=pl.DeviceIdType.MESH
        )
    for partner in (up, down):
        pl.semaphore_signal(
            barrier, inc=1, device_id={"dp": partner}, device_id_type=pl.DeviceIdType.MESH
        )
    pl.semaphore_wait(barrier, len(near) + 2)
    side = spot(z, y, 1 - core)
    state = {}

    def open_extras():
        spread = []
        for step in (1, 3, 2):
            there = lax.rem(z + step, SIDE)
            spread.append(
                copies.go(
                    wkv_ref.at[there], wkv_all_ref.at[z, y, core], "tensor", spot(there, y, core)
                )
            )
        state["spread"] = spread
        state["factors"] = [[], []]
        for held in range(2):
            slot = 2 * core + held
            for which, target in enumerate((up, down)):
                state["factors"][which].append(
                    copies.go(
                        shrink_ref.at[slot], factors_ref.at[:, 4 * group + slot], "dp", target
                    )
                )

    def kv(y_at, first=0, count=4):
        return wkv_all_ref.at[pl.ds(first, count), lax.rem(y_at, SIDE), core]

    def kv_extras(ready):
        for copy in state["spread"]:
            copy.wait_recv()
        homes[4].wait()
        block = kv(y)
        state["kv"] = [
            copies.go(block, block, "tensor", spot(z, y + 1, core)),
            copies.go(block, block, "tensor", spot(z, y + 3, core)),
        ]
        state["shared"] = [copies.go(block, block, "tensor", side)]

    def factor_extras(ready):
        state["far"] = []
        for which, (origin, target) in enumerate(((down, up), (up, down))):
            for copy in state["factors"][which]:
                copy.wait_recv()
            one = factors_ref.at[:, 4 * origin + 2 * core + which]
            state["far"].append(copies.go(one, one, "dp", target))
            both = factors_ref.at[:, pl.ds(4 * origin + 2 * core, 2)]
            state["shared"].append(copies.go(both, both, "tensor", side))
        pass_extras()

    def pass_extras():
        for which, (origin, target) in enumerate(((y + 3, y + 1), (y + 1, y + 3))):
            state["kv"][which].wait_recv()
            piece = kv(origin, 2 * which, 2)
            state["kv"].append(copies.go(piece, piece, "tensor", spot(z, target, core)))
            whole = kv(origin)
            state["shared"].append(copies.go(whole, whole, "tensor", side))

    def close_extras():
        for copy in state["far"]:
            copy.wait_recv()
        both = factors_ref.at[:, pl.ds(4 * opposite + 2 * core, 2)]
        state["shared"].append(copies.go(both, both, "tensor", side))
        state["kv"][2].wait_recv()
        state["kv"][3].wait_recv()
        whole = kv(y + 2)
        state["shared"].append(copies.go(whole, whole, "tensor", side))

    f32, bf16 = jnp.float32, jnp.bfloat16
    head = z
    requests = lens_ref.shape[1]
    adapters = slots_ref.shape[1]
    width = rows_ref.shape[-1]
    total = rows_ref.shape[0] * rows_ref.shape[1]
    half = depth // 2
    lane = lax.broadcasted_iota(jnp.int32, (1, depth), 1)
    low = lane < half
    total_rank = q_up_ref.shape[0]
    rank_lane = lax.div(
        lax.broadcasted_iota(jnp.int32, (1, total_rank), 1), total_rank // adapters
    ).astype(f32)

    def build_tables():
        down_ = lax.broadcasted_iota(jnp.int32, (requests, requests), 0)
        over = lax.broadcasted_iota(jnp.int32, (requests, requests), 1)

        def column(row, number):
            p = lax.broadcasted_iota(jnp.int32, (number, number), 0)
            q = lax.broadcasted_iota(jnp.int32, (number, number), 1)
            return jnp.sum(
                jnp.where(p == q, jnp.broadcast_to(row, (number, number)), 0.0),
                axis=1,
                keepdims=True,
            )

        lens = lens_ref[...].astype(f32)
        groups = groups_ref[...].astype(f32)
        slots = column(slots_ref[...].astype(f32), adapters)
        ends = jnp.sum(jnp.where(down_ <= over, column(lens, requests), 0.0), axis=0, keepdims=True)
        starts = ends - lens
        same = column(groups, requests) == groups
        firsts = jnp.min(jnp.where(same, column(starts, requests), 1e9), axis=0, keepdims=True)
        which = lax.broadcasted_iota(jnp.int32, (adapters, requests), 0)
        slot = jnp.sum(jnp.where(which == adapters_ref[...], slots, 0.0), axis=0, keepdims=True)
        tab[0:1, :] = starts
        tab[1:2, :] = ends
        tab[2:3, :] = firsts
        tab[3:4, :] = slot

    def look_up(row, which):
        row_f = row.astype(f32)
        inside = (row_f >= tab[0:1, :]) & (row_f < tab[1:2, :])
        return jnp.sum(jnp.where(inside, tab[which : which + 1, :], 0.0), axis=1, keepdims=True)

    def natural(first, count):
        return first + lax.broadcasted_iota(jnp.int32, (count, 1), 0)

    def turns(first, count):
        freq = jnp.exp(
            -jnp.where(low, lane, lane - half).astype(f32) * (2.0 * math.log(ROPE_BASE) / depth)
        )

        def some(number, carry):
            begin = pl.multiple_of(first + number * PAGE, PAGE)
            row = natural(begin, PAGE)
            rope = row.astype(f32) - look_up(row, 2)
            trig[pl.ds(begin, PAGE), :] = jnp.sin(
                rope * freq + jnp.where(low, 0.5 * math.pi, 0.0)
            )
            return carry

        lax.fori_loop(0, count // PAGE, some, jnp.int32(0))

    def unit(vector, norm_ref):
        return (
            vector
            * lax.rsqrt(jnp.mean(vector * vector, axis=-1, keepdims=True) + NORM_EPS)
            * norm_ref[...].astype(f32)
        )

    columns = across.shape[0]

    def project(cells):
        pair = 2 * rows_ref.shape[1]
        bases = [
            pl.multiple_of(spot(z + i, y + j, 0) * rows_ref.shape[1], pair) for i, j in cells
        ]
        x = jnp.concatenate(
            [rows_ref[pl.ds(spot(z + i, y + j, 0), 2)].reshape(pair, width) for i, j in cells],
            axis=0,
        )
        slot = jnp.concatenate([look_up(natural(base, pair), 3) for base in bases], axis=0)
        mixed_trig = jnp.concatenate([trig[pl.ds(base, pair), :] for base in bases], axis=0)
        other_trig = pltpu.roll(mixed_trig, half, 1)
        cosine = jnp.where(low, mixed_trig, other_trig)
        sine = jnp.where(low, -other_trig, mixed_trig)

        def turn(vector):
            return vector * cosine + pltpu.roll(vector, half, 1) * sine

        mine = slot == rank_lane
        projected = lax.dot_general(
            x, factors_ref[...].reshape(3 * total_rank, width), TRANSPOSED, preferred_element_type=f32
        )
        lora = []
        for part in range(3):
            shrunk = projected[:, part * total_rank : (part + 1) * total_rank]
            placed = jnp.where(mine, shrunk, 0.0).astype(bf16)
            if part == 0:
                up_table = q_up_ref[...]
            else:
                begin = pl.multiple_of(head * 2 * depth + (part - 1) * depth, depth)
                up_table = kv_up_ref[:, pl.ds(begin, depth)]
            lora.append(
                ADAPTER_FACTOR * jnp.dot(placed, up_table, preferred_element_type=f32)
            )
        query = jnp.dot(x, wq_ref[...], preferred_element_type=f32) + lora[0]
        query = turn(unit(query, q_gain_ref)).astype(bf16)
        both = lax.dot_general(x, wkv_held[...], TRANSPOSED, preferred_element_type=f32)
        raw = (both[:, :depth] + lora[1]).astype(bf16).astype(f32)
        key = turn(unit(raw, k_gain_ref)).astype(bf16)
        value = (both[:, depth:] + lora[2]).astype(bf16)
        offset = lax.rem(me, 8) * columns
        pick_row = lax.broadcasted_iota(jnp.int32, (columns, 2 * depth), 0) + offset
        pick_lane = lax.broadcasted_iota(jnp.int32, (columns, 2 * depth), 1)
        pick = jnp.where(pick_row == pick_lane, 1.0, 0.0).astype(bf16)
        turned = lax.dot_general(
            pick, jnp.concatenate([key, value], axis=1), TRANSPOSED, preferred_element_type=f32
        )
        for number, base in enumerate(bases):
            here = slice(number * pair, (number + 1) * pair)
            queries[pl.ds(base, pair), :] = query[here]
            keys[pl.ds(base, pair), :] = key[here]
            values[pl.ds(base, pair), 0:depth] = value[here]
            across[:, pl.ds(base, pair)] = turned[:, here]

    def opened(ready):
        kv_extras(ready)
        build_tables()
        turns(0, 512)

    def early(ready):
        turns(512, 512)

    def third(ready):
        factor_extras(ready)
        turns(1024, 512)
        turns(1536, 512)
        values[:, depth:] = jnp.broadcast_to(
            jnp.where(lane == 0, 1.0, 0.0), (total, depth)
        ).astype(bf16)
        across[:, total:] = jnp.zeros((columns, across.shape[1] - total), f32)

    def middle(ready):
        close_extras()
        for copy in state["shared"]:
            copy.wait_recv()
        for home in homes[:4]:
            home.wait()
        for fetch in fetches:
            fetch.wait()
        wkv_held[...] = (
            wkv_all_ref[...].astype(f32).reshape(wkv_held.shape).astype(bf16)
        )
        ready(EARLY)
        project(EARLY)

    def last(ready):
        ready(EARLY + MIDDLE)
        project(MIDDLE)

    open_extras()
    gather_rows(
        rows_ref,
        z,
        y,
        core,
        copies,
        {"opened": opened, "early": early, "third": third, "middle": middle, "last": last},
    )
    project(LAST)

    gap = lax.broadcasted_iota(jnp.int32, (BLOCK, KEY_BLOCK), 0) - lax.broadcasted_iota(
        jnp.int32, (BLOCK, KEY_BLOCK), 1
    )
    scale = depth**-0.5

    def store(step):
        return pltpu.make_async_copy(
            stage.at[step],
            terms_ref.at[pl.ds(pl.multiple_of(step * BLOCK, BLOCK), BLOCK)],
            store_sem.at[step],
        )

    def attend(step, carry):
        first_row = pl.multiple_of(step * BLOCK, BLOCK)
        row = natural(first_row, BLOCK)
        reach = (row.astype(f32) - look_up(row, 2)).astype(jnp.int32)
        mine = look_up(row, 3) == rank_lane
        query = queries[pl.ds(first_row, BLOCK), :]
        acc[...] = jnp.zeros_like(acc)

        def over_keys(number, carry):
            begin = pl.multiple_of(number * KEY_BLOCK, KEY_BLOCK)
            scores = lax.dot_general(
                query, keys[pl.ds(begin, KEY_BLOCK), :], TRANSPOSED, preferred_element_type=f32
            )
            behind = gap + (first_row - begin)
            raised = jnp.where((behind >= 0) & (behind <= reach), jnp.exp(scores * scale), 0.0)
            acc[...] += jnp.dot(
                raised.astype(bf16), values[pl.ds(begin, KEY_BLOCK), :], preferred_element_type=f32
            )
            return carry

        lax.fori_loop(0, (step + 1) * (BLOCK // KEY_BLOCK), over_keys, jnp.int32(0))
        mixed = (acc[:, :depth] / acc[:, depth : depth + 1]).astype(bf16)
        shrunk = lax.dot_general(mixed, shrink_o_ref[...], TRANSPOSED, preferred_element_type=f32)
        placed = jnp.where(mine, ADAPTER_FACTOR * shrunk, 0.0).astype(bf16)
        joined = jnp.concatenate([mixed, placed], axis=1)
        for begin in range(0, width, 512):
            stage[step, :, begin : begin + 512] = jnp.dot(
                joined, out_table[:, begin : begin + 512], preferred_element_type=f32
            ).astype(bf16)
        store(step).start()
        return carry

    lax.fori_loop(0, total // BLOCK, attend, jnp.int32(0))
    for step in range(total // BLOCK):
        store(step).wait()
    copies.settle()
    assert copies.n == GATHER_COPIES + EXTRA_COPIES, copies.n


def final_kernel(lens_s, pages_s, across, attn_ref, moe_ref, attn_out, moe_out, pages_ref):
    attn_out[...] = attn_ref[...]
    moe_out[...] = moe_ref[...]
    columns = pages_ref.shape[1]
    spot_lane = lax.broadcasted_iota(jnp.int32, (columns, PAGE), 1)

    def fill(number, start):
        length = lens_s[0, number]
        for part in range(2):
            begin = start + part * PAGE
            aligned = pl.multiple_of(lax.div(begin, PAGE) * PAGE, PAGE)
            window = across[:, pl.ds(aligned, 2 * PAGE)]
            shift = lax.rem(2 * PAGE - (begin - aligned), 2 * PAGE)
            rolled = pltpu.roll(window, shift, 1)[:, :PAGE]
            kept = jnp.where(spot_lane < length - part * PAGE, rolled, 0.0)
            pages_ref[pages_s[0, number * 2 + part]] = kept.astype(jnp.bfloat16)
        return start + length

    lax.fori_loop(0, lens_s.shape[1], fill, jnp.int32(0))


BLOCK = 512
KEY_BLOCK = 512
TRANSPOSED = (((1,), (1,)), ((), ()))


def front(
    lengths,
    groups,
    adapter_of_request,
    adapter_slot,
    q_gain,
    k_gain,
    gain,
    tokens,
    shrink,
    wkv,
    query_weight,
    query_up,
    kv_up,
    w_o,
    shrink_o,
    expand_o,
):
    rows, width = tokens.shape
    total = 32 * rows
    depth = query_weight.shape[1]
    columns = kv_up.shape[1] // 32
    count = GATHER_COPIES + EXTRA_COPIES
    vmem = pl.BlockSpec(memory_space=pltpu.VMEM)
    far = pl.BlockSpec(memory_space=pl.ANY)
    bf16, f32 = jnp.bfloat16, jnp.float32
    terms, across = pl.pallas_call(
        front_kernel,
        out_shape=(
            jax.ShapeDtypeStruct((total, width), bf16),
            jax.ShapeDtypeStruct((columns, total + 4 * PAGE), f32),
        ),
        in_specs=[vmem] * 8 + [far] * 8,
        out_specs=(far, vmem),
        scratch_shapes=[
            pltpu.VMEM((32, rows, width), bf16),
            pltpu.VMEM((shrink.shape[1], 4 * shrink.shape[0]) + shrink.shape[2:], bf16),
            pltpu.VMEM((4, 4, 2) + wkv.shape[1:], bf16),
            pltpu.VMEM((2 * depth, width), bf16),
            pltpu.VMEM(query_weight.shape, bf16),
            pltpu.VMEM(query_up.shape, bf16),
            pltpu.VMEM(kv_up.shape, bf16),
            pltpu.VMEM((w_o.shape[0] + expand_o.shape[0], width), bf16),
            pltpu.VMEM(shrink_o.shape, bf16),
            pltpu.VMEM((8, lengths.shape[1]), f32),
            pltpu.VMEM((total, depth), f32),
            pltpu.VMEM((total, depth), bf16),
            pltpu.VMEM((total, depth), bf16),
            pltpu.VMEM((total, 2 * depth), bf16),
            pltpu.VMEM((BLOCK, 2 * depth), f32),
            pltpu.VMEM((total // BLOCK, BLOCK, width), bf16),
            pltpu.SemaphoreType.DMA((6,)),
            pltpu.SemaphoreType.DMA((total // BLOCK,)),
            pltpu.SemaphoreType.DMA((5,)),
            pltpu.SemaphoreType.DMA((count,)),
            pltpu.SemaphoreType.DMA((count,)),
        ],
        compiler_params=pltpu.CompilerParams(
            collective_id=0, has_side_effects=True, vmem_limit_bytes=VMEM_LIMIT
        ),
    )(
        lengths,
        groups,
        adapter_of_request,
        adapter_slot.reshape(1, -1),
        q_gain.reshape(1, depth),
        k_gain.reshape(1, depth),
        gain,
        tokens,
        shrink,
        wkv,
        query_weight,
        query_up,
        kv_up,
        w_o,
        shrink_o,
        expand_o,
    )
    return terms, across


def final(lengths, page_table, across, attn, moe):
    pages = page_table.shape[1]
    vmem = pl.BlockSpec(memory_space=pltpu.VMEM)
    smem = pl.BlockSpec(memory_space=pltpu.SMEM)
    return pl.pallas_call(
        final_kernel,
        out_shape=(
            jax.ShapeDtypeStruct(attn.shape, attn.dtype),
            jax.ShapeDtypeStruct(moe.shape, moe.dtype),
            jax.ShapeDtypeStruct((pages, across.shape[0], PAGE), jnp.bfloat16),
        ),
        in_specs=[smem, smem, vmem, vmem, vmem],
        out_specs=(vmem, vmem, vmem),
        compiler_params=pltpu.CompilerParams(vmem_limit_bytes=VMEM_LIMIT),
    )(lengths, page_table, across, attn, moe)


def late_kernel(
    terms_ref,
    tokens_ref,
    gain_ref,
    ids_ref,
    gates_ref,
    w_gate_ref,
    w_up_ref,
    w_down_ref,
    out_ref,
    moe_ref,
    acc,
    sib,
    landed,
    local,
    total,
    rows,
    gate,
    up,
    down,
    slots,
    stage,
    pick,
    mix,
    weights_sem,
    send,
    recv,
):
    me, z, y, core = whereabouts()
    side = spot(z, y, 1 - core)
    f32, bf16 = jnp.float32, jnp.bfloat16
    experts, hidden_width, width = w_gate_ref.shape
    fetches = []
    for number, (source, held) in enumerate(
        ((w_gate_ref, gate), (w_up_ref, up), (w_down_ref, down))
    ):
        for expert in range(experts):
            fetch = pltpu.make_async_copy(
                source.at[expert], held.at[expert], weights_sem.at[number * experts + expert]
            )
            fetch.start()
            fetches.append(fetch)
    greet(partners(z, y, core))
    copies = Copies(send, recv)
    ensure, arrived = terms_from(terms_ref, acc, sib, local, z, y, core, copies)

    tokens_here = ids_ref.shape[1]
    places = experts * CAP_DEV
    slot = lax.broadcasted_iota(jnp.int32, (places, 1), 0)
    expert_of = me * experts + lax.div(slot, CAP_DEV)
    gates = gates_ref[...]
    gate_sum = jnp.sum(gates, axis=0, keepdims=True)
    hit = jnp.zeros((places, tokens_here), f32)
    weight = jnp.zeros((places, tokens_here), f32)
    for choice in range(ids_ref.shape[0]):
        same = ids_ref[choice : choice + 1, :] == expert_of
        hit = hit + jnp.where(same, 1.0, 0.0)
        weight = weight + jnp.where(same, gates_ref[choice : choice + 1, :], 0.0)
    weight = weight / gate_sum
    chunk = 256
    block = 64
    above = lax.broadcasted_iota(jnp.int32, (chunk, chunk), 0)
    right = lax.broadcasted_iota(jnp.int32, (chunk, chunk), 1)
    within = lax.div(above, block) == lax.div(right, block)
    prefix = jnp.where(within & (above <= right), 1.0, 0.0).astype(bf16)
    same_row = jnp.where(above == right, 1.0, 0.0).astype(bf16)
    number_in_block = (lax.rem(slot, CAP_DEV) + 1).astype(f32)
    for begin in range(0, tokens_here, chunk):
        piece = hit[:, begin : begin + chunk]
        count = jnp.dot(piece.astype(bf16), prefix, preferred_element_type=f32)
        taken = (piece > 0.5) & (count == number_in_block)
        pick[:, begin : begin + chunk] = jnp.where(taken, 1.0, 0.0).astype(bf16)
        shares = jnp.where(taken, weight[:, begin : begin + chunk], 0.0).astype(bf16)
        mix[pl.ds(begin, chunk), :] = lax.dot_general(
            same_row, shares, (((1,), (1,)), ((), ())), preferred_element_type=f32
        ).astype(bf16)

    scatter_rows(acc, sib, landed, z, y, core, copies, total, ensure, arrived)
    summed = total[...]
    out_ref[...] = summed.astype(out_ref.dtype)
    rows[me] = normalize(tokens_ref[...].astype(f32) + summed, gain_ref[...]).astype(rows.dtype)
    pair_rows = 2 * block
    lane_block = lax.div(lax.broadcasted_iota(jnp.int32, (1, pair_rows), 1), block)

    def apply_experts(cells):
        first = CELLS.index(cells[0])
        for number, (i, j) in enumerate(cells):
            index = spot(z + i, y + j, 0)
            piece = pick[:, pl.ds(pl.multiple_of(index * block, pair_rows), pair_rows)]
            spread = jnp.concatenate(
                [jnp.where(lane_block == part, piece, jnp.zeros_like(piece)) for part in range(2)],
                axis=0,
            )
            taken_rows = jnp.dot(
                spread, rows[pl.ds(index, 2)].reshape(pair_rows, width), preferred_element_type=f32
            )
            slots[2 * (first + number) : 2 * (first + number) + 2] = taken_rows.astype(bf16).reshape(
                2, places, width
            )
        blocks = slice(2 * first, 2 * (first + len(cells)))
        count = 2 * len(cells)

        def one_expert(expert):
            here = slice(expert * CAP_DEV, (expert + 1) * CAP_DEV)
            taken_rows = slots[blocks, here, :].reshape(count * CAP_DEV, width)
            gated = lax.dot_general(
                taken_rows, gate[expert], TRANSPOSED, preferred_element_type=f32
            )
            raised = lax.dot_general(taken_rows, up[expert], TRANSPOSED, preferred_element_type=f32)
            hidden = (gated / (1.0 + jnp.exp(-gated)) * raised).astype(bf16)
            for begin in range(0, width, 512):
                piece = jnp.dot(
                    hidden, down[expert, :, begin : begin + 512], preferred_element_type=f32
                ).astype(bf16)
                slots[blocks, here, begin : begin + 512] = piece.reshape(count, CAP_DEV, 512)

        for expert in range(experts):
            one_expert(expert)

    gather_rows(rows, z, y, core, copies, {})
    copies.settle()
    for fetch in fetches:
        fetch.wait()
    apply_experts(CELLS)

    shared = {}
    waited = set()

    def combine(i, j, which):
        index = spot(z + i, y + j, which)
        part = mix[pl.ds(pl.multiple_of(index * block, block), block), :]
        held = slots[2 * CELLS.index((i, j)) + which]
        return jnp.dot(part, held, preferred_element_type=f32).astype(bf16)

    def make(cells):
        for i, j in cells:
            if (i, j) in shared:
                continue
            stage[i, j] = combine(i, j, 1 - core)
            shared[i, j] = copies.go(stage.at[i, j], sib.at[i, j], "tensor", side)
            acc[i, j] = combine(i, j, core)

    def came(number, v, u):
        where = cell(number, v, u)
        make([where])
        if where not in waited:
            waited.add(where)
            shared[where].wait_recv()

    scatter_rows(acc, sib, landed, z, y, core, copies, total, make, came)
    moe_ref[...] = total[...].astype(moe_ref.dtype)
    copies.settle()
    assert copies.n == LATE_COPIES, copies.n


LATE_COPIES = FIRST_COPIES + GATHER_COPIES + SECOND_COPIES


def late(terms, tokens, gain, ids, gates, w_gate, w_up, w_down):
    rows, width = tokens.shape
    experts = w_gate.shape[0]
    places = experts * CAP_DEV
    everyone = terms.shape[0]
    vmem = pl.BlockSpec(memory_space=pltpu.VMEM)
    far = pl.BlockSpec(memory_space=pl.ANY)
    return pl.pallas_call(
        late_kernel,
        out_shape=(jax.ShapeDtypeStruct((rows, width), jnp.bfloat16),) * 2,
        in_specs=[far, vmem, vmem, vmem, vmem, far, far, far],
        out_specs=(vmem, vmem),
        scratch_shapes=scatter_scratch(width)
        + [
            pltpu.VMEM((rows, width), jnp.float32),
            pltpu.VMEM((everyone, rows, width), jnp.bfloat16),
            pltpu.VMEM(w_gate.shape, jnp.bfloat16),
            pltpu.VMEM(w_up.shape, jnp.bfloat16),
            pltpu.VMEM(w_down.shape, jnp.bfloat16),
            pltpu.VMEM((everyone, places, width), jnp.bfloat16),
            pltpu.VMEM((4, 4, rows, width), jnp.bfloat16),
            pltpu.VMEM((places, everyone * rows), jnp.bfloat16),
            pltpu.VMEM((everyone * rows, places), jnp.bfloat16),
            pltpu.SemaphoreType.DMA((3 * experts,)),
            pltpu.SemaphoreType.DMA((LATE_COPIES,)),
            pltpu.SemaphoreType.DMA((LATE_COPIES,)),
        ],
        compiler_params=pltpu.CompilerParams(
            collective_id=1, has_side_effects=True, vmem_limit_bytes=VMEM_LIMIT
        ),
    )(terms, tokens, gain, ids, gates, w_gate, w_up, w_down)


def local(
    tokens,
    attn_gain,
    moe_gain,
    q_gain,
    k_gain,
    query_weight,
    w_kv,
    w_o,
    w_gate,
    w_up,
    w_down,
    shrink_qkv,
    shrink_o,
    query_up_factors,
    key_value_up_factors,
    expand_o,
    lengths,
    groups,
    adapter_of_request,
    adapter_slot,
    page_table,
    expert_ids,
    expert_gates,
):
    parts = lax.axis_size("tensor")
    place = lax.axis_index("tensor")
    own_rows, width = tokens.shape
    grand_total = own_rows * parts
    adapters, rank, kv_width = key_value_up_factors.shape
    attn_terms, across = front(
        lengths,
        groups,
        adapter_of_request,
        adapter_slot,
        q_gain,
        k_gain,
        attn_gain,
        tokens,
        shrink_qkv.reshape(-1, 3, rank, width),
        w_kv.transpose(1, 0, 2),
        query_weight,
        query_up_factors.reshape(adapters * rank, -1),
        key_value_up_factors.reshape(adapters * rank, kv_width),
        w_o,
        shrink_o.reshape(adapters * rank, -1),
        expand_o.reshape(adapters * rank, width),
    )
    attn, moe = late(
        attn_terms.reshape(parts, own_rows, width),
        tokens,
        moe_gain,
        expert_ids.T,
        expert_gates.T,
        w_gate,
        w_up,
        w_down,
    )
    return tuple(final(lengths, page_table, across, attn, moe))


def solution(mesh):
    placed = (
        P(("dp", "tensor"), None),
        P(),
        P(),
        P(),
        P(),
        P(None, "tensor"),
        P("tensor", None, None),
        P("tensor", None),
        P("tensor", None, None),
        P("tensor", None, None),
        P("tensor", None, None),
        P("dp", None, None),
        P(None, None, "tensor"),
        P(None, None, "tensor"),
        P(),
        P(),
        P("dp", None),
        P("dp", None),
        P("dp", None),
        P(),
        P("dp", None),
        P("dp", None),
        P("dp", None),
    )
    return jax.shard_map(
        local,
        mesh=mesh,
        in_specs=placed,
        out_specs=(P(("dp", "tensor"), None), P(("dp", "tensor"), None), P("dp", "tensor", None)),
        check_vma=False,
    )
```
